256 devices in a mesh: context: 64 (over z, x, core), heads: 4 (over y).
Axes of the slice: x: 4, y: 4, z: 8, core: 2. Of those that a mesh axis runs over, the one named last changes fastest.
Arguments:
- residual: bfloat16 [8192, 2880], P('context'), may hold values from -6 to 6
- query_rows: bfloat16 [8192, 3584], P('context', 'heads'), may hold values from -6 to 6
- key_rows: bfloat16 [8192, 3584], P('context', 'heads'), may hold values from -6 to 6
- value_rows: bfloat16 [8192, 3584], P('context', 'heads'), may hold values from -6 to 6
- norm_gain: float32 [3584], P('heads'), may hold values from 0.1 to 1.9
- out_weight: bfloat16 [3584, 2880], P('heads'), may hold values from -0.09375 to 0.09375
- moe_gain: float32 [2880], replicated, may hold values from 0.1 to 1.9
- expert_ids: int32 [8192, 4], P('context'), may hold values from 0 to 31, all different within a row; in each aligned block of 128 rows (0 to 127, 128 to 255, ...) at most 24 rows name the same one
- gate_values: float32 [8192, 4], P('context'), may hold values from 0.2 to 1
- gate_weight: bfloat16 [64, 2880, 1440], P('context', None, 'heads'), may hold values from -0.109375 to 0.109375
- up_weight: bfloat16 [64, 2880, 1440], P('context', None, 'heads'), may hold values from -0.109375 to 0.109375
- down_weight: bfloat16 [64, 1440, 2880], P('context', 'heads'), may hold values from -0.109375 to 0.109375
Outputs:
- layer_out: bfloat16 [8192, 2880], P(('context', 'heads'))
The draws below stay inside these ranges and needn't reach their ends.
Inputs may be any that keep to these rules, and one draw needn't show every extreme that they name: `expert_ids`: each token names 4 different experts. Among the 128 tokens of one block at most 24 name the same expert, and in every draw some expert is named by exactly 24 tokens of some block.
All inputs are finite; a program needn't handle non-finite values.
Results may differ from the reference program's by a relative error of at most 0.017.
Values may be sent and summed in bfloat16 or wider, within the bound.
No kernel may reach another device: no remote copies, remote signals or barrier semaphores. Data moves between devices by JAX's collectives and lax.ppermute only.
A program may use at most 128 MiB of HBM per device.

```python
import math
import jax
import jax.numpy as jnp
import numpy as np
from jax import lax

D = 2880
FF = 2880
HEADS = 56
HD = 64
TOP = 4
CSPLIT = 2
TOK_DEV = 128
TOKENS = 8192
EXPERTS = 32
HSPLIT = 8
FF_DEV = 360
CAP = 24
N_CONTEXT = 64


def level_of(rng, dims, pieces, smallest, largest):
    gain, own = 1.0, jax.random.fold_in(rng, 6)
    for axis_at, parts in pieces:
        steps = jnp.exp(jax.random.uniform(jax.random.fold_in(own, axis_at), (parts,), jnp.float32, smallest / len(pieces), largest / len(pieces)))
        gain = gain * jnp.repeat(steps, dims[axis_at] // parts).reshape([-1 if axis == axis_at else 1 for axis in range(len(dims))])
    return gain


def assign_block(stream_key, own, number, rows, number_of, top, limit, slope):
    order = jax.random.permutation(stream_key, number_of)
    heavy_load, ordinary = shares(number_of, rows * top, limit, slope, True), shares(number_of, rows * top, limit, slope, False)
    places = jnp.arange(number_of)

    def named(lengths, turn):
        used = int((lengths > 0).sum())
        fixed = max(1, used // 4)
        shifted = fixed + (places - fixed + turn * (used - fixed)) % max(1, number_of - fixed)
        return jnp.zeros((number_of,), jnp.int32).at[order[jnp.where(places < fixed, places, shifted)]].set(jnp.asarray(lengths, jnp.int32))

    lengths = jnp.where(number % 4 == 0, named(heavy_load, number // 4), named(ordinary, number - number // 4 - 1))
    mixed = jax.random.permutation(jax.random.fold_in(own, 3), number_of)
    source_of, receiver = mixed[0:number_of // 2 * 2:2], mixed[1:number_of // 2 * 2:2]
    room = jnp.minimum(lengths[source_of] - 1, limit - lengths[receiver]) // 2
    room = jnp.where((source_of == order[0]) | (receiver == order[0]) | (lengths[receiver] == 0), 0, jnp.maximum(room, 0))
    shifted = jax.random.randint(jax.random.fold_in(own, 4), (number_of // 2,), 0, 1 << 20) % (room + 1)
    lengths = lengths.at[source_of].add(-shifted).at[receiver].add(shifted)
    members = jnp.searchsorted(jnp.cumsum(lengths), jnp.arange(rows * top), side="right").astype(jnp.int32)
    grid = members.reshape(top, rows).T
    grid = grid[jax.random.permutation(jax.random.fold_in(own, 1), rows)]
    turn = jax.random.randint(jax.random.fold_in(own, 2), (rows, 1), 0, top)
    return jnp.take_along_axis(grid, (jnp.arange(top)[None, :] + turn) % top, axis=1)


def shares(amount, total, bound, slope, full):
    loads = [(1 << 20) // math.isqrt(standing ** slope) + 1 for standing in range(1, amount + 1)]
    largest = bound if full else min(bound, max(-(-total // amount), total * loads[0] // sum(loads)))
    least = 1 if total - largest >= amount - 1 else 0
    given, spare = [largest] + [least] * (amount - 1), total - largest - least * (amount - 1)
    while spare > 0:
        movable = [i for i in range(1, amount) if given[i] < largest] or [i for i in range(1, amount) if given[i] < bound]
        whole, left = sum([loads[i] for i in movable]), spare
        for i in movable:
            more = min(bound - given[i], max(1, left * loads[i] // whole), spare)
            given[i] = given[i] + more
            spare = spare - more
    return np.array(given)


def noise(stream_key, extent, width, most, shards=(), kind=jnp.bfloat16):
    array = width * jax.random.normal(stream_key, extent, jnp.float32)
    if shards:
        array = array * level_of(stream_key, extent, shards, -0.22, 0.18)
    return jnp.clip(array, -most, most).astype(kind)


def setup_inputs(seed: int = 0) -> dict:
    splits = jax.random.split(jax.random.key(seed), 13)
    residual = noise(splits[0], (TOKENS, D), 1.0, 6.0, ((0, 64),))
    query_rows = noise(splits[1], (TOKENS, HEADS * HD), 1.0, 6.0, ((0, 64), (1, 4)))
    key_rows = noise(splits[2], (TOKENS, HEADS * HD), 1.0, 6.0, ((0, 64), (1, 4)))
    value_rows = noise(splits[3], (TOKENS, HEADS * HD), 1.0, 6.0, ((0, 64), (1, 4)))
    norm_gain = jnp.clip(1.0 + 0.18 * jax.random.normal(splits[4], (HEADS * HD,), jnp.float32), 0.1, 1.9)
    out_weight = noise(splits[5], (HEADS * HD, D), (HEADS * HD) ** -0.5, 0.09375, ((0, 4),))
    moe_gain = jnp.clip(1.0 + 0.18 * jax.random.normal(splits[6], (D,), jnp.float32), 0.1, 1.9)
    expert_ids_keys = jax.random.split(jax.random.fold_in(splits[7], 1), TOKENS // TOK_DEV)
    expert_ids_turns = jax.random.permutation(jax.random.fold_in(splits[7], 3), TOKENS // TOK_DEV)
    expert_ids = jax.vmap(lambda own, number: assign_block(jax.random.fold_in(splits[7], 2), own, number, TOK_DEV, EXPERTS, TOP, CAP, 1))(expert_ids_keys, expert_ids_turns).reshape((TOKENS, TOP))
    gate_values = jnp.clip(0.2 + 0.8 * jax.random.uniform(splits[8], (TOKENS, TOP), jnp.float32) ** level_of(splits[8], (TOKENS, TOP), ((0, 64),), -0.2, 0.2), 0.2, 1.0)
    gate_weight = noise(splits[9], (EXPERTS * CSPLIT, D, FF // CSPLIT), D ** -0.5, 0.109375, ((0, 64), (2, 4)))
    up_weight = noise(splits[10], (EXPERTS * CSPLIT, D, FF // CSPLIT), D ** -0.5, 0.109375, ((0, 64), (2, 4)))
    down_weight = noise(splits[11], (EXPERTS * CSPLIT, FF // CSPLIT, D), FF ** -0.5, 0.109375, ((0, 64), (1, 4)))
    return dict(residual=residual, query_rows=query_rows, key_rows=key_rows, value_rows=value_rows, norm_gain=norm_gain, out_weight=out_weight, moe_gain=moe_gain, expert_ids=expert_ids, gate_values=gate_values, gate_weight=gate_weight, up_weight=up_weight, down_weight=down_weight)


def round_trip(values_in):
    lowered = values_in.astype(jnp.bfloat16)
    lowered = lax.optimization_barrier(lowered)
    return lowered.astype(jnp.float32)

def block_attention(query_rows, key_rows, value_rows):
    shaped = (N_CONTEXT, TOK_DEV, HEADS, HD)
    query_blocks = query_rows.reshape(shaped)
    key_blocks = key_rows.reshape(shaped)
    value_blocks = value_rows.reshape(shaped)
    causal = jnp.arange(TOK_DEV)[:, None] >= jnp.arange(TOK_DEV)[None, :]

    def advance(carried, block_set):
        query_wide = block_set[0].astype(jnp.float32)
        key_wide = block_set[1].astype(jnp.float32)
        value_wide = block_set[2].astype(jnp.float32)
        scores = jnp.einsum('thd,shd->hts', query_wide, key_wide)
        weights = round_trip(jnp.where(causal[None], scores, 0.0))
        inner_part = jnp.einsum('hts,shd->thd', weights, value_wide)
        outer_part = jnp.einsum('thd,hde->the', query_wide, round_trip(carried))
        own_state = jnp.einsum('shd,she->hde', key_wide, value_wide)
        return (carried + own_state, inner_part + outer_part)
    initial = jnp.zeros((HEADS, HD, HD), jnp.float32)
    last_state, mixed = lax.scan(advance, initial, (query_blocks, key_blocks, value_blocks))
    return mixed.reshape(TOKENS, HEADS, HD)

def slot_ranks(expert_ids):
    flattened = expert_ids.reshape(N_CONTEXT, TOK_DEV * TOP)
    onehot = (flattened[:, :, None] == jnp.arange(EXPERTS, dtype=jnp.int32)[None, None, :]).astype(jnp.int32)
    before = jnp.cumsum(onehot, axis=1) - onehot
    return lax.optimization_barrier(jnp.sum(before * onehot, axis=2)).reshape(TOKENS, TOP).astype(jnp.int32)

def expert_rows(token_rows, gate_part, up_part, down_part):
    gate_act = jnp.dot(token_rows, gate_part, preferred_element_type=jnp.float32)
    up_act = jnp.dot(token_rows, up_part, preferred_element_type=jnp.float32)
    hidden = (jax.nn.silu(gate_act) * up_act).astype(jnp.bfloat16)
    grouped = hidden.reshape(token_rows.shape[0], HSPLIT, FF_DEV).astype(jnp.float32)
    down_grouped = down_part.reshape(HSPLIT, FF_DEV, D).astype(jnp.float32)
    partial_value = jnp.einsum('rgf,gfd->rgd', grouped, down_grouped)
    return lax.optimization_barrier(jnp.sum(round_trip(partial_value), axis=1))

def run_expert(packed_item):
    return expert_rows(packed_item[0], packed_item[1], packed_item[2], packed_item[3])

def reference(residual, query_rows, key_rows, value_rows, norm_gain, out_weight, moe_gain, expert_ids, gate_values, gate_weight, up_weight, down_weight):
    mixed = block_attention(query_rows, key_rows, value_rows)
    center = lax.optimization_barrier(jnp.mean(mixed, axis=-1, keepdims=True))
    spread = lax.optimization_barrier(jnp.mean(jnp.square(mixed - center), axis=-1, keepdims=True))
    heads_normed = ((mixed - center) * lax.rsqrt(spread + 1e-05) * norm_gain.reshape(HEADS, HD)).astype(jnp.bfloat16)
    attended = residual.astype(jnp.float32) + jnp.dot(heads_normed.reshape(TOKENS, HEADS * HD), out_weight, preferred_element_type=jnp.float32)
    scaling = lax.rsqrt(lax.optimization_barrier(jnp.mean(jnp.square(attended), axis=-1, keepdims=True)) + 1e-06)
    moe_in = (attended * scaling * moe_gain).astype(jnp.bfloat16)
    ranks = slot_ranks(expert_ids)
    block_index = (jnp.arange(TOKENS, dtype=jnp.int32) // TOK_DEV).astype(jnp.int32)[:, None]
    slot_rows = (block_index * CAP + ranks).astype(jnp.int32)
    buffers = jnp.zeros((EXPERTS, N_CONTEXT * CAP, D), jnp.bfloat16)
    buffers = buffers.at[expert_ids, slot_rows].set(jnp.broadcast_to(moe_in[:, None, :], (TOKENS, TOP, D)))
    half_width = FF // CSPLIT
    gate_full = gate_weight.reshape(EXPERTS, CSPLIT, D, half_width).transpose(0, 2, 1, 3).reshape(EXPERTS, D, FF)
    up_full = up_weight.reshape(EXPERTS, CSPLIT, D, half_width).transpose(0, 2, 1, 3).reshape(EXPERTS, D, FF)
    down_full = down_weight.reshape(EXPERTS, FF, D)
    results = lax.map(run_expert, (buffers, gate_full, up_full, down_full))
    picked = results[expert_ids, slot_rows]
    mixture = lax.optimization_barrier(jnp.sum(gate_values[:, :, None] * picked, axis=1))
    return (attended + mixture).astype(jnp.bfloat16)
```

```python
import functools

import jax
import jax.numpy as jnp
from jax import lax
from jax.experimental import pallas as pl
from jax.experimental.pallas import tpu as pltpu
from jax.sharding import Mesh
from jax.sharding import PartitionSpec as P

HD = 64
PAIR = 2 * HD
CORES = 2
SPARE = 48
BF = jnp.bfloat16
F32 = jnp.float32
VMEM_SPEC = pl.BlockSpec(memory_space=pltpu.VMEM)
SMEM_SPEC = pl.BlockSpec(memory_space=pltpu.SMEM)


def params():
    return pltpu.CompilerParams(vmem_limit_bytes=56 << 20)


def cost(flops, moved):
    return pl.CostEstimate(flops=int(flops), bytes_accessed=int(moved), transcendentals=0)


def dot(a, b, dims=((1,), (0,))):
    return lax.dot_general(a, b, (dims, ((), ())), preferred_element_type=F32)


def state_body(k_ref, v_ref, o_ref):
    first = lax.broadcasted_iota(jnp.int32, (HD, PAIR), 1) < HD
    for p in range(k_ref.shape[1] // PAIR):
        cols = slice(p * PAIR, (p + 1) * PAIR)
        both = dot(k_ref[:, cols], v_ref[:, cols], ((0,), (0,)))
        o_ref[:, cols] = jnp.where(first, both[:HD], both[HD:]).astype(BF)


def attend_body(h_ref, q_ref, k_ref, v_ref, s_ref, gain_ref, w_ref, o0, o1, o2, o3, normed, parts):
    tokens = q_ref.shape[0]
    lane = lax.broadcasted_iota(jnp.int32, (tokens, PAIR), 1)
    first = lane < HD
    lane_s = lax.broadcasted_iota(jnp.int32, (HD, PAIR), 1)
    causal = lax.broadcasted_iota(jnp.int32, (tokens, tokens), 0) >= lax.broadcasted_iota(
        jnp.int32, (tokens, tokens), 1
    )
    zero = jnp.zeros((tokens, PAIR), BF)

    def halves_mean(x):
        a = jnp.sum(jnp.where(first, x, 0.0), axis=1, keepdims=True)
        b = jnp.sum(jnp.where(first, 0.0, x), axis=1, keepdims=True)
        return jnp.where(first, a, b) * (1.0 / HD)

    for p in range(q_ref.shape[1] // PAIR):
        cols = slice(p * PAIR, (p + 1) * PAIR)
        q, k, v, s = q_ref[:, cols], k_ref[:, cols], v_ref[:, cols], s_ref[:, cols]
        s_zero = jnp.zeros_like(s)
        block = jnp.concatenate(
            [jnp.where(lane_s < HD, s, s_zero), jnp.where(lane_s < HD, s_zero, s)], axis=0
        )
        mixed = dot(q, block)
        inner = []
        for keep in (jnp.where(first, q, zero), jnp.where(first, zero, q)):
            scores = dot(keep, k, ((1,), (1,)))
            weights = jnp.where(causal, scores, 0.0).astype(BF)
            inner.append(dot(weights, v))
        mixed = mixed + jnp.where(first, inner[0], inner[1])
        centered = mixed - halves_mean(mixed)
        spread = halves_mean(centered * centered)
        normed[:, cols] = (centered * lax.rsqrt(spread + 1e-05) * gain_ref[:, cols]).astype(BF)
    whole = dot(normed[...], w_ref[...])
    quarter = o0.shape[1]
    for q in range(4):
        parts[q] = whole[:, q * quarter : (q + 1) * quarter].astype(BF)
    for j, o in enumerate((o0, o1, o2, o3)):
        o[...] = parts[lax.rem(h_ref[0] + j, 4)]


def route_body(experts, ids_ref, gates_ref, place_ref, high_ref, low_ref):
    top, tokens = ids_ref.shape
    rows = place_ref.shape[0]
    capacity = rows // experts
    expert = lax.broadcasted_iota(jnp.int32, (experts, tokens), 0)
    member = jnp.zeros((experts, tokens), F32)
    gate = jnp.zeros((experts, tokens), F32)
    for c in range(top):
        hit = ids_ref[c : c + 1, :] == expert
        member = member + jnp.where(hit, 1.0, 0.0)
        gate = gate + jnp.where(hit, gates_ref[c : c + 1, :], 0.0)
    earlier = lax.broadcasted_iota(jnp.int32, (tokens, tokens), 0) < lax.broadcasted_iota(
        jnp.int32, (tokens, tokens), 1
    )
    rank = dot(member.astype(BF), jnp.where(earlier, 1.0, 0.0).astype(BF))
    rank = jnp.where(member > 0.0, rank, -1.0)
    shape = (experts, capacity, tokens)
    slot = lax.broadcasted_iota(jnp.int32, shape, 1).astype(F32)
    placed = jnp.where(jnp.broadcast_to(rank[:, None, :], shape) == slot, 1.0, 0.0)
    weighted = (placed * jnp.broadcast_to(gate[:, None, :], shape)).reshape(rows, tokens)
    place_ref[...] = placed.reshape(rows, tokens).astype(BF)
    mix = weighted.T
    high = mix.astype(BF)
    high_ref[...] = high
    low_ref[...] = (mix - high.astype(F32)).astype(BF)


def pack_body(h_ref, p0, p1, p2, p3, res_ref, gain_ref, place_ref, packed_ref, att_ref, res, rows):
    quarter = p0.shape[1]
    for q in range(4):
        res[q] = res_ref[:, q * quarter : (q + 1) * quarter]
    att = res[h_ref[0]].astype(F32)
    for p in (p0, p1, p2, p3):
        att = att + p[...].astype(F32)
    att_ref[...] = att
    square = jnp.sum(att * att, axis=1, keepdims=True)
    high = square.astype(BF).astype(F32)
    middle = (square - high).astype(BF).astype(F32)
    low = square - high - middle
    lane = lax.broadcasted_iota(jnp.int32, (att.shape[0], SPARE), 1)
    extra = jnp.where(lane == 0, high, jnp.where(lane == 1, middle, jnp.where(lane == 2, low, 0.0)))
    rows[:, :quarter] = (att * gain_ref[...]).astype(BF)
    rows[:, quarter:] = extra.astype(BF)
    packed_ref[...] = dot(place_ref[...], rows[...]).astype(BF)


def expert_body(features, added, h_ref, x0, x1, x2, x3, gate_ref, up_ref, down_ref, *rest):
    outs = rest[4:] if added else rest
    quarter = gate_ref.shape[1]
    gate = up = square = None
    for j, x in enumerate((x0, x1, x2, x3)):
        q = lax.rem(h_ref[0] + j, 4)
        row = x[:, :quarter]
        tail = jnp.sum(x[:, quarter:].astype(F32), axis=1, keepdims=True)
        g, u = dot(row, gate_ref[q]), dot(row, up_ref[q])
        gate = g if j == 0 else gate + g
        up = u if j == 0 else up + u
        square = tail if j == 0 else square + tail
    scaling = lax.rsqrt(square * (1.0 / features) + 1e-06)
    gate, up = gate * scaling, up * scaling
    hidden = (gate / (1.0 + jnp.exp(-gate)) * up).astype(BF)
    for j in range(4):
        part = dot(hidden, down_ref[lax.rem(h_ref[0] + j, 4)])
        if added:
            part = part + rest[j][...].astype(F32)
        outs[j][...] = part.astype(BF)


def mix_body(h_ref, back_ref, high_ref, low_ref, att_ref, o0, o1, o2, o3, done):
    back = back_ref[...]
    mixture = dot(high_ref[...], back) + dot(low_ref[...], back)
    done[...] = (att_ref[...] + mixture).astype(BF)
    share = o0.shape[0]
    for j, o in enumerate((o0, o1, o2, o3)):
        start = pl.multiple_of(lax.rem(h_ref[0] + j, 4) * share, share)
        o[...] = done[pl.ds(start, share), :]


def join_body(h_ref, r0, r1, r2, r3, o_ref, held):
    quarter = r0.shape[1]
    for j, r in enumerate((r0, r1, r2, r3)):
        held[lax.rem(h_ref[0] + 4 - j, 4)] = r[...]
    for q in range(4):
        o_ref[:, q * quarter : (q + 1) * quarter] = held[q]


def shift(x, by):
    return lax.ppermute(x, "heads", [(i, (i + by) % 4) for i in range(4)])


def swap(x):
    return lax.ppermute(x, "core", [(0, 1), (1, 0)])


def on_device(
    residual,
    query_rows,
    key_rows,
    value_rows,
    norm_gain,
    out_weight,
    moe_gain,
    expert_ids,
    gate_values,
    gate_weight,
    up_weight,
    down_weight,
):
    tokens, width = query_rows.shape
    features = residual.shape[1]
    quarter = features // 4
    chips = lax.axis_size("chip")
    blocks = chips * CORES
    context = ("chip", "core")
    h = lax.axis_index("heads").astype(jnp.int32)
    h_arr = jnp.full((1,), h, jnp.int32)
    capacity = min(tokens, 3 * tokens * expert_ids.shape[1] // (2 * chips))
    rows = chips * capacity
    shape = jax.ShapeDtypeStruct

    own_state = pl.pallas_call(
        state_body,
        out_shape=shape((HD, width), BF),
        in_specs=[VMEM_SPEC] * 2,
        out_specs=VMEM_SPEC,
        compiler_params=params(),
        name="own_state",
    )(key_rows, value_rows)
    chunks = lax.all_to_all(own_state, context, 0, 0, tiled=True)
    before = (jnp.arange(blocks)[:, None] > jnp.arange(blocks)[None, :]).astype(BF)
    prefix = jnp.dot(before, chunks, preferred_element_type=F32).astype(BF)
    carried = lax.all_to_all(prefix, context, 0, 0, tiled=True)

    place, mix_high, mix_low = pl.pallas_call(
        functools.partial(route_body, chips),
        out_shape=(shape((rows, tokens), BF), shape((tokens, rows), BF), shape((tokens, rows), BF)),
        in_specs=[VMEM_SPEC] * 2,
        out_specs=(VMEM_SPEC,) * 3,
        compiler_params=params(),
        cost_estimate=cost(1e8, 1e6),
        name="route",
    )(expert_ids.T, gate_values.T)

    parts = pl.pallas_call(
        attend_body,
        out_shape=(shape((tokens, quarter), BF),) * 4,
        in_specs=[SMEM_SPEC] + [VMEM_SPEC] * 6,
        out_specs=(VMEM_SPEC,) * 4,
        scratch_shapes=[pltpu.VMEM((tokens, width), BF), pltpu.VMEM((4, tokens, quarter), BF)],
        compiler_params=params(),
        name="attend",
    )(h_arr, query_rows, key_rows, value_rows, carried, norm_gain.reshape(1, width), out_weight)
    pieces = [parts[0]] + [shift(parts[j], j) for j in (1, 2, 3)]

    gain = lax.dynamic_index_in_dim(moe_gain.reshape(4, 1, quarter), h, 0, keepdims=False)
    packed, attended = pl.pallas_call(
        pack_body,
        out_shape=(shape((rows, quarter + SPARE), BF), shape((tokens, quarter), F32)),
        in_specs=[SMEM_SPEC] + [VMEM_SPEC] * 7,
        out_specs=(VMEM_SPEC,) * 2,
        scratch_shapes=[
            pltpu.VMEM((4, tokens, quarter), BF),
            pltpu.VMEM((tokens, quarter + SPARE), BF),
        ],
        compiler_params=params(),
        name="pack",
    )(h_arr, *pieces, residual, gain, place)

    arrived = lax.all_to_all(
        packed.reshape(chips, capacity, quarter + SPARE), "chip", 0, 0, tiled=True
    ).reshape(rows, quarter + SPARE)
    half = rows // 2
    low, high = arrived[:half], arrived[half:]
    minus_low, plus_high = shift(low, 1), shift(high, -1)
    minus_high, plus_low = shift(high, 1), shift(low, -1)
    far_low, far_high = shift(minus_low, 1), shift(plus_high, -1)
    own_sets = ((low, plus_low, far_low, minus_low), (high, plus_high, far_high, minus_high))
    other_sets = tuple(tuple(swap(x) for x in group) for group in own_sets)

    gate_parts = gate_weight[0].reshape(4, quarter, -1)
    up_parts = up_weight[0].reshape(4, quarter, -1)
    hidden_count = gate_parts.shape[2]
    down_parts = down_weight[0].reshape(hidden_count, 4, quarter).transpose(1, 0, 2)
    tile = 128

    def experts(group, added):
        x_spec = pl.BlockSpec((tile, quarter + SPARE), lambda i: (i, 0))
        o_spec = pl.BlockSpec((tile, quarter), lambda i: (i, 0))
        w_spec = pl.BlockSpec((4, quarter, hidden_count), lambda i: (0, 0, 0))
        d_spec = pl.BlockSpec((4, hidden_count, quarter), lambda i: (0, 0, 0))
        return pl.pallas_call(
            functools.partial(expert_body, features, bool(added)),
            grid=(half // tile,),
            out_shape=(shape((half, quarter), BF),) * 4,
            in_specs=[SMEM_SPEC] + [x_spec] * 4 + [w_spec] * 2 + [d_spec] + [o_spec] * len(added),
            out_specs=(o_spec,) * 4,
            compiler_params=params(),
            cost_estimate=cost(6 * half * features * hidden_count, 12e6),
            name="experts",
        )(h_arr, *group, gate_parts, up_parts, down_parts, *added)

    other_low = experts(other_sets[0], ())
    other_high = experts(other_sets[1], ())
    from_low = tuple(swap(x) for x in other_low)
    from_high = tuple(swap(x) for x in other_high)
    sum_low = experts(own_sets[0], from_low)
    sum_high = experts(own_sets[1], from_high)

    def plus(*terms):
        total = terms[0].astype(F32)
        for term in terms[1:]:
            total = total + term.astype(F32)
        return total.astype(BF)

    via_low, via_high = shift(sum_low[2], 1), shift(sum_high[2], -1)
    got_low_plus, got_high_minus = shift(sum_low[3], -1), shift(sum_high[1], 1)
    got_low_minus = shift(plus(sum_low[1], via_low), 1)
    got_high_plus = shift(plus(sum_high[3], via_high), -1)
    total_low = plus(sum_low[0], got_low_minus, got_low_plus)
    total_high = plus(sum_high[0], got_high_minus, got_high_plus)
    leaving = jnp.concatenate([total_low, total_high], axis=0).reshape(chips, capacity, quarter)
    returned = lax.all_to_all(leaving, "chip", 0, 0, tiled=True).reshape(rows, quarter)

    share = tokens // 4
    ends = pl.pallas_call(
        mix_body,
        out_shape=(shape((share, quarter), BF),) * 4,
        in_specs=[SMEM_SPEC] + [VMEM_SPEC] * 4,
        out_specs=(VMEM_SPEC,) * 4,
        scratch_shapes=[pltpu.VMEM((tokens, quarter), BF)],
        compiler_params=params(),
        name="mix",
    )(h_arr, returned, mix_high, mix_low, attended)
    finals = [ends[0]] + [shift(ends[j], j) for j in (1, 2, 3)]
    return pl.pallas_call(
        join_body,
        out_shape=shape((share, features), BF),
        in_specs=[SMEM_SPEC] + [VMEM_SPEC] * 4,
        out_specs=VMEM_SPEC,
        scratch_shapes=[pltpu.VMEM((4, share, quarter), BF)],
        compiler_params=params(),
        name="join",
    )(h_arr, *finals)


def solution(mesh):
    devices = mesh.devices
    split = Mesh(
        devices.reshape(devices.shape[0] // CORES, CORES, devices.shape[1]),
        ("chip", "core", "heads"),
    )
    context = ("chip", "core")
    in_specs = (
        P(context, None),
        P(context, "heads"),
        P(context, "heads"),
        P(context, "heads"),
        P("heads"),
        P("heads", None),
        P(),
        P(context, None),
        P(context, None),
        P(context, None, "heads"),
        P(context, None, "heads"),
        P(context, "heads", None),
    )
    return jax.shard_map(
        on_device,
        mesh=split,
        in_specs=in_specs,
        out_specs=P(("chip", "core", "heads"), None),
        check_vma=False,
    )
```

```python
import functools

import jax
import jax.numpy as jnp
from jax import lax
from jax.experimental import pallas as pl
from jax.experimental.pallas import tpu as pltpu
from jax.sharding import Mesh
from jax.sharding import PartitionSpec as P

HD = 64
PAIR = 2 * HD
CORES = 2
BREADTH = 4
SPARE = 48
BF = jnp.bfloat16
F32 = jnp.float32
VMEM_SPEC = pl.BlockSpec(memory_space=pltpu.VMEM)
SMEM_SPEC = pl.BlockSpec(memory_space=pltpu.SMEM)


def params():
    return pltpu.CompilerParams(vmem_limit_bytes=56 << 20)


def cost(flops, moved):
    return pl.CostEstimate(flops=int(flops), bytes_accessed=int(moved), transcendentals=0)


def dot(a, b, dims=((1,), (0,))):
    return lax.dot_general(a, b, (dims, ((), ())), preferred_element_type=F32)


def state_body(core_ref, k_ref, v_ref, keep_ref, send_ref, both_ref):
    first = lax.broadcasted_iota(jnp.int32, (HD, PAIR), 1) < HD
    half = HD // 2
    for p in range(k_ref.shape[1] // PAIR):
        cols = slice(p * PAIR, (p + 1) * PAIR)
        both = dot(k_ref[:, cols], v_ref[:, cols], ((0,), (0,)))
        state = jnp.where(first, both[:HD], both[HD:]).astype(BF)
        both_ref[0, :, cols] = state[:half]
        both_ref[1, :, cols] = state[half:]
    keep_ref[...] = both_ref[core_ref[0]]
    send_ref[...] = both_ref[1 - core_ref[0]]


def inner_body(q_ref, k_ref, v_ref, o_ref):
    tokens = q_ref.shape[0]
    first = lax.broadcasted_iota(jnp.int32, (tokens, PAIR), 1) < HD
    causal = lax.broadcasted_iota(jnp.int32, (tokens, tokens), 0) >= lax.broadcasted_iota(
        jnp.int32, (tokens, tokens), 1
    )
    zero = jnp.zeros((tokens, PAIR), BF)
    for p in range(q_ref.shape[1] // PAIR):
        cols = slice(p * PAIR, (p + 1) * PAIR)
        q, k, v = q_ref[:, cols], k_ref[:, cols], v_ref[:, cols]
        inner = []
        for keep in (jnp.where(first, q, zero), jnp.where(first, zero, q)):
            scores = dot(keep, k, ((1,), (1,)))
            weights = jnp.where(causal, scores, 0.0).astype(BF)
            inner.append(dot(weights, v))
        o_ref[:, cols] = jnp.where(first, inner[0], inner[1])


def attend_body(
    place_ref, q_ref, inner_ref, mine_ref, other_ref, gain_ref, w_ref, o0, o1, o2, o3, normed, state
):
    tokens = q_ref.shape[0]
    first = lax.broadcasted_iota(jnp.int32, (tokens, PAIR), 1) < HD
    first_s = lax.broadcasted_iota(jnp.int32, (HD, PAIR), 1) < HD
    state[place_ref[1]] = mine_ref[...]
    state[1 - place_ref[1]] = other_ref[...]

    def halves_mean(x):
        a = jnp.sum(jnp.where(first, x, 0.0), axis=1, keepdims=True)
        b = jnp.sum(jnp.where(first, 0.0, x), axis=1, keepdims=True)
        return jnp.where(first, a, b) * (1.0 / HD)

    for p in range(q_ref.shape[1] // PAIR):
        cols = slice(p * PAIR, (p + 1) * PAIR)
        s = jnp.concatenate([state[0, :, cols], state[1, :, cols]], axis=0)
        s_zero = jnp.zeros_like(s)
        block = jnp.concatenate(
            [jnp.where(first_s, s, s_zero), jnp.where(first_s, s_zero, s)], axis=0
        )
        mixed = inner_ref[:, cols] + dot(q_ref[:, cols], block)
        centered = mixed - halves_mean(mixed)
        spread = halves_mean(centered * centered)
        normed[:, cols] = (centered * lax.rsqrt(spread + 1e-05) * gain_ref[:, cols]).astype(BF)
    quarter = w_ref.shape[0] // 4
    pad = jnp.zeros((tokens, o0.shape[1] - quarter), BF)
    for j, o in enumerate((o0, o1, o2, o3)):
        start = pl.multiple_of(lax.rem(place_ref[0] + j, 4) * quarter, quarter)
        part = dot(normed[...], w_ref[pl.ds(start, quarter), :], ((1,), (1,)))
        o[:, :quarter] = part.astype(BF)
        o[:, quarter:] = pad


def route_body(experts, ids_ref, gates_ref, place_ref, high_ref, low_ref):
    top, tokens = ids_ref.shape
    rows = place_ref.shape[0]
    capacity = rows // experts
    expert = lax.broadcasted_iota(jnp.int32, (experts, tokens), 0)
    member = jnp.zeros((experts, tokens), F32)
    gate = jnp.zeros((experts, tokens), F32)
    for c in range(top):
        hit = ids_ref[c : c + 1, :] == expert
        member = member + jnp.where(hit, 1.0, 0.0)
        gate = gate + jnp.where(hit, gates_ref[c : c + 1, :], 0.0)
    earlier = lax.broadcasted_iota(jnp.int32, (tokens, tokens), 0) < lax.broadcasted_iota(
        jnp.int32, (tokens, tokens), 1
    )
    rank = dot(member.astype(BF), jnp.where(earlier, 1.0, 0.0).astype(BF))
    rank = jnp.where(member > 0.0, rank, -1.0)
    shape = (experts, capacity, tokens)
    slot = lax.broadcasted_iota(jnp.int32, shape, 1).astype(F32)
    placed = jnp.where(jnp.broadcast_to(rank[:, None, :], shape) == slot, 1.0, 0.0)
    weighted = (placed * jnp.broadcast_to(gate[:, None, :], shape)).reshape(rows, tokens)
    place_ref[...] = placed.reshape(rows, tokens).astype(BF)
    mix = weighted.T
    high = mix.astype(BF)
    high_ref[...] = high
    low_ref[...] = (mix - high.astype(F32)).astype(BF)


def pack_body(h_ref, p0, p1, p2, p3, res_ref, gain_ref, place_ref, packed_ref, att_ref, rows):
    quarter = att_ref.shape[1]
    start = pl.multiple_of(h_ref[0] * quarter, quarter)
    att = res_ref[pl.ds(start, quarter), :].astype(F32).T
    for p in (p0, p1, p2, p3):
        att = att + p[:, :quarter].astype(F32)
    att_ref[...] = att
    square = jnp.sum(att * att, axis=1, keepdims=True)
    high = square.astype(BF).astype(F32)
    middle = (square - high).astype(BF).astype(F32)
    low = square - high - middle
    lane = lax.broadcasted_iota(jnp.int32, (att.shape[0], SPARE), 1)
    extra = jnp.where(lane == 0, high, jnp.where(lane == 1, middle, jnp.where(lane == 2, low, 0.0)))
    rows[:, :quarter] = (att * gain_ref[...]).astype(BF)
    rows[:, quarter:] = extra.astype(BF)
    packed_ref[...] = dot(place_ref[...], rows[...]).astype(BF)


def weights_body(h_ref, gate_ref, up_ref, down_ref, *outs):
    quarter = gate_ref.shape[1] // 4
    for ref, out in zip((gate_ref, up_ref, down_ref), outs):
        pad = jnp.zeros((out.shape[1], out.shape[2] - quarter), BF)
        for q in range(4):
            place = lax.rem(q + 4 - h_ref[0], 4)
            part = ref[:, q * quarter : (q + 1) * quarter]
            out[place] = jnp.concatenate([part, pad], axis=1)


def expert_body(features, added, x0, x1, x2, x3, gate_ref, up_ref, down_ref, *rest):
    xs, gate_sum, up_sum = rest[-3:]
    quarter = features // 4
    square = None
    for j, x in enumerate((x0, x1, x2, x3)):
        xs[j] = x[...]
        tail = jnp.sum(x[:, quarter:].astype(F32), axis=1, keepdims=True)
        square = tail if j == 0 else square + tail
    gate_sum[...] = jnp.zeros_like(gate_sum)
    up_sum[...] = jnp.zeros_like(up_sum)

    def gather(j, carry):
        row = xs[j]
        gate_sum[...] += dot(row, gate_ref[j], ((1,), (1,)))
        up_sum[...] += dot(row, up_ref[j], ((1,), (1,)))
        return carry

    lax.fori_loop(0, 4, gather, 0)
    scaling = lax.rsqrt(square * (1.0 / features) + 1e-06)
    gate, up = gate_sum[...] * scaling, up_sum[...] * scaling
    hidden = (gate / (1.0 + jnp.exp(-gate)) * up).astype(BF)

    def spread(j, carry):
        part = dot(hidden, down_ref[j])
        if added:
            xs[j] = (part + rest[0][j].astype(F32)).astype(BF)
        else:
            rest[0][j] = part.astype(BF)
        return carry

    lax.fori_loop(0, 4, spread, 0)
    if added:
        for j in range(4):
            rest[1 + j][...] = xs[j]


def mix_body(h_ref, back_ref, high_ref, low_ref, att_ref, o0, o1, o2, o3, done):
    back = back_ref[...]
    quarter = att_ref.shape[1]
    mixture = dot(high_ref[...], back) + dot(low_ref[...], back)
    done[:, :quarter] = (att_ref[...] + mixture[:, :quarter]).astype(BF)
    done[:, quarter:] = mixture[:, quarter:].astype(BF)
    share = o0.shape[0]
    for j, o in enumerate((o0, o1, o2, o3)):
        start = pl.multiple_of(lax.rem(h_ref[0] + j, 4) * share, share)
        o[...] = done[pl.ds(start, share), :]


def join_body(h_ref, r0, r1, r2, r3, o_ref, held):
    quarter = o_ref.shape[1] // 4
    for j, r in enumerate((r0, r1, r2, r3)):
        held[lax.rem(h_ref[0] + 4 - j, 4)] = r[...]
    for q in range(4):
        o_ref[:, q * quarter : (q + 1) * quarter] = held[q, :, :quarter]


def shift(x, by):
    return lax.ppermute(x, "heads", [(i, (i + by) % 4) for i in range(4)])


def swap(x):
    return lax.ppermute(x, "core", [(0, 1), (1, 0)])


def plus(*terms):
    total = terms[0].astype(F32)
    for term in terms[1:]:
        total = total + term.astype(F32)
    return total.astype(BF)


def on_device(
    residual,
    query_rows,
    key_rows,
    value_rows,
    norm_gain,
    out_weight,
    moe_gain,
    expert_ids,
    gate_values,
    gate_weight,
    up_weight,
    down_weight,
):
    tokens, width = query_rows.shape
    features = residual.shape[1]
    quarter = features // 4
    padded = quarter + SPARE
    chip = ("z", "x")
    chips = lax.axis_size("z") * lax.axis_size("x")
    h = lax.axis_index("heads").astype(jnp.int32)
    core = lax.axis_index("core").astype(jnp.int32)
    h_arr = jnp.full((1,), h, jnp.int32)
    core_arr = jnp.full((1,), core, jnp.int32)
    place_arr = jnp.stack([h, core])
    capacity = min(tokens, 3 * tokens * expert_ids.shape[1] // (2 * chips))
    rows = chips * capacity
    shape = jax.ShapeDtypeStruct

    keep, send = pl.pallas_call(
        state_body,
        out_shape=(shape((HD // 2, width), BF),) * 2,
        in_specs=[SMEM_SPEC] + [VMEM_SPEC] * 2,
        out_specs=(VMEM_SPEC,) * 2,
        scratch_shapes=[pltpu.VMEM((2, HD // 2, width), BF)],
        compiler_params=params(),
        name="own_state",
    )(core_arr, key_rows, value_rows)
    taken = swap(send)
    inner = pl.pallas_call(
        inner_body,
        out_shape=shape((tokens, width), F32),
        in_specs=[VMEM_SPEC] * 3,
        out_specs=VMEM_SPEC,
        compiler_params=params(),
        cost_estimate=cost(2e9, 2e6),
        name="inner",
    )(query_rows, key_rows, value_rows)
    chip_state = plus(keep, taken)
    depth, breadth = lax.axis_size("z"), lax.axis_size("x")
    beside = [
        lax.ppermute(chip_state, "x", [(i, (i + j) % breadth) for i in range(breadth)])
        for j in range(1, breadth)
    ]
    slab_state = plus(chip_state, *beside)
    behind = [
        lax.ppermute(slab_state, "z", [(i, i + j) for i in range(depth - j)])
        for j in range(1, depth)
    ]
    base = jnp.zeros(keep.shape, F32)
    for j, term in enumerate(beside):
        base = base + jnp.where(lax.axis_index("x") > j, term.astype(F32), 0.0)
    for term in behind:
        base = base + term.astype(F32)
    later = lax.axis_index("core") == 1
    mine = (base + jnp.where(later, taken.astype(F32), 0.0)).astype(BF)
    theirs = (base + jnp.where(later, 0.0, keep.astype(F32))).astype(BF)
    other = swap(theirs)

    place, mix_high, mix_low = pl.pallas_call(
        functools.partial(route_body, chips),
        out_shape=(shape((rows, tokens), BF), shape((tokens, rows), BF), shape((tokens, rows), BF)),
        in_specs=[VMEM_SPEC] * 2,
        out_specs=(VMEM_SPEC,) * 3,
        compiler_params=params(),
        cost_estimate=cost(1e8, 1e6),
        name="route",
    )(expert_ids.T, gate_values.T)

    parts = pl.pallas_call(
        attend_body,
        out_shape=(shape((tokens, padded), BF),) * 4,
        in_specs=[SMEM_SPEC] + [VMEM_SPEC] * 6,
        out_specs=(VMEM_SPEC,) * 4,
        scratch_shapes=[pltpu.VMEM((tokens, width), BF), pltpu.VMEM((2, HD // 2, width), BF)],
        compiler_params=params(),
        name="attend",
    )(place_arr, query_rows, inner, mine, other, norm_gain.reshape(1, width), out_weight.T)
    pieces = [parts[0]] + [shift(parts[j], j) for j in (1, 2, 3)]

    gain = lax.dynamic_index_in_dim(moe_gain.reshape(4, 1, quarter), h, 0, keepdims=False)
    packed, attended = pl.pallas_call(
        pack_body,
        out_shape=(shape((rows, padded), BF), shape((tokens, quarter), F32)),
        in_specs=[SMEM_SPEC] + [VMEM_SPEC] * 7,
        out_specs=(VMEM_SPEC,) * 2,
        scratch_shapes=[pltpu.VMEM((tokens, padded), BF)],
        compiler_params=params(),
        name="pack",
    )(h_arr, *pieces, residual.T, gain, place)

    arrived = lax.all_to_all(
        packed.reshape(chips, capacity, padded), chip, 0, 0, tiled=True
    ).reshape(rows, padded)
    half = rows // 2
    low, high = arrived[:half], arrived[half:]
    minus_low, plus_high = shift(low, 1), shift(high, -1)
    minus_high, plus_low = shift(high, 1), shift(low, -1)
    far_low, far_high = shift(minus_low, 1), shift(plus_high, -1)
    own_sets = ((low, plus_low, far_low, minus_low), (high, plus_high, far_high, minus_high))
    other_sets = tuple(tuple(swap(x) for x in group) for group in own_sets)

    hidden_count = gate_weight.shape[2]
    stacked = shape((4, hidden_count, padded), BF)
    weights = pl.pallas_call(
        weights_body,
        out_shape=(stacked,) * 3,
        in_specs=[SMEM_SPEC] + [VMEM_SPEC] * 3,
        out_specs=(VMEM_SPEC,) * 3,
        compiler_params=params(),
        cost_estimate=cost(5e9, 13e6),
        name="weights",
    )(h_arr, gate_weight[0].T, up_weight[0].T, down_weight[0])

    def experts(group, added):
        if added:
            out_shape, out_specs = (shape((half, padded), BF),) * 4, (VMEM_SPEC,) * 4
        else:
            out_shape, out_specs = shape((4, half, padded), BF), VMEM_SPEC
        return pl.pallas_call(
            functools.partial(expert_body, features, bool(added)),
            out_shape=out_shape,
            in_specs=[VMEM_SPEC] * (7 + len(added)),
            out_specs=out_specs,
            scratch_shapes=[
                pltpu.VMEM((4, half, padded), BF),
                pltpu.VMEM((half, hidden_count), F32),
                pltpu.VMEM((half, hidden_count), F32),
            ],
            compiler_params=params(),
            cost_estimate=cost(6 * half * features * hidden_count, 12e6),
            name="experts",
        )(*group, *weights, *added)

    from_low = swap(experts(other_sets[0], ()))
    from_high = swap(experts(other_sets[1], ()))
    sum_low = experts(own_sets[0], (from_low,))
    sum_high = experts(own_sets[1], (from_high,))

    via_low, via_high = shift(sum_low[2], 1), shift(sum_high[2], -1)
    got_low_plus, got_high_minus = shift(sum_low[3], -1), shift(sum_high[1], 1)
    got_low_minus = shift(plus(sum_low[1], via_low), 1)
    got_high_plus = shift(plus(sum_high[3], via_high), -1)
    total_low = plus(sum_low[0], got_low_minus, got_low_plus)
    total_high = plus(sum_high[0], got_high_minus, got_high_plus)
    leaving = jnp.concatenate([total_low, total_high], axis=0).reshape(chips, capacity, padded)
    returned = lax.all_to_all(leaving, chip, 0, 0, tiled=True).reshape(rows, padded)

    share = tokens // 4
    ends = pl.pallas_call(
        mix_body,
        out_shape=(shape((share, padded), BF),) * 4,
        in_specs=[SMEM_SPEC] + [VMEM_SPEC] * 4,
        out_specs=(VMEM_SPEC,) * 4,
        scratch_shapes=[pltpu.VMEM((tokens, padded), BF)],
        compiler_params=params(),
        name="mix",
    )(h_arr, returned, mix_high, mix_low, attended)
    finals = [ends[0]] + [shift(ends[j], j) for j in (1, 2, 3)]
    return pl.pallas_call(
        join_body,
        out_shape=shape((share, features), BF),
        in_specs=[SMEM_SPEC] + [VMEM_SPEC] * 4,
        out_specs=VMEM_SPEC,
        scratch_shapes=[pltpu.VMEM((4, share, padded), BF)],
        compiler_params=params(),
        name="join",
    )(h_arr, *finals)


def solution(mesh):
    devices = mesh.devices
    split = Mesh(
        devices.reshape(-1, BREADTH, CORES, devices.shape[1]), ("z", "x", "core", "heads")
    )
    context = ("z", "x", "core")
    in_specs = (
        P(context, None),
        P(context, "heads"),
        P(context, "heads"),
        P(context, "heads"),
        P("heads"),
        P("heads", None),
        P(),
        P(context, None),
        P(context, None),
        P(context, None, "heads"),
        P(context, None, "heads"),
        P(context, "heads", None),
    )
    return jax.shard_map(
        on_device,
        mesh=split,
        in_specs=in_specs,
        out_specs=P(("z", "x", "core", "heads"), None),
        check_vma=False,
    )
```

```python
import functools

import jax
import jax.numpy as jnp
from jax import lax
from jax.experimental import pallas as pl
from jax.experimental.pallas import tpu as pltpu
from jax.sharding import Mesh
from jax.sharding import PartitionSpec as P

HD = 64
PAIR = 2 * HD
CORES = 2
BREADTH = 4
SPARE = 48
BF = jnp.bfloat16
F32 = jnp.float32
VMEM_SPEC = pl.BlockSpec(memory_space=pltpu.VMEM)
SMEM_SPEC = pl.BlockSpec(memory_space=pltpu.SMEM)


def params(mib):
    return pltpu.CompilerParams(vmem_limit_bytes=mib << 20)


def cost(flops, moved):
    return pl.CostEstimate(flops=int(flops), bytes_accessed=int(moved), transcendentals=0)


def dot(a, b, dims=((1,), (0,))):
    return lax.dot_general(a, b, (dims, ((), ())), preferred_element_type=F32)


def state_body(core_ref, k_ref, v_ref, keep_ref, send_ref, both_ref):
    first = lax.broadcasted_iota(jnp.int32, (HD, PAIR), 1) < HD
    half = HD // 2
    for p in range(k_ref.shape[1] // PAIR):
        cols = slice(p * PAIR, (p + 1) * PAIR)
        both = dot(k_ref[:, cols], v_ref[:, cols], ((0,), (0,)))
        state = jnp.where(first, both[:HD], both[HD:]).astype(BF)
        both_ref[0, :, cols] = state[:half]
        both_ref[1, :, cols] = state[half:]
    keep_ref[...] = both_ref[core_ref[0]]
    send_ref[...] = both_ref[1 - core_ref[0]]


def inner_body(q_ref, k_ref, v_ref, o_ref):
    tokens = q_ref.shape[0]
    first = lax.broadcasted_iota(jnp.int32, (tokens, PAIR), 1) < HD
    causal = lax.broadcasted_iota(jnp.int32, (tokens, tokens), 0) >= lax.broadcasted_iota(
        jnp.int32, (tokens, tokens), 1
    )
    zero = jnp.zeros((tokens, PAIR), BF)
    for p in range(q_ref.shape[1] // PAIR):
        cols = slice(p * PAIR, (p + 1) * PAIR)
        q, k, v = q_ref[:, cols], k_ref[:, cols], v_ref[:, cols]
        inner = []
        for keep in (jnp.where(first, q, zero), jnp.where(first, zero, q)):
            scores = dot(keep, k, ((1,), (1,)))
            weights = jnp.where(causal, scores, 0.0).astype(BF)
            inner.append(dot(weights, v))
        o_ref[:, cols] = jnp.where(first, inner[0], inner[1])


def attend_body(
    place_ref, q_ref, inner_ref, mine_ref, other_ref, gain_ref, w_ref, o0, o1, o2, o3, normed, state
):
    tokens = q_ref.shape[0]
    first = lax.broadcasted_iota(jnp.int32, (tokens, PAIR), 1) < HD
    first_s = lax.broadcasted_iota(jnp.int32, (HD, PAIR), 1) < HD
    state[place_ref[1]] = mine_ref[...]
    state[1 - place_ref[1]] = other_ref[...]

    def halves_mean(x):
        a = jnp.sum(jnp.where(first, x, 0.0), axis=1, keepdims=True)
        b = jnp.sum(jnp.where(first, 0.0, x), axis=1, keepdims=True)
        return jnp.where(first, a, b) * (1.0 / HD)

    for p in range(q_ref.shape[1] // PAIR):
        cols = slice(p * PAIR, (p + 1) * PAIR)
        s = jnp.concatenate([state[0, :, cols], state[1, :, cols]], axis=0)
        s_zero = jnp.zeros_like(s)
        block = jnp.concatenate(
            [jnp.where(first_s, s, s_zero), jnp.where(first_s, s_zero, s)], axis=0
        )
        mixed = inner_ref[:, cols] + dot(q_ref[:, cols], block)
        centered = mixed - halves_mean(mixed)
        spread = halves_mean(centered * centered)
        normed[:, cols] = (centered * lax.rsqrt(spread + 1e-05) * gain_ref[:, cols]).astype(BF)
    quarter = w_ref.shape[0] // 4
    pad = jnp.zeros((tokens, o0.shape[1] - quarter), BF)
    for j, o in enumerate((o0, o1, o2, o3)):
        start = pl.multiple_of(lax.rem(place_ref[0] + j, 4) * quarter, quarter)
        part = dot(normed[...], w_ref[pl.ds(start, quarter), :], ((1,), (1,)))
        o[:, :quarter] = part.astype(BF)
        o[:, quarter:] = pad


def route_body(experts, ids_ref, gates_ref, place_ref, high_ref, low_ref):
    top, tokens = ids_ref.shape
    rows = place_ref.shape[0]
    capacity = rows // experts
    expert = lax.broadcasted_iota(jnp.int32, (experts, tokens), 0)
    member = jnp.zeros((experts, tokens), F32)
    gate = jnp.zeros((experts, tokens), F32)
    for c in range(top):
        hit = ids_ref[c : c + 1, :] == expert
        member = member + jnp.where(hit, 1.0, 0.0)
        gate = gate + jnp.where(hit, gates_ref[c : c + 1, :], 0.0)
    earlier = lax.broadcasted_iota(jnp.int32, (tokens, tokens), 0) < lax.broadcasted_iota(
        jnp.int32, (tokens, tokens), 1
    )
    rank = dot(member.astype(BF), jnp.where(earlier, 1.0, 0.0).astype(BF))
    rank = jnp.where(member > 0.0, rank, -1.0)
    shape = (experts, capacity, tokens)
    slot = lax.broadcasted_iota(jnp.int32, shape, 1).astype(F32)
    placed = jnp.where(jnp.broadcast_to(rank[:, None, :], shape) == slot, 1.0, 0.0)
    weighted = (placed * jnp.broadcast_to(gate[:, None, :], shape)).reshape(rows, tokens)
    place_ref[...] = placed.reshape(rows, tokens).astype(BF)
    mix = weighted.T
    high = mix.astype(BF)
    high_ref[...] = high
    low_ref[...] = (mix - high.astype(F32)).astype(BF)


def pack_body(h_ref, p0, p1, p2, p3, res_ref, gain_ref, place_ref, packed_ref, att_ref, rows):
    quarter = att_ref.shape[1]
    start = pl.multiple_of(h_ref[0] * quarter, quarter)
    att = res_ref[pl.ds(start, quarter), :].astype(F32).T
    for p in (p0, p1, p2, p3):
        att = att + p[:, :quarter].astype(F32)
    att_ref[...] = att
    square = jnp.sum(att * att, axis=1, keepdims=True)
    high = square.astype(BF).astype(F32)
    middle = (square - high).astype(BF).astype(F32)
    low = square - high - middle
    lane = lax.broadcasted_iota(jnp.int32, (att.shape[0], SPARE), 1)
    extra = jnp.where(lane == 0, high, jnp.where(lane == 1, middle, jnp.where(lane == 2, low, 0.0)))
    rows[:, :quarter] = (att * gain_ref[...]).astype(BF)
    rows[:, quarter:] = extra.astype(BF)
    packed_ref[...] = dot(place_ref[...], rows[...]).astype(BF)


def weights_body(h_ref, gate_ref, up_ref, down_ref, mid_ref, out_ref):
    hidden, features = down_ref.shape
    quarter = features // 4
    padded = mid_ref.shape[1]
    wide = mid_ref.shape[2] // 2
    for q in range(4):
        place = lax.rem(q + 4 - h_ref[0], 4)
        cols = slice(q * quarter, (q + 1) * quarter)
        for side, ref in enumerate((gate_ref, up_ref)):
            lanes = slice(side * wide, (side + 1) * wide)
            tall = [ref[:, cols].astype(F32), jnp.zeros((wide - hidden, quarter), F32)]
            mid_ref[place, :quarter, lanes] = jnp.concatenate(tall, axis=0).T.astype(BF)
            mid_ref[place, quarter:, lanes] = jnp.zeros((padded - quarter, wide), BF)
        pad = jnp.zeros((hidden, padded - quarter), BF)
        out_ref[place] = jnp.concatenate([down_ref[:, cols], pad], axis=1)


def expert_body(features, added, x0, x1, x2, x3, mid_ref, out_ref, *rest):
    quarter = features // 4
    hidden_count = out_ref.shape[1]
    wide = mid_ref.shape[2] // 2
    both = square = None
    for j, x in enumerate((x0, x1, x2, x3)):
        tail = jnp.sum(x[:, quarter:].astype(F32), axis=1, keepdims=True)
        term = dot(x[...], mid_ref[j])
        both = term if j == 0 else both + term
        square = tail if j == 0 else square + tail
    scaling = lax.rsqrt(square * (1.0 / features) + 1e-06)
    gate = both[:, :hidden_count] * scaling
    up = both[:, wide : wide + hidden_count] * scaling
    hidden = (gate / (1.0 + jnp.exp(-gate)) * up).astype(BF)
    target = rest[-1] if added else rest[0]

    def spread(j, carry):
        part = dot(hidden, out_ref[j])
        if added:
            part = part + rest[0][j].astype(F32)
        target[j] = part.astype(BF)
        return carry

    lax.fori_loop(0, 4, spread, 0)
    if added:
        for j in range(4):
            rest[1 + j][...] = target[j]


def mix_body(h_ref, back_ref, high_ref, low_ref, att_ref, o0, o1, o2, o3, done):
    back = back_ref[...]
    quarter = att_ref.shape[1]
    mixture = dot(high_ref[...], back) + dot(low_ref[...], back)
    done[:, :quarter] = (att_ref[...] + mixture[:, :quarter]).astype(BF)
    done[:, quarter:] = mixture[:, quarter:].astype(BF)
    share = o0.shape[0]
    for j, o in enumerate((o0, o1, o2, o3)):
        start = pl.multiple_of(lax.rem(h_ref[0] + j, 4) * share, share)
        o[...] = done[pl.ds(start, share), :]


def join_body(h_ref, r0, r1, r2, r3, o_ref, held):
    quarter = o_ref.shape[1] // 4
    for j, r in enumerate((r0, r1, r2, r3)):
        held[lax.rem(h_ref[0] + 4 - j, 4)] = r[...]
    for q in range(4):
        o_ref[:, q * quarter : (q + 1) * quarter] = held[q, :, :quarter]


def shift(x, by):
    return lax.ppermute(x, "heads", [(i, (i + by) % 4) for i in range(4)])


def swap(x):
    return lax.ppermute(x, "core", [(0, 1), (1, 0)])


def plus(*terms):
    total = terms[0].astype(F32)
    for term in terms[1:]:
        total = total + term.astype(F32)
    return total.astype(BF)


def on_device(
    residual,
    query_rows,
    key_rows,
    value_rows,
    norm_gain,
    out_weight,
    moe_gain,
    expert_ids,
    gate_values,
    gate_weight,
    up_weight,
    down_weight,
):
    tokens, width = query_rows.shape
    features = residual.shape[1]
    quarter = features // 4
    padded = quarter + SPARE
    chip = ("z", "x")
    chips = lax.axis_size("z") * lax.axis_size("x")
    h = lax.axis_index("heads").astype(jnp.int32)
    core = lax.axis_index("core").astype(jnp.int32)
    h_arr = jnp.full((1,), h, jnp.int32)
    core_arr = jnp.full((1,), core, jnp.int32)
    place_arr = jnp.stack([h, core])
    capacity = min(tokens, 3 * tokens * expert_ids.shape[1] // (2 * chips))
    rows = chips * capacity
    shape = jax.ShapeDtypeStruct

    keep, send = pl.pallas_call(
        state_body,
        out_shape=(shape((HD // 2, width), BF),) * 2,
        in_specs=[SMEM_SPEC] + [VMEM_SPEC] * 2,
        out_specs=(VMEM_SPEC,) * 2,
        scratch_shapes=[pltpu.VMEM((2, HD // 2, width), BF)],
        compiler_params=params(8),
        name="own_state",
    )(core_arr, key_rows, value_rows)
    taken = swap(send)
    inner = pl.pallas_call(
        inner_body,
        out_shape=shape((tokens, width), F32),
        in_specs=[VMEM_SPEC] * 3,
        out_specs=VMEM_SPEC,
        compiler_params=params(8),
        cost_estimate=cost(2e9, 2e6),
        name="inner",
    )(query_rows, key_rows, value_rows)
    chip_state = plus(keep, taken)
    depth, breadth = lax.axis_size("z"), lax.axis_size("x")
    beside = [
        lax.ppermute(chip_state, "x", [(i, (i + j) % breadth) for i in range(breadth)])
        for j in range(1, breadth)
    ]
    slab_state = plus(chip_state, *beside)

    def down(x, j):
        return lax.ppermute(x, "z", [(i, i + j) for i in range(depth - j)])

    near = [down(slab_state, 1), down(slab_state, 2)]
    triple = plus(slab_state, *near)
    base = jnp.zeros(keep.shape, F32)
    for term in near + [down(triple, j) for j in range(3, depth, 3)]:
        base = base + term.astype(F32)
    for j, term in enumerate(beside):
        base = base + jnp.where(lax.axis_index("x") > j, term.astype(F32), 0.0)
    later = lax.axis_index("core") == 1
    mine = (base + jnp.where(later, taken.astype(F32), 0.0)).astype(BF)
    theirs = (base + jnp.where(later, 0.0, keep.astype(F32))).astype(BF)
    other = swap(theirs)

    place, mix_high, mix_low = pl.pallas_call(
        functools.partial(route_body, chips),
        out_shape=(shape((rows, tokens), BF), shape((tokens, rows), BF), shape((tokens, rows), BF)),
        in_specs=[VMEM_SPEC] * 2,
        out_specs=(VMEM_SPEC,) * 3,
        compiler_params=params(10),
        cost_estimate=cost(1e8, 1e6),
        name="route",
    )(expert_ids.T, gate_values.T)

    parts = pl.pallas_call(
        attend_body,
        out_shape=(shape((tokens, padded), BF),) * 4,
        in_specs=[SMEM_SPEC] + [VMEM_SPEC] * 6,
        out_specs=(VMEM_SPEC,) * 4,
        scratch_shapes=[pltpu.VMEM((tokens, width), BF), pltpu.VMEM((2, HD // 2, width), BF)],
        compiler_params=params(16),
        name="attend",
    )(place_arr, query_rows, inner, mine, other, norm_gain.reshape(1, width), out_weight.T)
    pieces = [parts[0]] + [shift(parts[j], j) for j in (1, 2, 3)]

    gain = lax.dynamic_index_in_dim(moe_gain.reshape(4, 1, quarter), h, 0, keepdims=False)
    packed, attended = pl.pallas_call(
        pack_body,
        out_shape=(shape((rows, padded), BF), shape((tokens, quarter), F32)),
        in_specs=[SMEM_SPEC] + [VMEM_SPEC] * 7,
        out_specs=(VMEM_SPEC,) * 2,
        scratch_shapes=[pltpu.VMEM((tokens, padded), BF)],
        compiler_params=params(12),
        name="pack",
    )(h_arr, *pieces, residual.T, gain, place)

    arrived = lax.all_to_all(
        packed.reshape(chips, capacity, padded), chip, 0, 0, tiled=True
    ).reshape(rows, padded)
    half = rows // 2
    hidden_count = gate_weight.shape[2]
    wide = -(-hidden_count // 128) * 128
    arrived, late_h = lax.optimization_barrier((arrived, h_arr))
    low, high = arrived[:half], arrived[half:]

    minus_low, plus_low = shift(low, 1), shift(low, -1)
    weights = pl.pallas_call(
        weights_body,
        out_shape=(shape((4, padded, 2 * wide), BF), shape((4, hidden_count, padded), BF)),
        in_specs=[SMEM_SPEC] + [VMEM_SPEC] * 3,
        out_specs=(VMEM_SPEC,) * 2,
        compiler_params=params(28),
        cost_estimate=cost(5e9, 13e6),
        name="weights",
    )(late_h, gate_weight[0].T, up_weight[0].T, down_weight[0])

    def experts(group, added):
        if added:
            out_shape, out_specs = (shape((half, padded), BF),) * 4, (VMEM_SPEC,) * 4
            scratch = [pltpu.VMEM((4, half, padded), BF)]
        else:
            out_shape, out_specs, scratch = shape((4, half, padded), BF), VMEM_SPEC, []
        return pl.pallas_call(
            functools.partial(expert_body, features, bool(added)),
            out_shape=out_shape,
            in_specs=[VMEM_SPEC] * (6 + len(added)),
            out_specs=out_specs,
            scratch_shapes=scratch,
            compiler_params=params(28),
            cost_estimate=cost(6 * half * features * hidden_count, 12e6),
            name="experts",
        )(*group, *weights, *added)

    swap_low = swap(low)
    minus_low, plus_low, high, weights = lax.optimization_barrier(
        (minus_low, plus_low, high, weights)
    )
    far_low, plus_high = shift(minus_low, 1), shift(high, -1)
    swap_plus_low, swap_minus_low, swap_high = swap(plus_low), swap(minus_low), swap(high)
    far_low, plus_high, high = lax.optimization_barrier((far_low, plus_high, high))
    far_high, minus_high = shift(plus_high, -1), shift(high, 1)
    swap_far_low, swap_plus_high = swap(far_low), swap(plus_high)
    part_low = experts((swap_low, swap_plus_low, swap_far_low, swap_minus_low), ())
    from_low = swap(part_low)
    far_high, minus_high, part_low = lax.optimization_barrier((far_high, minus_high, part_low))
    swap_far_high, swap_minus_high = swap(far_high), swap(minus_high)
    sum_low = experts((low, plus_low, far_low, minus_low), (from_low,))
    via_low, got_low_plus = shift(sum_low[2], 1), shift(sum_low[3], -1)
    sum_low, swap_far_high, swap_minus_high = lax.optimization_barrier(
        (sum_low, swap_far_high, swap_minus_high)
    )
    part_high = experts((swap_high, swap_plus_high, swap_far_high, swap_minus_high), ())
    from_high = swap(part_high)
    sum_high = experts((high, plus_high, far_high, minus_high), (from_high,))
    via_low, got_low_plus, sum_high = lax.optimization_barrier((via_low, got_low_plus, sum_high))
    got_low_minus = shift(plus(sum_low[1], via_low), 1)
    via_high = shift(sum_high[2], -1)
    got_low_minus, via_high, sum_high = lax.optimization_barrier((got_low_minus, via_high, sum_high))
    got_high_minus = shift(sum_high[1], 1)
    got_high_plus = shift(plus(sum_high[3], via_high), -1)
    total_low = plus(sum_low[0], got_low_minus, got_low_plus)
    total_high = plus(sum_high[0], got_high_minus, got_high_plus)
    leaving = jnp.concatenate([total_low, total_high], axis=0).reshape(chips, capacity, padded)
    returned = lax.all_to_all(leaving, chip, 0, 0, tiled=True).reshape(rows, padded)

    share = tokens // 4
    ends = pl.pallas_call(
        mix_body,
        out_shape=(shape((share, padded), BF),) * 4,
        in_specs=[SMEM_SPEC] + [VMEM_SPEC] * 4,
        out_specs=(VMEM_SPEC,) * 4,
        scratch_shapes=[pltpu.VMEM((tokens, padded), BF)],
        compiler_params=params(10),
        name="mix",
    )(h_arr, returned, mix_high, mix_low, attended)
    finals = [ends[0]] + [shift(ends[j], j) for j in (1, 2, 3)]
    return pl.pallas_call(
        join_body,
        out_shape=shape((share, features), BF),
        in_specs=[SMEM_SPEC] + [VMEM_SPEC] * 4,
        out_specs=VMEM_SPEC,
        scratch_shapes=[pltpu.VMEM((4, share, padded), BF)],
        compiler_params=params(6),
        name="join",
    )(h_arr, *finals)


def solution(mesh):
    devices = mesh.devices
    split = Mesh(
        devices.reshape(-1, BREADTH, CORES, devices.shape[1]), ("z", "x", "core", "heads")
    )
    context = ("z", "x", "core")
    in_specs = (
        P(context, None),
        P(context, "heads"),
        P(context, "heads"),
        P(context, "heads"),
        P("heads"),
        P("heads", None),
        P(),
        P(context, None),
        P(context, None),
        P(context, None, "heads"),
        P(context, None, "heads"),
        P(context, "heads", None),
    )
    return jax.shard_map(
        on_device,
        mesh=split,
        in_specs=in_specs,
        out_specs=P(("z", "x", "core", "heads"), None),
        check_vma=False,
    )
```

```python
import functools

import jax
import jax.numpy as jnp
from jax import lax
from jax.experimental import pallas as pl
from jax.experimental.pallas import tpu as pltpu
from jax.sharding import Mesh
from jax.sharding import PartitionSpec as P

HD = 64
PAIR = 2 * HD
CORES = 2
BREADTH = 4
SPARE = 48
BF = jnp.bfloat16
F32 = jnp.float32
VMEM_SPEC = pl.BlockSpec(memory_space=pltpu.VMEM)
SMEM_SPEC = pl.BlockSpec(memory_space=pltpu.SMEM)


def params(mib):
    return pltpu.CompilerParams(vmem_limit_bytes=mib << 20)


def cost(flops, moved):
    return pl.CostEstimate(flops=int(flops), bytes_accessed=int(moved), transcendentals=0)


def dot(a, b, dims=((1,), (0,))):
    return lax.dot_general(a, b, (dims, ((), ())), preferred_element_type=F32)


def state_body(core_ref, k_ref, v_ref, keep_ref, send_ref, both_ref):
    first = lax.broadcasted_iota(jnp.int32, (HD, PAIR), 1) < HD
    half = HD // 2
    for p in range(k_ref.shape[1] // PAIR):
        cols = slice(p * PAIR, (p + 1) * PAIR)
        both = dot(k_ref[:, cols], v_ref[:, cols], ((0,), (0,)))
        state = jnp.where(first, both[:HD], both[HD:]).astype(BF)
        both_ref[0, :, cols] = state[:half]
        both_ref[1, :, cols] = state[half:]
    keep_ref[...] = both_ref[core_ref[0]]
    send_ref[...] = both_ref[1 - core_ref[0]]


def inner_body(q_ref, k_ref, v_ref, o_ref):
    tokens = q_ref.shape[0]
    first = lax.broadcasted_iota(jnp.int32, (tokens, PAIR), 1) < HD
    causal = lax.broadcasted_iota(jnp.int32, (tokens, tokens), 0) >= lax.broadcasted_iota(
        jnp.int32, (tokens, tokens), 1
    )
    zero = jnp.zeros((tokens, PAIR), BF)
    for p in range(q_ref.shape[1] // PAIR):
        cols = slice(p * PAIR, (p + 1) * PAIR)
        q, k, v = q_ref[:, cols], k_ref[:, cols], v_ref[:, cols]
        inner = []
        for keep in (jnp.where(first, q, zero), jnp.where(first, zero, q)):
            scores = dot(keep, k, ((1,), (1,)))
            weights = jnp.where(causal, scores, 0.0).astype(BF)
            inner.append(dot(weights, v))
        o_ref[:, cols] = jnp.where(first, inner[0], inner[1])


def attend_body(
    place_ref, q_ref, inner_ref, mine_ref, other_ref, gain_ref, w_ref, o0, o1, o2, o3, normed, state
):
    tokens = q_ref.shape[0]
    first = lax.broadcasted_iota(jnp.int32, (tokens, PAIR), 1) < HD
    first_s = lax.broadcasted_iota(jnp.int32, (HD, PAIR), 1) < HD
    state[place_ref[1]] = mine_ref[...]
    state[1 - place_ref[1]] = other_ref[...]

    def halves_mean(x):
        a = jnp.sum(jnp.where(first, x, 0.0), axis=1, keepdims=True)
        b = jnp.sum(jnp.where(first, 0.0, x), axis=1, keepdims=True)
        return jnp.where(first, a, b) * (1.0 / HD)

    for p in range(q_ref.shape[1] // PAIR):
        cols = slice(p * PAIR, (p + 1) * PAIR)
        s = jnp.concatenate([state[0, :, cols], state[1, :, cols]], axis=0)
        s_zero = jnp.zeros_like(s)
        block = jnp.concatenate(
            [jnp.where(first_s, s, s_zero), jnp.where(first_s, s_zero, s)], axis=0
        )
        mixed = inner_ref[:, cols] + dot(q_ref[:, cols], block)
        centered = mixed - halves_mean(mixed)
        spread = halves_mean(centered * centered)
        normed[:, cols] = (centered * lax.rsqrt(spread + 1e-05) * gain_ref[:, cols]).astype(BF)
    quarter = w_ref.shape[0] // 4
    pad = jnp.zeros((tokens, o0.shape[1] - quarter), BF)
    for j, o in enumerate((o0, o1, o2, o3)):
        start = pl.multiple_of(lax.rem(place_ref[0] + j, 4) * quarter, quarter)
        part = dot(normed[...], w_ref[pl.ds(start, quarter), :], ((1,), (1,)))
        o[:, :quarter] = part.astype(BF)
        o[:, quarter:] = pad


def route_body(experts, ids_ref, gates_ref, place_ref, high_ref, low_ref):
    top, tokens = ids_ref.shape
    rows = place_ref.shape[0]
    capacity = rows // experts
    expert = lax.broadcasted_iota(jnp.int32, (experts, tokens), 0)
    member = jnp.zeros((experts, tokens), F32)
    gate = jnp.zeros((experts, tokens), F32)
    for c in range(top):
        hit = ids_ref[c : c + 1, :] == expert
        member = member + jnp.where(hit, 1.0, 0.0)
        gate = gate + jnp.where(hit, gates_ref[c : c + 1, :], 0.0)
    earlier = lax.broadcasted_iota(jnp.int32, (tokens, tokens), 0) < lax.broadcasted_iota(
        jnp.int32, (tokens, tokens), 1
    )
    rank = dot(member.astype(BF), jnp.where(earlier, 1.0, 0.0).astype(BF))
    rank = jnp.where(member > 0.0, rank, -1.0)
    shape = (experts, capacity, tokens)
    slot = lax.broadcasted_iota(jnp.int32, shape, 1).astype(F32)
    placed = jnp.where(jnp.broadcast_to(rank[:, None, :], shape) == slot, 1.0, 0.0)
    weighted = (placed * jnp.broadcast_to(gate[:, None, :], shape)).reshape(rows, tokens)
    place_ref[...] = placed.reshape(rows, tokens).astype(BF)
    mix = weighted.T
    high = mix.astype(BF)
    high_ref[...] = high
    low_ref[...] = (mix - high.astype(F32)).astype(BF)


def pack_body(h_ref, p0, p1, p2, p3, res_ref, gain_ref, place_ref, packed_ref, att_ref, rows):
    quarter = att_ref.shape[1]
    start = pl.multiple_of(h_ref[0] * quarter, quarter)
    att = res_ref[pl.ds(start, quarter), :].astype(F32).T
    for p in (p0, p1, p2, p3):
        att = att + p[:, :quarter].astype(F32)
    att_ref[...] = att
    square = jnp.sum(att * att, axis=1, keepdims=True)
    high = square.astype(BF).astype(F32)
    middle = (square - high).astype(BF).astype(F32)
    low = square - high - middle
    lane = lax.broadcasted_iota(jnp.int32, (att.shape[0], SPARE), 1)
    extra = jnp.where(lane == 0, high, jnp.where(lane == 1, middle, jnp.where(lane == 2, low, 0.0)))
    rows[:, :quarter] = (att * gain_ref[...]).astype(BF)
    rows[:, quarter:] = extra.astype(BF)
    packed_ref[...] = dot(place_ref[...], rows[...]).astype(BF)


def weights_body(h_ref, gate_ref, up_ref, down_ref, mid_ref, out_ref):
    hidden, features = down_ref.shape
    quarter = features // 4
    padded = mid_ref.shape[1]
    wide = mid_ref.shape[2] // 2
    for q in range(4):
        place = lax.rem(q + 4 - h_ref[0], 4)
        cols = slice(q * quarter, (q + 1) * quarter)
        for side, ref in enumerate((gate_ref, up_ref)):
            lanes = slice(side * wide, (side + 1) * wide)
            tall = [ref[:, cols].astype(F32), jnp.zeros((wide - hidden, quarter), F32)]
            mid_ref[place, :quarter, lanes] = jnp.concatenate(tall, axis=0).T.astype(BF)
            mid_ref[place, quarter:, lanes] = jnp.zeros((padded - quarter, wide), BF)
        pad = jnp.zeros((hidden, padded - quarter), BF)
        out_ref[place] = jnp.concatenate([down_ref[:, cols], pad], axis=1)


def expert_body(features, x0, x1, x2, x3, mid0, out0, mid1, out1, t0, t1, t2, t3, done):
    quarter = features // 4
    hidden_count = out0.shape[1]
    wide = mid0.shape[2] // 2
    square = None
    for j, x in enumerate((x0, x1, x2, x3)):
        tail = jnp.sum(x[:, quarter:].astype(F32), axis=1, keepdims=True)
        square = tail if j == 0 else square + tail
    scaling = lax.rsqrt(square * (1.0 / features) + 1e-06)
    hidden = []
    for mid in (mid0, mid1):
        both = None
        for j, x in enumerate((x0, x1, x2, x3)):
            term = dot(x[...], mid[j])
            both = term if j == 0 else both + term
        gate = both[:, :hidden_count] * scaling
        up = both[:, wide : wide + hidden_count] * scaling
        hidden.append((gate / (1.0 + jnp.exp(-gate)) * up).astype(BF))

    def spread(j, carry):
        done[j] = (dot(hidden[0], out0[j]) + dot(hidden[1], out1[j])).astype(BF)
        return carry

    lax.fori_loop(0, 4, spread, 0)
    for j, t in enumerate((t0, t1, t2, t3)):
        t[...] = done[j]


def mix_body(h_ref, back_ref, high_ref, low_ref, att_ref, o0, o1, o2, o3, done):
    back = back_ref[...]
    quarter = att_ref.shape[1]
    mixture = dot(high_ref[...], back) + dot(low_ref[...], back)
    done[:, :quarter] = (att_ref[...] + mixture[:, :quarter]).astype(BF)
    done[:, quarter:] = mixture[:, quarter:].astype(BF)
    share = o0.shape[0]
    for j, o in enumerate((o0, o1, o2, o3)):
        start = pl.multiple_of(lax.rem(h_ref[0] + j, 4) * share, share)
        o[...] = done[pl.ds(start, share), :]


def join_body(h_ref, r0, r1, r2, r3, o_ref, held):
    quarter = o_ref.shape[1] // 4
    for j, r in enumerate((r0, r1, r2, r3)):
        held[lax.rem(h_ref[0] + 4 - j, 4)] = r[...]
    for q in range(4):
        o_ref[:, q * quarter : (q + 1) * quarter] = held[q, :, :quarter]


def shift(x, by):
    return lax.ppermute(x, "heads", [(i, (i + by) % 4) for i in range(4)])


def swap(x):
    return lax.ppermute(x, "core", [(0, 1), (1, 0)])


def plus(*terms):
    total = terms[0].astype(F32)
    for term in terms[1:]:
        total = total + term.astype(F32)
    return total.astype(BF)


def on_device(
    residual,
    query_rows,
    key_rows,
    value_rows,
    norm_gain,
    out_weight,
    moe_gain,
    expert_ids,
    gate_values,
    gate_weight,
    up_weight,
    down_weight,
):
    tokens, width = query_rows.shape
    features = residual.shape[1]
    quarter = features // 4
    padded = quarter + SPARE
    chip = ("z", "x")
    chips = lax.axis_size("z") * lax.axis_size("x")
    h = lax.axis_index("heads").astype(jnp.int32)
    core = lax.axis_index("core").astype(jnp.int32)
    h_arr = jnp.full((1,), h, jnp.int32)
    core_arr = jnp.full((1,), core, jnp.int32)
    place_arr = jnp.stack([h, core])
    capacity = min(tokens, 3 * tokens * expert_ids.shape[1] // (2 * chips))
    rows = chips * capacity
    shape = jax.ShapeDtypeStruct

    keep, send = pl.pallas_call(
        state_body,
        out_shape=(shape((HD // 2, width), BF),) * 2,
        in_specs=[SMEM_SPEC] + [VMEM_SPEC] * 2,
        out_specs=(VMEM_SPEC,) * 2,
        scratch_shapes=[pltpu.VMEM((2, HD // 2, width), BF)],
        compiler_params=params(8),
        name="own_state",
    )(core_arr, key_rows, value_rows)
    taken = swap(send)
    hidden_count = gate_weight.shape[2]
    wide = -(-hidden_count // 128) * 128
    weights = pl.pallas_call(
        weights_body,
        out_shape=(shape((4, padded, 2 * wide), BF), shape((4, hidden_count, padded), BF)),
        in_specs=[SMEM_SPEC] + [VMEM_SPEC] * 3,
        out_specs=(VMEM_SPEC,) * 2,
        compiler_params=params(28),
        cost_estimate=cost(5e9, 13e6),
        name="weights",
    )(h_arr, gate_weight[0].T, up_weight[0].T, down_weight[0])
    inner = pl.pallas_call(
        inner_body,
        out_shape=shape((tokens, width), F32),
        in_specs=[VMEM_SPEC] * 3,
        out_specs=VMEM_SPEC,
        compiler_params=params(8),
        cost_estimate=cost(2e9, 2e6),
        name="inner",
    )(query_rows, key_rows, value_rows)
    chip_state = plus(keep, taken)
    depth, breadth = lax.axis_size("z"), lax.axis_size("x")
    beside = [
        lax.ppermute(chip_state, "x", [(i, (i + j) % breadth) for i in range(breadth)])
        for j in range(1, breadth)
    ]
    beside, weights = lax.optimization_barrier((beside, weights))
    other_weights = tuple(swap(x) for x in weights)
    slab_state = plus(chip_state, *beside)

    def deeper(x, j):
        moved = lax.ppermute(x, "z", [(i, (i + j) % depth) for i in range(depth)])
        return jnp.where(lax.axis_index("z") >= j, moved.astype(F32), 0.0)

    near = [deeper(slab_state, 1), deeper(slab_state, 2)]
    triple = plus(slab_state, *near)
    base = jnp.zeros(keep.shape, F32)
    for term in near + [deeper(triple, j) for j in range(3, depth, 3)]:
        base = base + term
    for j, term in enumerate(beside):
        base = base + jnp.where(lax.axis_index("x") > j, term.astype(F32), 0.0)
    later = lax.axis_index("core") == 1
    mine = (base + jnp.where(later, taken.astype(F32), 0.0)).astype(BF)
    theirs = (base + jnp.where(later, 0.0, keep.astype(F32))).astype(BF)
    other = swap(theirs)

    place, mix_high, mix_low = pl.pallas_call(
        functools.partial(route_body, chips),
        out_shape=(shape((rows, tokens), BF), shape((tokens, rows), BF), shape((tokens, rows), BF)),
        in_specs=[VMEM_SPEC] * 2,
        out_specs=(VMEM_SPEC,) * 3,
        compiler_params=params(10),
        cost_estimate=cost(1e8, 1e6),
        name="route",
    )(expert_ids.T, gate_values.T)

    parts = pl.pallas_call(
        attend_body,
        out_shape=(shape((tokens, padded), BF),) * 4,
        in_specs=[SMEM_SPEC] + [VMEM_SPEC] * 6,
        out_specs=(VMEM_SPEC,) * 4,
        scratch_shapes=[pltpu.VMEM((tokens, width), BF), pltpu.VMEM((2, HD // 2, width), BF)],
        compiler_params=params(16),
        name="attend",
    )(place_arr, query_rows, inner, mine, other, norm_gain.reshape(1, width), out_weight.T)
    pieces = [parts[0]] + [shift(parts[j], j) for j in (1, 2, 3)]

    gain = lax.dynamic_index_in_dim(moe_gain.reshape(4, 1, quarter), h, 0, keepdims=False)
    packed, attended = pl.pallas_call(
        pack_body,
        out_shape=(shape((rows, padded), BF), shape((tokens, quarter), F32)),
        in_specs=[SMEM_SPEC] + [VMEM_SPEC] * 7,
        out_specs=(VMEM_SPEC,) * 2,
        scratch_shapes=[pltpu.VMEM((tokens, padded), BF)],
        compiler_params=params(12),
        name="pack",
    )(h_arr, *pieces, residual.T, gain, place)

    arrived = lax.all_to_all(
        packed.reshape(chips, capacity, padded), chip, 0, 0, tiled=True
    ).reshape(rows, padded)
    half = rows // 2
    low, high = arrived[:half], arrived[half:]

    def experts(group):
        return pl.pallas_call(
            functools.partial(expert_body, features),
            out_shape=(shape((half, padded), BF),) * 4,
            in_specs=[VMEM_SPEC] * 8,
            out_specs=(VMEM_SPEC,) * 4,
            scratch_shapes=[pltpu.VMEM((4, half, padded), BF)],
            compiler_params=params(36),
            cost_estimate=cost(1e6, 1e5),
            name="experts",
        )(*group, *weights, *other_weights)

    minus_low, plus_low = shift(low, 1), shift(low, -1)
    minus_low, plus_low, high = lax.optimization_barrier((minus_low, plus_low, high))
    far_low, plus_high = shift(minus_low, 1), shift(high, -1)
    far_low, plus_high, high = lax.optimization_barrier((far_low, plus_high, high))
    far_high, minus_high = shift(plus_high, -1), shift(high, 1)
    sum_low = experts((low, plus_low, far_low, minus_low))
    far_high, minus_high, sum_low = lax.optimization_barrier((far_high, minus_high, sum_low))
    via_low, got_low_plus = shift(sum_low[2], 1), shift(sum_low[3], -1)
    sum_high = experts((high, plus_high, far_high, minus_high))
    via_low, got_low_plus, sum_high = lax.optimization_barrier((via_low, got_low_plus, sum_high))
    got_low_minus = shift(plus(sum_low[1], via_low), 1)
    via_high = shift(sum_high[2], -1)
    got_low_minus, via_high, sum_high = lax.optimization_barrier((got_low_minus, via_high, sum_high))
    got_high_minus = shift(sum_high[1], 1)
    got_high_plus = shift(plus(sum_high[3], via_high), -1)
    total_low = plus(sum_low[0], got_low_minus, got_low_plus)
    total_high = plus(sum_high[0], got_high_minus, got_high_plus)
    leaving = jnp.concatenate([total_low, total_high], axis=0).reshape(chips, capacity, padded)
    returned = lax.all_to_all(leaving, chip, 0, 0, tiled=True).reshape(rows, padded)

    share = tokens // 4
    ends = pl.pallas_call(
        mix_body,
        out_shape=(shape((share, padded), BF),) * 4,
        in_specs=[SMEM_SPEC] + [VMEM_SPEC] * 4,
        out_specs=(VMEM_SPEC,) * 4,
        scratch_shapes=[pltpu.VMEM((tokens, padded), BF)],
        compiler_params=params(10),
        name="mix",
    )(h_arr, returned, mix_high, mix_low, attended)
    finals = [ends[0]] + [shift(ends[j], j) for j in (1, 2, 3)]
    return pl.pallas_call(
        join_body,
        out_shape=shape((share, features), BF),
        in_specs=[SMEM_SPEC] + [VMEM_SPEC] * 4,
        out_specs=VMEM_SPEC,
        scratch_shapes=[pltpu.VMEM((4, share, padded), BF)],
        compiler_params=params(6),
        name="join",
    )(h_arr, *finals)


def solution(mesh):
    devices = mesh.devices
    split = Mesh(
        devices.reshape(-1, BREADTH, CORES, devices.shape[1]), ("z", "x", "core", "heads")
    )
    context = ("z", "x", "core")
    in_specs = (
        P(context, None),
        P(context, "heads"),
        P(context, "heads"),
        P(context, "heads"),
        P("heads"),
        P("heads", None),
        P(),
        P(context, None),
        P(context, None),
        P(context, None, "heads"),
        P(context, None, "heads"),
        P(context, "heads", None),
    )
    return jax.shard_map(
        on_device,
        mesh=split,
        in_specs=in_specs,
        out_specs=P(("z", "x", "core", "heads"), None),
        check_vma=False,
    )
```

```python
import functools

import jax
import jax.numpy as jnp
from jax import lax
from jax.experimental import pallas as pl
from jax.experimental.pallas import tpu as pltpu
from jax.sharding import Mesh
from jax.sharding import PartitionSpec as P

HD = 64
PAIR = 2 * HD
CORES = 2
BREADTH = 4
SPARE = 48
BF = jnp.bfloat16
F32 = jnp.float32
VMEM_SPEC = pl.BlockSpec(memory_space=pltpu.VMEM)
SMEM_SPEC = pl.BlockSpec(memory_space=pltpu.SMEM)


def params(mib):
    return pltpu.CompilerParams(vmem_limit_bytes=mib << 20)


def cost(flops, moved):
    return pl.CostEstimate(flops=int(flops), bytes_accessed=int(moved), transcendentals=0)


def dot(a, b, dims=((1,), (0,))):
    return lax.dot_general(a, b, (dims, ((), ())), preferred_element_type=F32)


def state_body(core_ref, k_ref, v_ref, keep_ref, send_ref, both_ref):
    first = lax.broadcasted_iota(jnp.int32, (HD, PAIR), 1) < HD
    half = HD // 2
    for p in range(k_ref.shape[1] // PAIR):
        cols = slice(p * PAIR, (p + 1) * PAIR)
        both = dot(k_ref[:, cols], v_ref[:, cols], ((0,), (0,)))
        state = jnp.where(first, both[:HD], both[HD:]).astype(BF)
        both_ref[0, :, cols] = state[:half]
        both_ref[1, :, cols] = state[half:]
    keep_ref[...] = both_ref[core_ref[0]]
    send_ref[...] = both_ref[1 - core_ref[0]]


def inner_body(q_ref, k_ref, v_ref, o_ref):
    tokens = q_ref.shape[0]
    first = lax.broadcasted_iota(jnp.int32, (tokens, PAIR), 1) < HD
    causal = lax.broadcasted_iota(jnp.int32, (tokens, tokens), 0) >= lax.broadcasted_iota(
        jnp.int32, (tokens, tokens), 1
    )
    zero = jnp.zeros((tokens, PAIR), BF)
    for p in range(q_ref.shape[1] // PAIR):
        cols = slice(p * PAIR, (p + 1) * PAIR)
        q, k, v = q_ref[:, cols], k_ref[:, cols], v_ref[:, cols]
        inner = []
        for keep in (jnp.where(first, q, zero), jnp.where(first, zero, q)):
            scores = dot(keep, k, ((1,), (1,)))
            weights = jnp.where(causal, scores, 0.0).astype(BF)
            inner.append(dot(weights, v))
        o_ref[:, cols] = jnp.where(first, inner[0], inner[1])


def attend_body(
    place_ref, q_ref, inner_ref, mine_ref, other_ref, gain_ref, w_hbm, o0, o1, o2, o3, normed, state, w_ref, parts, sem
):
    fetch = pltpu.make_async_copy(w_hbm, w_ref, sem)
    fetch.start()
    tokens = q_ref.shape[0]
    first = lax.broadcasted_iota(jnp.int32, (tokens, PAIR), 1) < HD
    first_s = lax.broadcasted_iota(jnp.int32, (HD, PAIR), 1) < HD
    state[place_ref[1]] = mine_ref[...]
    state[1 - place_ref[1]] = other_ref[...]

    def halves_mean(x):
        a = jnp.sum(jnp.where(first, x, 0.0), axis=1, keepdims=True)
        b = jnp.sum(jnp.where(first, 0.0, x), axis=1, keepdims=True)
        return jnp.where(first, a, b) * (1.0 / HD)

    for p in range(q_ref.shape[1] // PAIR):
        cols = slice(p * PAIR, (p + 1) * PAIR)
        s = jnp.concatenate([state[0, :, cols], state[1, :, cols]], axis=0)
        s_zero = jnp.zeros_like(s)
        block = jnp.concatenate(
            [jnp.where(first_s, s, s_zero), jnp.where(first_s, s_zero, s)], axis=0
        )
        mixed = inner_ref[:, cols] + dot(q_ref[:, cols], block)
        centered = mixed - halves_mean(mixed)
        spread = halves_mean(centered * centered)
        normed[:, cols] = (centered * lax.rsqrt(spread + 1e-05) * gain_ref[:, cols]).astype(BF)
    quarter = w_ref.shape[0] // 4
    pad = jnp.zeros((tokens, o0.shape[1] - quarter), BF)
    fetch.wait()

    def project(j, carry):
        start = pl.multiple_of(lax.rem(place_ref[0] + j, 4) * quarter, quarter)
        part = dot(normed[...], w_ref[pl.ds(start, quarter), :], ((1,), (1,)))
        parts[j, :, :quarter] = part.astype(BF)
        parts[j, :, quarter:] = pad
        return carry

    lax.fori_loop(0, 4, project, 0)
    for j, o in enumerate((o0, o1, o2, o3)):
        o[...] = parts[j]


def route_body(experts, ids_ref, gates_ref, place_ref, high_ref, low_ref):
    top, tokens = ids_ref.shape
    rows = place_ref.shape[0]
    capacity = rows // experts
    expert = lax.broadcasted_iota(jnp.int32, (experts, tokens), 0)
    member = jnp.zeros((experts, tokens), F32)
    gate = jnp.zeros((experts, tokens), F32)
    for c in range(top):
        hit = ids_ref[c : c + 1, :] == expert
        member = member + jnp.where(hit, 1.0, 0.0)
        gate = gate + jnp.where(hit, gates_ref[c : c + 1, :], 0.0)
    earlier = lax.broadcasted_iota(jnp.int32, (tokens, tokens), 0) < lax.broadcasted_iota(
        jnp.int32, (tokens, tokens), 1
    )
    rank = dot(member.astype(BF), jnp.where(earlier, 1.0, 0.0).astype(BF))
    rank = jnp.where(member > 0.0, rank, -1.0)
    shape = (experts, capacity, tokens)
    slot = lax.broadcasted_iota(jnp.int32, shape, 1).astype(F32)
    placed = jnp.where(jnp.broadcast_to(rank[:, None, :], shape) == slot, 1.0, 0.0)
    weighted = (placed * jnp.broadcast_to(gate[:, None, :], shape)).reshape(rows, tokens)
    place_ref[...] = placed.reshape(rows, tokens).astype(BF)
    mix = weighted.T
    high = mix.astype(BF)
    high_ref[...] = high
    low_ref[...] = (mix - high.astype(F32)).astype(BF)


def pack_body(h_ref, p0, p1, p2, p3, res_ref, gain_ref, place_ref, packed_ref, att_ref, rows):
    quarter = att_ref.shape[1]
    start = pl.multiple_of(h_ref[0] * quarter, quarter)
    att = res_ref[pl.ds(start, quarter), :].astype(F32).T
    for p in (p0, p1, p2, p3):
        att = att + p[:, :quarter].astype(F32)
    att_ref[...] = att
    square = jnp.sum(att * att, axis=1, keepdims=True)
    high = square.astype(BF).astype(F32)
    middle = (square - high).astype(BF).astype(F32)
    low = square - high - middle
    lane = lax.broadcasted_iota(jnp.int32, (att.shape[0], SPARE), 1)
    extra = jnp.where(lane == 0, high, jnp.where(lane == 1, middle, jnp.where(lane == 2, low, 0.0)))
    rows[:, :quarter] = (att * gain_ref[...]).astype(BF)
    rows[:, quarter:] = extra.astype(BF)
    packed_ref[...] = dot(place_ref[...], rows[...]).astype(BF)


def weights_body(h_ref, gate_ref, up_ref, down_ref, mid_ref, out_ref):
    hidden, features = down_ref.shape
    quarter = features // 4
    padded = mid_ref.shape[1]
    wide = mid_ref.shape[2] // 2
    for q in range(4):
        place = lax.rem(q + 4 - h_ref[0], 4)
        cols = slice(q * quarter, (q + 1) * quarter)
        for side, ref in enumerate((gate_ref, up_ref)):
            lanes = slice(side * wide, (side + 1) * wide)
            tall = [ref[:, cols].astype(F32), jnp.zeros((wide - hidden, quarter), F32)]
            mid_ref[place, :quarter, lanes] = jnp.concatenate(tall, axis=0).T.astype(BF)
            mid_ref[place, quarter:, lanes] = jnp.zeros((padded - quarter, wide), BF)
        pad = jnp.zeros((hidden, padded - quarter), BF)
        out_ref[place] = jnp.concatenate([down_ref[:, cols], pad], axis=1)


def expert_body(features, x0, x1, x2, x3, mid0, out0, mid1, out1, t0, t1, t2, t3, held, total):
    quarter = features // 4
    hidden_count = out0.shape[1]
    wide = mid0.shape[2] // 2
    square = None
    for j, x in enumerate((x0, x1, x2, x3)):
        held[j] = x[...]
        tail = jnp.sum(x[:, quarter:].astype(F32), axis=1, keepdims=True)
        square = tail if j == 0 else square + tail
    scaling = lax.rsqrt(square * (1.0 / features) + 1e-06)
    total[...] = jnp.zeros_like(total)

    def gather(j, carry):
        row = held[j]
        total[0] += dot(row, mid0[j])
        total[1] += dot(row, mid1[j])
        return carry

    lax.fori_loop(0, 4, gather, 0)
    hidden = []
    for side in range(2):
        gate = total[side, :, :hidden_count] * scaling
        up = total[side, :, wide : wide + hidden_count] * scaling
        hidden.append((gate / (1.0 + jnp.exp(-gate)) * up).astype(BF))

    def spread(j, carry):
        held[j] = (dot(hidden[0], out0[j]) + dot(hidden[1], out1[j])).astype(BF)
        return carry

    lax.fori_loop(0, 4, spread, 0)
    for j, t in enumerate((t0, t1, t2, t3)):
        t[...] = held[j]


def mix_body(h_ref, back_ref, high_ref, low_ref, att_ref, o0, o1, o2, o3, done):
    back = back_ref[...]
    quarter = att_ref.shape[1]
    mixture = dot(high_ref[...], back) + dot(low_ref[...], back)
    done[:, :quarter] = (att_ref[...] + mixture[:, :quarter]).astype(BF)
    done[:, quarter:] = mixture[:, quarter:].astype(BF)
    share = o0.shape[0]
    for j, o in enumerate((o0, o1, o2, o3)):
        start = pl.multiple_of(lax.rem(h_ref[0] + j, 4) * share, share)
        o[...] = done[pl.ds(start, share), :]


def join_body(h_ref, r0, r1, r2, r3, o_ref, held):
    quarter = o_ref.shape[1] // 4
    for j, r in enumerate((r0, r1, r2, r3)):
        held[lax.rem(h_ref[0] + 4 - j, 4)] = r[...]
    for q in range(4):
        o_ref[:, q * quarter : (q + 1) * quarter] = held[q, :, :quarter]


def shift(x, by):
    return lax.ppermute(x, "heads", [(i, (i + by) % 4) for i in range(4)])


def swap(x):
    return lax.ppermute(x, "core", [(0, 1), (1, 0)])


def plus(*terms):
    total = terms[0].astype(F32)
    for term in terms[1:]:
        total = total + term.astype(F32)
    return total.astype(BF)


def on_device(
    residual,
    query_rows,
    key_rows,
    value_rows,
    norm_gain,
    out_weight,
    moe_gain,
    expert_ids,
    gate_values,
    gate_weight,
    up_weight,
    down_weight,
):
    tokens, width = query_rows.shape
    features = residual.shape[1]
    quarter = features // 4
    padded = quarter + SPARE
    chip = ("z", "x")
    chips = lax.axis_size("z") * lax.axis_size("x")
    h = lax.axis_index("heads").astype(jnp.int32)
    core = lax.axis_index("core").astype(jnp.int32)
    h_arr = jnp.full((1,), h, jnp.int32)
    core_arr = jnp.full((1,), core, jnp.int32)
    place_arr = jnp.stack([h, core])
    capacity = min(tokens, 3 * tokens * expert_ids.shape[1] // (2 * chips))
    rows = chips * capacity
    shape = jax.ShapeDtypeStruct

    keep, send = pl.pallas_call(
        state_body,
        out_shape=(shape((HD // 2, width), BF),) * 2,
        in_specs=[SMEM_SPEC] + [VMEM_SPEC] * 2,
        out_specs=(VMEM_SPEC,) * 2,
        scratch_shapes=[pltpu.VMEM((2, HD // 2, width), BF)],
        compiler_params=params(60),
        name="own_state",
    )(core_arr, key_rows, value_rows)
    taken = swap(send)
    inner = pl.pallas_call(
        inner_body,
        out_shape=shape((tokens, width), F32),
        in_specs=[VMEM_SPEC] * 3,
        out_specs=VMEM_SPEC,
        compiler_params=params(60),
        cost_estimate=cost(2e9, 2e6),
        name="inner",
    )(query_rows, key_rows, value_rows)
    chip_state = plus(keep, taken)
    depth, breadth = lax.axis_size("z"), lax.axis_size("x")
    beside = [
        lax.ppermute(chip_state, "x", [(i, (i + j) % breadth) for i in range(breadth)])
        for j in range(1, breadth)
    ]
    slab_state = plus(chip_state, *beside)

    def deeper(x, j):
        moved = lax.ppermute(x, "z", [(i, (i + j) % depth) for i in range(depth)])
        return jnp.where(lax.axis_index("z") >= j, moved.astype(F32), 0.0)

    near = [deeper(slab_state, 1), deeper(slab_state, 2)]
    triple = plus(slab_state, *near)
    base = jnp.zeros(keep.shape, F32)
    for term in near + [deeper(triple, j) for j in range(3, depth, 3)]:
        base = base + term
    for j, term in enumerate(beside):
        base = base + jnp.where(lax.axis_index("x") > j, term.astype(F32), 0.0)
    later = lax.axis_index("core") == 1
    mine = (base + jnp.where(later, taken.astype(F32), 0.0)).astype(BF)
    theirs = (base + jnp.where(later, 0.0, keep.astype(F32))).astype(BF)
    other = swap(theirs)

    place, mix_high, mix_low = pl.pallas_call(
        functools.partial(route_body, chips),
        out_shape=(shape((rows, tokens), BF), shape((tokens, rows), BF), shape((tokens, rows), BF)),
        in_specs=[VMEM_SPEC] * 2,
        out_specs=(VMEM_SPEC,) * 3,
        compiler_params=params(10),
        cost_estimate=cost(1e8, 1e6),
        name="route",
    )(expert_ids.T, gate_values.T)

    parts = pl.pallas_call(
        attend_body,
        out_shape=(shape((tokens, padded), BF),) * 4,
        in_specs=[SMEM_SPEC] + [VMEM_SPEC] * 5 + [pl.BlockSpec(memory_space=pltpu.HBM)],
        out_specs=(VMEM_SPEC,) * 4,
        scratch_shapes=[
            pltpu.VMEM((tokens, width), BF),
            pltpu.VMEM((2, HD // 2, width), BF),
            pltpu.VMEM((features, width), BF),
            pltpu.VMEM((4, tokens, padded), BF),
            pltpu.SemaphoreType.DMA,
        ],
        compiler_params=params(60),
        name="attend",
    )(place_arr, query_rows, inner, mine, other, norm_gain.reshape(1, width), out_weight.T)
    pieces = [parts[0]] + [shift(parts[j], j) for j in (1, 2, 3)]

    gain = lax.dynamic_index_in_dim(moe_gain.reshape(4, 1, quarter), h, 0, keepdims=False)
    packed, attended = pl.pallas_call(
        pack_body,
        out_shape=(shape((rows, padded), BF), shape((tokens, quarter), F32)),
        in_specs=[SMEM_SPEC] + [VMEM_SPEC] * 7,
        out_specs=(VMEM_SPEC,) * 2,
        scratch_shapes=[pltpu.VMEM((tokens, padded), BF)],
        compiler_params=params(12),
        name="pack",
    )(h_arr, *pieces, residual.T, gain, place)

    arrived = lax.all_to_all(
        packed.reshape(chips, capacity, padded), chip, 0, 0, tiled=True
    ).reshape(rows, padded)
    half = rows // 2
    arrived, late_h = lax.optimization_barrier((arrived, h_arr))
    low, high = arrived[:half], arrived[half:]

    minus_low, plus_low = shift(low, 1), shift(low, -1)
    hidden_count = gate_weight.shape[2]
    wide = -(-hidden_count // 128) * 128
    weights = pl.pallas_call(
        weights_body,
        out_shape=(shape((4, padded, 2 * wide), BF), shape((4, hidden_count, padded), BF)),
        in_specs=[SMEM_SPEC] + [VMEM_SPEC] * 3,
        out_specs=(VMEM_SPEC,) * 2,
        compiler_params=params(28),
        cost_estimate=cost(5e9, 13e6),
        name="weights",
    )(late_h, gate_weight[0].T, up_weight[0].T, down_weight[0])
    minus_low, plus_low, high, weights = lax.optimization_barrier(
        (minus_low, plus_low, high, weights)
    )
    other_weights = tuple(swap(x) for x in weights)

    def experts(group):
        return pl.pallas_call(
            functools.partial(expert_body, features),
            out_shape=(shape((half, padded), BF),) * 4,
            in_specs=[VMEM_SPEC] * 8,
            out_specs=(VMEM_SPEC,) * 4,
            scratch_shapes=[
                pltpu.VMEM((4, half, padded), BF),
                pltpu.VMEM((2, half, 2 * wide), F32),
            ],
            compiler_params=params(28),
            cost_estimate=cost(1e6, 1e5),
            name="experts",
        )(*group, *weights, *other_weights)

    far_low, plus_high = shift(minus_low, 1), shift(high, -1)
    far_low, plus_high, high = lax.optimization_barrier((far_low, plus_high, high))
    far_high, minus_high = shift(plus_high, -1), shift(high, 1)
    sum_low = experts((low, plus_low, far_low, minus_low))
    far_high, minus_high, sum_low = lax.optimization_barrier((far_high, minus_high, sum_low))
    via_low, got_low_plus = shift(sum_low[2], 1), shift(sum_low[3], -1)
    sum_high = experts((high, plus_high, far_high, minus_high))
    via_low, got_low_plus, sum_high = lax.optimization_barrier((via_low, got_low_plus, sum_high))
    got_low_minus = shift(plus(sum_low[1], via_low), 1)
    via_high = shift(sum_high[2], -1)
    got_low_minus, via_high, sum_high = lax.optimization_barrier((got_low_minus, via_high, sum_high))
    got_high_minus = shift(sum_high[1], 1)
    got_high_plus = shift(plus(sum_high[3], via_high), -1)
    total_low = plus(sum_low[0], got_low_minus, got_low_plus)
    total_high = plus(sum_high[0], got_high_minus, got_high_plus)
    leaving = jnp.concatenate([total_low, total_high], axis=0).reshape(chips, capacity, padded)
    returned = lax.all_to_all(leaving, chip, 0, 0, tiled=True).reshape(rows, padded)

    share = tokens // 4
    ends = pl.pallas_call(
        mix_body,
        out_shape=(shape((share, padded), BF),) * 4,
        in_specs=[SMEM_SPEC] + [VMEM_SPEC] * 4,
        out_specs=(VMEM_SPEC,) * 4,
        scratch_shapes=[pltpu.VMEM((tokens, padded), BF)],
        compiler_params=params(10),
        name="mix",
    )(h_arr, returned, mix_high, mix_low, attended)
    finals = [ends[0]] + [shift(ends[j], j) for j in (1, 2, 3)]
    return pl.pallas_call(
        join_body,
        out_shape=shape((share, features), BF),
        in_specs=[SMEM_SPEC] + [VMEM_SPEC] * 4,
        out_specs=VMEM_SPEC,
        scratch_shapes=[pltpu.VMEM((4, share, padded), BF)],
        compiler_params=params(6),
        name="join",
    )(h_arr, *finals)


def solution(mesh):
    devices = mesh.devices
    split = Mesh(
        devices.reshape(-1, BREADTH, CORES, devices.shape[1]), ("z", "x", "core", "heads")
    )
    context = ("z", "x", "core")
    in_specs = (
        P(context, None),
        P(context, "heads"),
        P(context, "heads"),
        P(context, "heads"),
        P("heads"),
        P("heads", None),
        P(),
        P(context, None),
        P(context, None),
        P(context, None, "heads"),
        P(context, None, "heads"),
        P(context, "heads", None),
    )
    return jax.shard_map(
        on_device,
        mesh=split,
        in_specs=in_specs,
        out_specs=P(("z", "x", "core", "heads"), None),
        check_vma=False,
    )
```

```python
import functools

import jax
import jax.numpy as jnp
from jax import lax
from jax.experimental import pallas as pl
from jax.experimental.pallas import tpu as pltpu
from jax.sharding import Mesh
from jax.sharding import PartitionSpec as P

HD = 64
PAIR = 2 * HD
CORES = 2
BREADTH = 4
SPARE = 48
BF = jnp.bfloat16
F32 = jnp.float32
VMEM_SPEC = pl.BlockSpec(memory_space=pltpu.VMEM)
SMEM_SPEC = pl.BlockSpec(memory_space=pltpu.SMEM)


def params(mib):
    return pltpu.CompilerParams(vmem_limit_bytes=mib << 20)


def cost(flops, moved):
    return pl.CostEstimate(flops=int(flops), bytes_accessed=int(moved), transcendentals=0)


def dot(a, b, dims=((1,), (0,))):
    return lax.dot_general(a, b, (dims, ((), ())), preferred_element_type=F32)


def state_body(at_ref, k_ref, v_ref, keep_ref, send_ref, both_ref):
    first = lax.broadcasted_iota(jnp.int32, (HD, PAIR), 1) < HD
    half = HD // 2
    for p in range(k_ref.shape[1] // PAIR):
        cols = slice(p * PAIR, (p + 1) * PAIR)
        both = dot(k_ref[:, cols], v_ref[:, cols], ((0,), (0,)))
        state = jnp.where(first, both[:HD], both[HD:]).astype(BF)
        both_ref[0, :, cols] = state[:half]
        both_ref[1, :, cols] = state[half:]
    keep_ref[...] = both_ref[at_ref[1]]
    send_ref[...] = both_ref[1 - at_ref[1]]


def flag(condition):
    return jnp.where(condition, 1.0, 0.0)


def triple_body(at_ref, slab_ref, near_ref, next_ref, o_ref):
    z = at_ref[2]
    total = slab_ref[...].astype(F32) + flag(z >= 1) * near_ref[...].astype(F32)
    o_ref[...] = (total + flag(z >= 2) * next_ref[...].astype(F32)).astype(BF)


def before_body(at_ref, keep_ref, taken_ref, *rest):
    mine_ref, theirs_ref = rest[-2:]
    z, x, later = at_ref[2], at_ref[3], flag(at_ref[1] == 1)
    weights = [flag(z >= j) for j in (1, 2, 3, 6)] + [flag(x > j) for j in range(3)]
    base = jnp.zeros(keep_ref.shape, F32)
    for weight, ref in zip(weights, rest[:-2]):
        base = base + weight * ref[...].astype(F32)
    mine_ref[...] = (base + later * taken_ref[...].astype(F32)).astype(BF)
    theirs_ref[...] = (base + (1.0 - later) * keep_ref[...].astype(F32)).astype(BF)


def inner_body(q_ref, k_ref, v_ref, o_ref):
    tokens = q_ref.shape[0]
    first = lax.broadcasted_iota(jnp.int32, (tokens, PAIR), 1) < HD
    causal = lax.broadcasted_iota(jnp.int32, (tokens, tokens), 0) >= lax.broadcasted_iota(
        jnp.int32, (tokens, tokens), 1
    )
    zero = jnp.zeros((tokens, PAIR), BF)
    for p in range(q_ref.shape[1] // PAIR):
        cols = slice(p * PAIR, (p + 1) * PAIR)
        q, k, v = q_ref[:, cols], k_ref[:, cols], v_ref[:, cols]
        inner = []
        for keep in (jnp.where(first, q, zero), jnp.where(first, zero, q)):
            scores = dot(keep, k, ((1,), (1,)))
            weights = jnp.where(causal, scores, 0.0).astype(BF)
            inner.append(dot(weights, v))
        o_ref[:, cols] = jnp.where(first, inner[0], inner[1])


def attend_body(
    at_ref, q_ref, inner_ref, mine_ref, other_ref, gain_ref, w_ref, o0, o1, o2, o3, normed, state
):
    tokens = q_ref.shape[0]
    first = lax.broadcasted_iota(jnp.int32, (tokens, PAIR), 1) < HD
    first_s = lax.broadcasted_iota(jnp.int32, (HD, PAIR), 1) < HD
    state[at_ref[1]] = mine_ref[...]
    state[1 - at_ref[1]] = other_ref[...]

    def halves_mean(x):
        a = jnp.sum(jnp.where(first, x, 0.0), axis=1, keepdims=True)
        b = jnp.sum(jnp.where(first, 0.0, x), axis=1, keepdims=True)
        return jnp.where(first, a, b) * (1.0 / HD)

    for p in range(q_ref.shape[1] // PAIR):
        cols = slice(p * PAIR, (p + 1) * PAIR)
        s = jnp.concatenate([state[0, :, cols], state[1, :, cols]], axis=0)
        s_zero = jnp.zeros_like(s)
        block = jnp.concatenate(
            [jnp.where(first_s, s, s_zero), jnp.where(first_s, s_zero, s)], axis=0
        )
        mixed = inner_ref[:, cols] + dot(q_ref[:, cols], block)
        centered = mixed - halves_mean(mixed)
        spread = halves_mean(centered * centered)
        normed[:, cols] = (centered * lax.rsqrt(spread + 1e-05) * gain_ref[:, cols]).astype(BF)
    quarter = w_ref.shape[0] // 4
    pad = jnp.zeros((tokens, o0.shape[1] - quarter), BF)
    for j, o in enumerate((o0, o1, o2, o3)):
        start = pl.multiple_of(lax.rem(at_ref[0] + j, 4) * quarter, quarter)
        part = dot(normed[...], w_ref[pl.ds(start, quarter), :], ((1,), (1,)))
        o[:, :quarter] = part.astype(BF)
        o[:, quarter:] = pad


def route_body(experts, ids_ref, gates_ref, place_ref, higat_ref, low_ref):
    top, tokens = ids_ref.shape
    rows = place_ref.shape[0]
    capacity = rows // experts
    expert = lax.broadcasted_iota(jnp.int32, (experts, tokens), 0)
    member = jnp.zeros((experts, tokens), F32)
    gate = jnp.zeros((experts, tokens), F32)
    for c in range(top):
        hit = ids_ref[c : c + 1, :] == expert
        member = member + jnp.where(hit, 1.0, 0.0)
        gate = gate + jnp.where(hit, gates_ref[c : c + 1, :], 0.0)
    earlier = lax.broadcasted_iota(jnp.int32, (tokens, tokens), 0) < lax.broadcasted_iota(
        jnp.int32, (tokens, tokens), 1
    )
    rank = dot(member.astype(BF), jnp.where(earlier, 1.0, 0.0).astype(BF))
    rank = jnp.where(member > 0.0, rank, -1.0)
    shape = (experts, capacity, tokens)
    slot = lax.broadcasted_iota(jnp.int32, shape, 1).astype(F32)
    placed = jnp.where(jnp.broadcast_to(rank[:, None, :], shape) == slot, 1.0, 0.0)
    weighted = (placed * jnp.broadcast_to(gate[:, None, :], shape)).reshape(rows, tokens)
    place_ref[...] = placed.reshape(rows, tokens).astype(BF)
    mix = weighted.T
    high = mix.astype(BF)
    higat_ref[...] = high
    low_ref[...] = (mix - high.astype(F32)).astype(BF)


def pack_body(at_ref, p0, p1, p2, p3, res_ref, gain_ref, place_ref, packed_ref, att_ref, rows, gains):
    quarter = att_ref.shape[1]
    start = pl.multiple_of(at_ref[0] * quarter, quarter)
    att = res_ref[pl.ds(start, quarter), :].astype(F32).T
    for p in (p0, p1, p2, p3):
        att = att + p[:, :quarter].astype(F32)
    att_ref[...] = att
    square = jnp.sum(att * att, axis=1, keepdims=True)
    high = square.astype(BF).astype(F32)
    middle = (square - high).astype(BF).astype(F32)
    low = square - high - middle
    lane = lax.broadcasted_iota(jnp.int32, (att.shape[0], SPARE), 1)
    extra = jnp.where(lane == 0, high, jnp.where(lane == 1, middle, jnp.where(lane == 2, low, 0.0)))
    for q in range(4):
        gains[q] = gain_ref[:, q * quarter : (q + 1) * quarter]
    rows[:, :quarter] = (att * gains[at_ref[0]]).astype(BF)
    rows[:, quarter:] = extra.astype(BF)
    packed_ref[...] = dot(place_ref[...], rows[...]).astype(BF)


def weights_body(at_ref, gate_ref, up_ref, down_ref, mid_ref, out_ref):
    hidden, features = down_ref.shape
    quarter = features // 4
    padded = mid_ref.shape[1]
    wide = mid_ref.shape[2] // 2
    for q in range(4):
        place = lax.rem(q + 4 - at_ref[0], 4)
        cols = slice(q * quarter, (q + 1) * quarter)
        for side, ref in enumerate((gate_ref, up_ref)):
            lanes = slice(side * wide, (side + 1) * wide)
            tall = [ref[:, cols].astype(F32), jnp.zeros((wide - hidden, quarter), F32)]
            mid_ref[place, :quarter, lanes] = jnp.concatenate(tall, axis=0).T.astype(BF)
            mid_ref[place, quarter:, lanes] = jnp.zeros((padded - quarter, wide), BF)
        pad = jnp.zeros((hidden, padded - quarter), BF)
        out_ref[place] = jnp.concatenate([down_ref[:, cols], pad], axis=1)


def expert_body(features, x0, x1, x2, x3, mid0, out0, mid1, out1, t0, t1, t2, t3, held, total):
    quarter = features // 4
    hidden_count = out0.shape[1]
    wide = mid0.shape[2] // 2
    square = None
    for j, x in enumerate((x0, x1, x2, x3)):
        held[j] = x[...]
        tail = jnp.sum(x[:, quarter:].astype(F32), axis=1, keepdims=True)
        square = tail if j == 0 else square + tail
    scaling = lax.rsqrt(square * (1.0 / features) + 1e-06)
    total[...] = jnp.zeros_like(total)

    def gather(j, carry):
        row = held[j]
        total[0] += dot(row, mid0[j])
        total[1] += dot(row, mid1[j])
        return carry

    lax.fori_loop(0, 4, gather, 0)
    hidden = []
    for side in range(2):
        gate = total[side, :, :hidden_count] * scaling
        up = total[side, :, wide : wide + hidden_count] * scaling
        hidden.append((gate / (1.0 + jnp.exp(-gate)) * up).astype(BF))

    def spread(j, carry):
        held[j] = (dot(hidden[0], out0[j]) + dot(hidden[1], out1[j])).astype(BF)
        return carry

    lax.fori_loop(0, 4, spread, 0)
    for j, t in enumerate((t0, t1, t2, t3)):
        t[...] = held[j]


def mix_body(at_ref, back_ref, higat_ref, low_ref, att_ref, o0, o1, o2, o3, done):
    back = back_ref[...]
    quarter = att_ref.shape[1]
    mixture = dot(higat_ref[...], back) + dot(low_ref[...], back)
    done[:, :quarter] = (att_ref[...] + mixture[:, :quarter]).astype(BF)
    done[:, quarter:] = mixture[:, quarter:].astype(BF)
    share = o0.shape[0]
    for j, o in enumerate((o0, o1, o2, o3)):
        start = pl.multiple_of(lax.rem(at_ref[0] + j, 4) * share, share)
        o[...] = done[pl.ds(start, share), :]


def join_body(at_ref, r0, r1, r2, r3, o_ref, held):
    quarter = o_ref.shape[1] // 4
    for j, r in enumerate((r0, r1, r2, r3)):
        held[lax.rem(at_ref[0] + 4 - j, 4)] = r[...]
    for q in range(4):
        o_ref[:, q * quarter : (q + 1) * quarter] = held[q, :, :quarter]


def shift(x, by):
    return lax.ppermute(x, "heads", [(i, (i + by) % 4) for i in range(4)])


def swap(x):
    return lax.ppermute(x, "core", [(0, 1), (1, 0)])


def plus(*terms):
    total = terms[0].astype(F32)
    for term in terms[1:]:
        total = total + term.astype(F32)
    return total.astype(BF)


def on_device(
    residual,
    query_rows,
    key_rows,
    value_rows,
    norm_gain,
    out_weight,
    moe_gain,
    expert_ids,
    gate_values,
    gate_weight,
    up_weight,
    down_weight,
):
    tokens, width = query_rows.shape
    features = residual.shape[1]
    quarter = features // 4
    padded = quarter + SPARE
    chip = ("z", "x")
    chips = lax.axis_size("z") * lax.axis_size("x")
    at = jnp.stack([lax.axis_index(name) for name in ("heads", "core", "z", "x")])
    at, key_rows = lax.optimization_barrier((at.astype(jnp.int32), key_rows))
    capacity = min(tokens, 3 * tokens * expert_ids.shape[1] // (2 * chips))
    rows = chips * capacity
    shape = jax.ShapeDtypeStruct

    keep, send = pl.pallas_call(
        state_body,
        out_shape=(shape((HD // 2, width), BF),) * 2,
        in_specs=[SMEM_SPEC] + [VMEM_SPEC] * 2,
        out_specs=(VMEM_SPEC,) * 2,
        scratch_shapes=[pltpu.VMEM((2, HD // 2, width), BF)],
        compiler_params=params(60),
        name="own_state",
    )(at, key_rows, value_rows)
    taken = swap(send)
    inner = pl.pallas_call(
        inner_body,
        out_shape=shape((tokens, width), F32),
        in_specs=[VMEM_SPEC] * 3,
        out_specs=VMEM_SPEC,
        compiler_params=params(28),
        cost_estimate=cost(2e9, 2e6),
        name="inner",
    )(query_rows, key_rows, value_rows)
    chip_state = plus(keep, taken)
    depth, breadth = lax.axis_size("z"), lax.axis_size("x")
    beside = [
        lax.ppermute(chip_state, "x", [(i, (i + j) % breadth) for i in range(breadth)])
        for j in range(1, breadth)
    ]
    slab_state = plus(chip_state, *beside)

    def deeper(x, j):
        return lax.ppermute(x, "z", [(i, (i + j) % depth) for i in range(depth)])

    near = [deeper(slab_state, 1), deeper(slab_state, 2)]
    near, inner = lax.optimization_barrier((near, inner))
    triple = pl.pallas_call(
        triple_body,
        out_shape=shape(keep.shape, BF),
        in_specs=[SMEM_SPEC] + [VMEM_SPEC] * 3,
        out_specs=VMEM_SPEC,
        compiler_params=params(28),
        name="triple",
    )(at, slab_state, *near)
    mine, theirs = pl.pallas_call(
        before_body,
        out_shape=(shape(keep.shape, BF),) * 2,
        in_specs=[SMEM_SPEC] + [VMEM_SPEC] * 9,
        out_specs=(VMEM_SPEC,) * 2,
        compiler_params=params(28),
        name="before",
    )(at, keep, taken, *near, deeper(triple, 3), deeper(triple, 6), *beside)
    other = swap(theirs)

    place, mix_high, mix_low = pl.pallas_call(
        functools.partial(route_body, chips),
        out_shape=(shape((rows, tokens), BF), shape((tokens, rows), BF), shape((tokens, rows), BF)),
        in_specs=[VMEM_SPEC] * 2,
        out_specs=(VMEM_SPEC,) * 3,
        compiler_params=params(28),
        cost_estimate=cost(1e8, 1e6),
        name="route",
    )(expert_ids.T, gate_values.T)

    parts = pl.pallas_call(
        attend_body,
        out_shape=(shape((tokens, padded), BF),) * 4,
        in_specs=[SMEM_SPEC] + [VMEM_SPEC] * 6,
        out_specs=(VMEM_SPEC,) * 4,
        scratch_shapes=[pltpu.VMEM((tokens, width), BF), pltpu.VMEM((2, HD // 2, width), BF)],
        compiler_params=params(28),
        name="attend",
    )(at, query_rows, inner, mine, other, norm_gain.reshape(1, width), out_weight.T)
    pieces = [parts[0]] + [shift(parts[j], j) for j in (1, 2, 3)]

    packed, attended = pl.pallas_call(
        pack_body,
        out_shape=(shape((rows, padded), BF), shape((tokens, quarter), F32)),
        in_specs=[SMEM_SPEC] + [VMEM_SPEC] * 7,
        out_specs=(VMEM_SPEC,) * 2,
        scratch_shapes=[pltpu.VMEM((tokens, padded), BF), pltpu.VMEM((4, 1, quarter), F32)],
        compiler_params=params(28),
        name="pack",
    )(at, *pieces, residual.T, moe_gain.reshape(1, features), place)

    arrived = lax.all_to_all(
        packed.reshape(chips, capacity, padded), chip, 0, 0, tiled=True
    ).reshape(rows, padded)
    half = rows // 2
    arrived, late_h = lax.optimization_barrier((arrived, at))
    low, high = arrived[:half], arrived[half:]

    minus_low, plus_low = shift(low, 1), shift(low, -1)
    hidden_count = gate_weight.shape[2]
    wide = -(-hidden_count // 128) * 128
    weights = pl.pallas_call(
        weights_body,
        out_shape=(shape((4, padded, 2 * wide), BF), shape((4, hidden_count, padded), BF)),
        in_specs=[SMEM_SPEC] + [VMEM_SPEC] * 3,
        out_specs=(VMEM_SPEC,) * 2,
        compiler_params=params(28),
        cost_estimate=cost(5e9, 13e6),
        name="weights",
    )(late_h, gate_weight[0].T, up_weight[0].T, down_weight[0])
    minus_low, plus_low, high, weights = lax.optimization_barrier(
        (minus_low, plus_low, high, weights)
    )
    other_weights = tuple(swap(x) for x in weights)

    def experts(group):
        return pl.pallas_call(
            functools.partial(expert_body, features),
            out_shape=(shape((half, padded), BF),) * 4,
            in_specs=[VMEM_SPEC] * 8,
            out_specs=(VMEM_SPEC,) * 4,
            scratch_shapes=[
                pltpu.VMEM((4, half, padded), BF),
                pltpu.VMEM((2, half, 2 * wide), F32),
            ],
            compiler_params=params(28),
            cost_estimate=cost(1e6, 1e5),
            name="experts",
        )(*group, *weights, *other_weights)

    far_low, plus_high = shift(minus_low, 1), shift(high, -1)
    far_low, plus_high, high = lax.optimization_barrier((far_low, plus_high, high))
    far_high, minus_high = shift(plus_high, -1), shift(high, 1)
    sum_low = experts((low, plus_low, far_low, minus_low))
    via_low, got_low_plus = shift(sum_low[2], 1), shift(sum_low[3], -1)
    sum_high = experts((high, plus_high, far_high, minus_high))
    via_low, got_low_plus, sum_high = lax.optimization_barrier((via_low, got_low_plus, sum_high))
    got_low_minus = shift(plus(sum_low[1], via_low), 1)
    via_high = shift(sum_high[2], -1)
    got_low_minus, via_high, sum_high = lax.optimization_barrier((got_low_minus, via_high, sum_high))
    got_high_minus = shift(sum_high[1], 1)
    got_high_plus = shift(plus(sum_high[3], via_high), -1)
    total_low = plus(sum_low[0], got_low_minus, got_low_plus)
    total_high = plus(sum_high[0], got_high_minus, got_high_plus)
    leaving = jnp.concatenate([total_low, total_high], axis=0).reshape(chips, capacity, padded)
    returned = lax.all_to_all(leaving, chip, 0, 0, tiled=True).reshape(rows, padded)

    share = tokens // 4
    ends = pl.pallas_call(
        mix_body,
        out_shape=(shape((share, padded), BF),) * 4,
        in_specs=[SMEM_SPEC] + [VMEM_SPEC] * 4,
        out_specs=(VMEM_SPEC,) * 4,
        scratch_shapes=[pltpu.VMEM((tokens, padded), BF)],
        compiler_params=params(28),
        name="mix",
    )(at, returned, mix_high, mix_low, attended)
    finals = [ends[0]] + [shift(ends[j], j) for j in (1, 2, 3)]
    return pl.pallas_call(
        join_body,
        out_shape=shape((share, features), BF),
        in_specs=[SMEM_SPEC] + [VMEM_SPEC] * 4,
        out_specs=VMEM_SPEC,
        scratch_shapes=[pltpu.VMEM((4, share, padded), BF)],
        compiler_params=params(28),
        name="join",
    )(at, *finals)


def solution(mesh):
    devices = mesh.devices
    split = Mesh(
        devices.reshape(-1, BREADTH, CORES, devices.shape[1]), ("z", "x", "core", "heads")
    )
    context = ("z", "x", "core")
    in_specs = (
        P(context, None),
        P(context, "heads"),
        P(context, "heads"),
        P(context, "heads"),
        P("heads"),
        P("heads", None),
        P(),
        P(context, None),
        P(context, None),
        P(context, None, "heads"),
        P(context, None, "heads"),
        P(context, "heads", None),
    )
    return jax.shard_map(
        on_device,
        mesh=split,
        in_specs=in_specs,
        out_specs=P(("z", "x", "core", "heads"), None),
        check_vma=False,
    )
```

```python
import functools

import jax
import jax.numpy as jnp
from jax import lax
from jax.experimental import pallas as pl
from jax.experimental.pallas import tpu as pltpu
from jax.sharding import Mesh
from jax.sharding import PartitionSpec as P

HD = 64
PAIR = 2 * HD
CORES = 2
BREADTH = 4
SPARE = 48
BF = jnp.bfloat16
F32 = jnp.float32
VMEM_SPEC = pl.BlockSpec(memory_space=pltpu.VMEM)
SMEM_SPEC = pl.BlockSpec(memory_space=pltpu.SMEM)


def params(mib):
    return pltpu.CompilerParams(vmem_limit_bytes=mib << 20)


def cost(flops, moved):
    return pl.CostEstimate(flops=int(flops), bytes_accessed=int(moved), transcendentals=0)


def dot(a, b, dims=((1,), (0,))):
    return lax.dot_general(a, b, (dims, ((), ())), preferred_element_type=F32)


def state_body(at_ref, k_ref, v_ref, keep_ref, send_ref, both_ref):
    first = lax.broadcasted_iota(jnp.int32, (HD, PAIR), 1) < HD
    half = HD // 2
    for p in range(k_ref.shape[1] // PAIR):
        cols = slice(p * PAIR, (p + 1) * PAIR)
        both = dot(k_ref[:, cols], v_ref[:, cols], ((0,), (0,)))
        state = jnp.where(first, both[:HD], both[HD:]).astype(BF)
        both_ref[0, :, cols] = state[:half]
        both_ref[1, :, cols] = state[half:]
    keep_ref[...] = both_ref[at_ref[0]]
    send_ref[...] = both_ref[1 - at_ref[0]]


def flag(condition):
    return jnp.where(condition, 1.0, 0.0)


def triple_body(at_ref, slab_ref, near_ref, next_ref, o_ref):
    z = at_ref[0]
    total = slab_ref[...].astype(F32) + flag(z >= 1) * near_ref[...].astype(F32)
    o_ref[...] = (total + flag(z >= 2) * next_ref[...].astype(F32)).astype(BF)


def before_body(core_ref, z_ref, x_ref, keep_ref, taken_ref, *rest):
    mine_ref, theirs_ref = rest[-2:]
    z, x, later = z_ref[0], x_ref[0], flag(core_ref[0] == 1)
    weights = [flag(z >= j) for j in (1, 2, 3, 6)] + [flag(x > j) for j in range(3)]
    base = jnp.zeros(keep_ref.shape, F32)
    for weight, ref in zip(weights, rest[:-2]):
        base = base + weight * ref[...].astype(F32)
    mine_ref[...] = (base + later * taken_ref[...].astype(F32)).astype(BF)
    theirs_ref[...] = (base + (1.0 - later) * keep_ref[...].astype(F32)).astype(BF)


def inner_body(q_ref, k_ref, v_ref, o_ref):
    tokens = q_ref.shape[0]
    first = lax.broadcasted_iota(jnp.int32, (tokens, PAIR), 1) < HD
    causal = lax.broadcasted_iota(jnp.int32, (tokens, tokens), 0) >= lax.broadcasted_iota(
        jnp.int32, (tokens, tokens), 1
    )
    zero = jnp.zeros((tokens, PAIR), BF)
    for p in range(q_ref.shape[1] // PAIR):
        cols = slice(p * PAIR, (p + 1) * PAIR)
        q, k, v = q_ref[:, cols], k_ref[:, cols], v_ref[:, cols]
        inner = []
        for keep in (jnp.where(first, q, zero), jnp.where(first, zero, q)):
            scores = dot(keep, k, ((1,), (1,)))
            weights = jnp.where(causal, scores, 0.0).astype(BF)
            inner.append(dot(weights, v))
        o_ref[:, cols] = jnp.where(first, inner[0], inner[1])


def attend_body(
    at_ref, core_ref, q_ref, inner_ref, mine_ref, other_ref, gain_ref, w_ref, o0, o1, o2, o3, normed, state
):
    tokens = q_ref.shape[0]
    first = lax.broadcasted_iota(jnp.int32, (tokens, PAIR), 1) < HD
    first_s = lax.broadcasted_iota(jnp.int32, (HD, PAIR), 1) < HD
    state[core_ref[0]] = mine_ref[...]
    state[1 - core_ref[0]] = other_ref[...]

    def halves_mean(x):
        a = jnp.sum(jnp.where(first, x, 0.0), axis=1, keepdims=True)
        b = jnp.sum(jnp.where(first, 0.0, x), axis=1, keepdims=True)
        return jnp.where(first, a, b) * (1.0 / HD)

    for p in range(q_ref.shape[1] // PAIR):
        cols = slice(p * PAIR, (p + 1) * PAIR)
        s = jnp.concatenate([state[0, :, cols], state[1, :, cols]], axis=0)
        s_zero = jnp.zeros_like(s)
        block = jnp.concatenate(
            [jnp.where(first_s, s, s_zero), jnp.where(first_s, s_zero, s)], axis=0
        )
        mixed = inner_ref[:, cols] + dot(q_ref[:, cols], block)
        centered = mixed - halves_mean(mixed)
        spread = halves_mean(centered * centered)
        normed[:, cols] = (centered * lax.rsqrt(spread + 1e-05) * gain_ref[:, cols]).astype(BF)
    quarter = w_ref.shape[0] // 4
    pad = jnp.zeros((tokens, o0.shape[1] - quarter), BF)
    for j, o in enumerate((o0, o1, o2, o3)):
        start = pl.multiple_of(lax.rem(at_ref[0] + j, 4) * quarter, quarter)
        part = dot(normed[...], w_ref[pl.ds(start, quarter), :], ((1,), (1,)))
        o[:, :quarter] = part.astype(BF)
        o[:, quarter:] = pad


def route_body(experts, ids_ref, gates_ref, place_ref, higat_ref, low_ref):
    top, tokens = ids_ref.shape
    rows = place_ref.shape[0]
    capacity = rows // experts
    expert = lax.broadcasted_iota(jnp.int32, (experts, tokens), 0)
    member = jnp.zeros((experts, tokens), F32)
    gate = jnp.zeros((experts, tokens), F32)
    for c in range(top):
        hit = ids_ref[c : c + 1, :] == expert
        member = member + jnp.where(hit, 1.0, 0.0)
        gate = gate + jnp.where(hit, gates_ref[c : c + 1, :], 0.0)
    earlier = lax.broadcasted_iota(jnp.int32, (tokens, tokens), 0) < lax.broadcasted_iota(
        jnp.int32, (tokens, tokens), 1
    )
    rank = dot(member.astype(BF), jnp.where(earlier, 1.0, 0.0).astype(BF))
    rank = jnp.where(member > 0.0, rank, -1.0)
    shape = (experts, capacity, tokens)
    slot = lax.broadcasted_iota(jnp.int32, shape, 1).astype(F32)
    placed = jnp.where(jnp.broadcast_to(rank[:, None, :], shape) == slot, 1.0, 0.0)
    weighted = (placed * jnp.broadcast_to(gate[:, None, :], shape)).reshape(rows, tokens)
    place_ref[...] = placed.reshape(rows, tokens).astype(BF)
    mix = weighted.T
    high = mix.astype(BF)
    higat_ref[...] = high
    low_ref[...] = (mix - high.astype(F32)).astype(BF)


def pack_body(at_ref, p0, p1, p2, p3, res_ref, gain_ref, place_ref, packed_ref, att_ref, rows, gains):
    quarter = att_ref.shape[1]
    start = pl.multiple_of(at_ref[0] * quarter, quarter)
    att = res_ref[pl.ds(start, quarter), :].astype(F32).T
    for p in (p0, p1, p2, p3):
        att = att + p[:, :quarter].astype(F32)
    att_ref[...] = att
    square = jnp.sum(att * att, axis=1, keepdims=True)
    high = square.astype(BF).astype(F32)
    middle = (square - high).astype(BF).astype(F32)
    low = square - high - middle
    lane = lax.broadcasted_iota(jnp.int32, (att.shape[0], SPARE), 1)
    extra = jnp.where(lane == 0, high, jnp.where(lane == 1, middle, jnp.where(lane == 2, low, 0.0)))
    for q in range(4):
        gains[q] = gain_ref[:, q * quarter : (q + 1) * quarter]
    rows[:, :quarter] = (att * gains[at_ref[0]]).astype(BF)
    rows[:, quarter:] = extra.astype(BF)
    packed_ref[...] = dot(place_ref[...], rows[...]).astype(BF)


def weights_body(at_ref, gate_ref, up_ref, down_ref, mid_ref, out_ref):
    hidden, features = down_ref.shape
    quarter = features // 4
    padded = mid_ref.shape[1]
    wide = mid_ref.shape[2] // 2
    for q in range(4):
        place = lax.rem(q + 4 - at_ref[0], 4)
        cols = slice(q * quarter, (q + 1) * quarter)
        for side, ref in enumerate((gate_ref, up_ref)):
            lanes = slice(side * wide, (side + 1) * wide)
            tall = [ref[:, cols].astype(F32), jnp.zeros((wide - hidden, quarter), F32)]
            mid_ref[place, :quarter, lanes] = jnp.concatenate(tall, axis=0).T.astype(BF)
            mid_ref[place, quarter:, lanes] = jnp.zeros((padded - quarter, wide), BF)
        pad = jnp.zeros((hidden, padded - quarter), BF)
        out_ref[place] = jnp.concatenate([down_ref[:, cols], pad], axis=1)


def expert_body(features, x0, x1, x2, x3, mid0, out0, mid1, out1, t0, t1, t2, t3, held, total):
    quarter = features // 4
    hidden_count = out0.shape[1]
    wide = mid0.shape[2] // 2
    square = None
    for j, x in enumerate((x0, x1, x2, x3)):
        held[j] = x[...]
        tail = jnp.sum(x[:, quarter:].astype(F32), axis=1, keepdims=True)
        square = tail if j == 0 else square + tail
    scaling = lax.rsqrt(square * (1.0 / features) + 1e-06)
    total[...] = jnp.zeros_like(total)

    def gather(j, carry):
        row = held[j]
        total[0] += dot(row, mid0[j])
        total[1] += dot(row, mid1[j])
        return carry

    lax.fori_loop(0, 4, gather, 0)
    hidden = []
    for side in range(2):
        gate = total[side, :, :hidden_count] * scaling
        up = total[side, :, wide : wide + hidden_count] * scaling
        hidden.append((gate / (1.0 + jnp.exp(-gate)) * up).astype(BF))

    def spread(j, carry):
        held[j] = (dot(hidden[0], out0[j]) + dot(hidden[1], out1[j])).astype(BF)
        return carry

    lax.fori_loop(0, 4, spread, 0)
    for j, t in enumerate((t0, t1, t2, t3)):
        t[...] = held[j]


def mix_body(at_ref, back_ref, higat_ref, low_ref, att_ref, o0, o1, o2, o3, done):
    back = back_ref[...]
    quarter = att_ref.shape[1]
    mixture = dot(higat_ref[...], back) + dot(low_ref[...], back)
    done[:, :quarter] = (att_ref[...] + mixture[:, :quarter]).astype(BF)
    done[:, quarter:] = mixture[:, quarter:].astype(BF)
    share = o0.shape[0]
    for j, o in enumerate((o0, o1, o2, o3)):
        start = pl.multiple_of(lax.rem(at_ref[0] + j, 4) * share, share)
        o[...] = done[pl.ds(start, share), :]


def join_body(at_ref, r0, r1, r2, r3, o_ref, held):
    quarter = o_ref.shape[1] // 4
    for j, r in enumerate((r0, r1, r2, r3)):
        held[lax.rem(at_ref[0] + 4 - j, 4)] = r[...]
    for q in range(4):
        o_ref[:, q * quarter : (q + 1) * quarter] = held[q, :, :quarter]


def shift(x, by):
    return lax.ppermute(x, "heads", [(i, (i + by) % 4) for i in range(4)])


def swap(x):
    return lax.ppermute(x, "core", [(0, 1), (1, 0)])


def plus(*terms):
    total = terms[0].astype(F32)
    for term in terms[1:]:
        total = total + term.astype(F32)
    return total.astype(BF)


def on_device(
    residual,
    query_rows,
    key_rows,
    value_rows,
    norm_gain,
    out_weight,
    moe_gain,
    expert_ids,
    gate_values,
    gate_weight,
    up_weight,
    down_weight,
):
    tokens, width = query_rows.shape
    features = residual.shape[1]
    quarter = features // 4
    padded = quarter + SPARE
    chip = ("z", "x")
    chips = lax.axis_size("z") * lax.axis_size("x")
    ids = tuple(
        jnp.full((1,), lax.axis_index(name).astype(jnp.int32)) for name in ("heads", "core", "z", "x")
    )
    (h_at, core_at, z_at, x_at), key_rows = lax.optimization_barrier((ids, key_rows))
    capacity = min(tokens, 3 * tokens * expert_ids.shape[1] // (2 * chips))
    rows = chips * capacity
    shape = jax.ShapeDtypeStruct

    keep, send = pl.pallas_call(
        state_body,
        out_shape=(shape((HD // 2, width), BF),) * 2,
        in_specs=[SMEM_SPEC] + [VMEM_SPEC] * 2,
        out_specs=(VMEM_SPEC,) * 2,
        scratch_shapes=[pltpu.VMEM((2, HD // 2, width), BF)],
        compiler_params=params(28),
        name="own_state",
    )(core_at, key_rows, value_rows)
    taken = swap(send)
    inner = pl.pallas_call(
        inner_body,
        out_shape=shape((tokens, width), F32),
        in_specs=[VMEM_SPEC] * 3,
        out_specs=VMEM_SPEC,
        compiler_params=params(60),
        cost_estimate=cost(2e9, 2e6),
        name="inner",
    )(query_rows, key_rows, value_rows)
    chip_state = plus(keep, taken)
    depth, breadth = lax.axis_size("z"), lax.axis_size("x")
    beside = [
        lax.ppermute(chip_state, "x", [(i, (i + j) % breadth) for i in range(breadth)])
        for j in range(1, breadth)
    ]
    slab_state = plus(chip_state, *beside)

    def deeper(x, j):
        return lax.ppermute(x, "z", [(i, (i + j) % depth) for i in range(depth)])

    near = [deeper(slab_state, 1), deeper(slab_state, 2)]
    near, inner = lax.optimization_barrier((near, inner))
    triple = pl.pallas_call(
        triple_body,
        out_shape=shape(keep.shape, BF),
        in_specs=[SMEM_SPEC] + [VMEM_SPEC] * 3,
        out_specs=VMEM_SPEC,
        compiler_params=params(28),
        name="triple",
    )(z_at, slab_state, *near)
    mine, theirs = pl.pallas_call(
        before_body,
        out_shape=(shape(keep.shape, BF),) * 2,
        in_specs=[SMEM_SPEC] * 3 + [VMEM_SPEC] * 9,
        out_specs=(VMEM_SPEC,) * 2,
        compiler_params=params(28),
        name="before",
    )(core_at, z_at, x_at, keep, taken, *near, deeper(triple, 3), deeper(triple, 6), *beside)
    other = swap(theirs)

    place, mix_high, mix_low = pl.pallas_call(
        functools.partial(route_body, chips),
        out_shape=(shape((rows, tokens), BF), shape((tokens, rows), BF), shape((tokens, rows), BF)),
        in_specs=[VMEM_SPEC] * 2,
        out_specs=(VMEM_SPEC,) * 3,
        compiler_params=params(28),
        cost_estimate=cost(1e8, 1e6),
        name="route",
    )(expert_ids.T, gate_values.T)

    parts = pl.pallas_call(
        attend_body,
        out_shape=(shape((tokens, padded), BF),) * 4,
        in_specs=[SMEM_SPEC] * 2 + [VMEM_SPEC] * 6,
        out_specs=(VMEM_SPEC,) * 4,
        scratch_shapes=[pltpu.VMEM((tokens, width), BF), pltpu.VMEM((2, HD // 2, width), BF)],
        compiler_params=params(28),
        name="attend",
    )(h_at, core_at, query_rows, inner, mine, other, norm_gain.reshape(1, width), out_weight.T)
    across = shift(parts[2], 2)
    pieces = [parts[0], shift(parts[1], 1), across, shift(parts[3], 3)]

    packed, attended = pl.pallas_call(
        pack_body,
        out_shape=(shape((rows, padded), BF), shape((tokens, quarter), F32)),
        in_specs=[SMEM_SPEC] + [VMEM_SPEC] * 7,
        out_specs=(VMEM_SPEC,) * 2,
        scratch_shapes=[pltpu.VMEM((tokens, padded), BF), pltpu.VMEM((4, 1, quarter), F32)],
        compiler_params=params(28),
        name="pack",
    )(h_at, *pieces, residual.T, moe_gain.reshape(1, features), place)

    arrived = lax.all_to_all(
        packed.reshape(chips, capacity, padded), chip, 0, 0, tiled=True
    ).reshape(rows, padded)
    half = rows // 2
    arrived, late_h = lax.optimization_barrier((arrived, h_at))
    low, high = arrived[:half], arrived[half:]

    minus_low, plus_low = shift(low, 1), shift(low, -1)
    hidden_count = gate_weight.shape[2]
    wide = -(-hidden_count // 128) * 128
    weights = pl.pallas_call(
        weights_body,
        out_shape=(shape((4, padded, 2 * wide), BF), shape((4, hidden_count, padded), BF)),
        in_specs=[SMEM_SPEC] + [VMEM_SPEC] * 3,
        out_specs=(VMEM_SPEC,) * 2,
        compiler_params=params(28),
        cost_estimate=cost(5e9, 13e6),
        name="weights",
    )(late_h, gate_weight[0].T, up_weight[0].T, down_weight[0])
    minus_low, plus_low, high, weights = lax.optimization_barrier(
        (minus_low, plus_low, high, weights)
    )
    other_weights = tuple(swap(x) for x in weights)

    def experts(group):
        return pl.pallas_call(
            functools.partial(expert_body, features),
            out_shape=(shape((half, padded), BF),) * 4,
            in_specs=[VMEM_SPEC] * 8,
            out_specs=(VMEM_SPEC,) * 4,
            scratch_shapes=[
                pltpu.VMEM((4, half, padded), BF),
                pltpu.VMEM((2, half, 2 * wide), F32),
            ],
            compiler_params=params(28),
            cost_estimate=cost(1e6, 1e5),
            name="experts",
        )(*group, *weights, *other_weights)

    far_low, plus_high = shift(minus_low, 1), shift(high, -1)
    far_low, plus_high, high = lax.optimization_barrier((far_low, plus_high, high))
    far_high, minus_high = shift(plus_high, -1), shift(high, 1)
    sum_low = experts((low, plus_low, far_low, minus_low))
    via_low, got_low_plus = shift(sum_low[2], 1), shift(sum_low[3], -1)
    sum_high = experts((high, plus_high, far_high, minus_high))
    via_low, got_low_plus, sum_high = lax.optimization_barrier((via_low, got_low_plus, sum_high))
    got_low_minus = shift(plus(sum_low[1], via_low), 1)
    via_high = shift(sum_high[2], -1)
    got_low_minus, via_high, sum_high = lax.optimization_barrier((got_low_minus, via_high, sum_high))
    got_high_minus = shift(sum_high[1], 1)
    got_high_plus = shift(plus(sum_high[3], via_high), -1)
    total_low = plus(sum_low[0], got_low_minus, got_low_plus)
    total_high = plus(sum_high[0], got_high_minus, got_high_plus)
    leaving = jnp.concatenate([total_low, total_high], axis=0).reshape(chips, capacity, padded)
    returned = lax.all_to_all(leaving, chip, 0, 0, tiled=True).reshape(rows, padded)

    share = tokens // 4
    ends = pl.pallas_call(
        mix_body,
        out_shape=(shape((share, padded), BF),) * 4,
        in_specs=[SMEM_SPEC] + [VMEM_SPEC] * 4,
        out_specs=(VMEM_SPEC,) * 4,
        scratch_shapes=[pltpu.VMEM((tokens, padded), BF)],
        compiler_params=params(28),
        name="mix",
    )(h_at, returned, mix_high, mix_low, attended)
    across = shift(ends[2], 2)
    finals = [ends[0], shift(ends[1], 1), across, shift(ends[3], 3)]
    return pl.pallas_call(
        join_body,
        out_shape=shape((share, features), BF),
        in_specs=[SMEM_SPEC] + [VMEM_SPEC] * 4,
        out_specs=VMEM_SPEC,
        scratch_shapes=[pltpu.VMEM((4, share, padded), BF)],
        compiler_params=params(28),
        name="join",
    )(h_at, *finals)


def solution(mesh):
    devices = mesh.devices
    split = Mesh(
        devices.reshape(-1, BREADTH, CORES, devices.shape[1]), ("z", "x", "core", "heads")
    )
    context = ("z", "x", "core")
    in_specs = (
        P(context, None),
        P(context, "heads"),
        P(context, "heads"),
        P(context, "heads"),
        P("heads"),
        P("heads", None),
        P(),
        P(context, None),
        P(context, None),
        P(context, None, "heads"),
        P(context, None, "heads"),
        P(context, "heads", None),
    )
    return jax.shard_map(
        on_device,
        mesh=split,
        in_specs=in_specs,
        out_specs=P(("z", "x", "core", "heads"), None),
        check_vma=False,
    )
```

```python
import functools

import jax
import jax.numpy as jnp
from jax import lax
from jax.experimental import pallas as pl
from jax.experimental.pallas import tpu as pltpu
from jax.sharding import Mesh
from jax.sharding import PartitionSpec as P

HD = 64
PAIR = 2 * HD
CORES = 2
BREADTH = 4
SPARE = 48
BF = jnp.bfloat16
F32 = jnp.float32
VMEM_SPEC = pl.BlockSpec(memory_space=pltpu.VMEM)
SMEM_SPEC = pl.BlockSpec(memory_space=pltpu.SMEM)


def params(mib):
    return pltpu.CompilerParams(vmem_limit_bytes=mib << 20)


def cost(flops, moved):
    return pl.CostEstimate(flops=int(flops), bytes_accessed=int(moved), transcendentals=0)


def dot(a, b, dims=((1,), (0,))):
    return lax.dot_general(a, b, (dims, ((), ())), preferred_element_type=F32)


def state_body(at_ref, k_ref, v_ref, keep_ref, send_ref, k_out, v_out, both_ref):
    k_out[...] = k_ref[...]
    v_out[...] = v_ref[...]
    first = lax.broadcasted_iota(jnp.int32, (HD, PAIR), 1) < HD
    half = HD // 2
    for p in range(k_ref.shape[1] // PAIR):
        cols = slice(p * PAIR, (p + 1) * PAIR)
        both = dot(k_ref[:, cols], v_ref[:, cols], ((0,), (0,)))
        state = jnp.where(first, both[:HD], both[HD:]).astype(BF)
        both_ref[0, :, cols] = state[:half]
        both_ref[1, :, cols] = state[half:]
    keep_ref[...] = both_ref[at_ref[0]]
    send_ref[...] = both_ref[1 - at_ref[0]]


def flag(condition):
    return jnp.where(condition, 1.0, 0.0)


def triple_body(at_ref, slab_ref, near_ref, next_ref, o_ref):
    z = at_ref[0]
    total = slab_ref[...].astype(F32) + flag(z >= 1) * near_ref[...].astype(F32)
    o_ref[...] = (total + flag(z >= 2) * next_ref[...].astype(F32)).astype(BF)


def before_body(core_ref, z_ref, x_ref, keep_ref, taken_ref, *rest):
    mine_ref, theirs_ref = rest[-2:]
    z, x, later = z_ref[0], x_ref[0], flag(core_ref[0] == 1)
    weights = [flag(z >= j) for j in (1, 2, 3, 6)] + [flag(x > j) for j in range(3)]
    base = jnp.zeros(keep_ref.shape, F32)
    for weight, ref in zip(weights, rest[:-2]):
        base = base + weight * ref[...].astype(F32)
    mine_ref[...] = (base + later * taken_ref[...].astype(F32)).astype(BF)
    theirs_ref[...] = (base + (1.0 - later) * keep_ref[...].astype(F32)).astype(BF)


def inner_body(q_ref, k_ref, v_ref, o_ref):
    tokens = q_ref.shape[0]
    first = lax.broadcasted_iota(jnp.int32, (tokens, PAIR), 1) < HD
    causal = lax.broadcasted_iota(jnp.int32, (tokens, tokens), 0) >= lax.broadcasted_iota(
        jnp.int32, (tokens, tokens), 1
    )
    zero = jnp.zeros((tokens, PAIR), BF)
    for p in range(q_ref.shape[1] // PAIR):
        cols = slice(p * PAIR, (p + 1) * PAIR)
        q, k, v = q_ref[:, cols], k_ref[:, cols], v_ref[:, cols]
        inner = []
        for keep in (jnp.where(first, q, zero), jnp.where(first, zero, q)):
            scores = dot(keep, k, ((1,), (1,)))
            weights = jnp.where(causal, scores, 0.0).astype(BF)
            inner.append(dot(weights, v))
        o_ref[:, cols] = jnp.where(first, inner[0], inner[1])


def attend_body(
    at_ref, core_ref, q_ref, inner_ref, mine_ref, other_ref, gain_ref, w_ref, o0, o1, o2, o3, normed, state
):
    tokens = q_ref.shape[0]
    first = lax.broadcasted_iota(jnp.int32, (tokens, PAIR), 1) < HD
    first_s = lax.broadcasted_iota(jnp.int32, (HD, PAIR), 1) < HD
    state[core_ref[0]] = mine_ref[...]
    state[1 - core_ref[0]] = other_ref[...]

    def halves_mean(x):
        a = jnp.sum(jnp.where(first, x, 0.0), axis=1, keepdims=True)
        b = jnp.sum(jnp.where(first, 0.0, x), axis=1, keepdims=True)
        return jnp.where(first, a, b) * (1.0 / HD)

    for p in range(q_ref.shape[1] // PAIR):
        cols = slice(p * PAIR, (p + 1) * PAIR)
        s = jnp.concatenate([state[0, :, cols], state[1, :, cols]], axis=0)
        s_zero = jnp.zeros_like(s)
        block = jnp.concatenate(
            [jnp.where(first_s, s, s_zero), jnp.where(first_s, s_zero, s)], axis=0
        )
        mixed = inner_ref[:, cols] + dot(q_ref[:, cols], block)
        centered = mixed - halves_mean(mixed)
        spread = halves_mean(centered * centered)
        normed[:, cols] = (centered * lax.rsqrt(spread + 1e-05) * gain_ref[:, cols]).astype(BF)
    quarter = w_ref.shape[0] // 4
    pad = jnp.zeros((tokens, o0.shape[1] - quarter), BF)
    for j, o in enumerate((o0, o1, o2, o3)):
        start = pl.multiple_of(lax.rem(at_ref[0] + j, 4) * quarter, quarter)
        part = dot(normed[...], w_ref[pl.ds(start, quarter), :], ((1,), (1,)))
        o[:, :quarter] = part.astype(BF)
        o[:, quarter:] = pad


def route_body(experts, ids_ref, gates_ref, place_ref, higat_ref, low_ref):
    top, tokens = ids_ref.shape
    rows = place_ref.shape[0]
    capacity = rows // experts
    expert = lax.broadcasted_iota(jnp.int32, (experts, tokens), 0)
    member = jnp.zeros((experts, tokens), F32)
    gate = jnp.zeros((experts, tokens), F32)
    for c in range(top):
        hit = ids_ref[c : c + 1, :] == expert
        member = member + jnp.where(hit, 1.0, 0.0)
        gate = gate + jnp.where(hit, gates_ref[c : c + 1, :], 0.0)
    earlier = lax.broadcasted_iota(jnp.int32, (tokens, tokens), 0) < lax.broadcasted_iota(
        jnp.int32, (tokens, tokens), 1
    )
    rank = dot(member.astype(BF), jnp.where(earlier, 1.0, 0.0).astype(BF))
    rank = jnp.where(member > 0.0, rank, -1.0)
    shape = (experts, capacity, tokens)
    slot = lax.broadcasted_iota(jnp.int32, shape, 1).astype(F32)
    placed = jnp.where(jnp.broadcast_to(rank[:, None, :], shape) == slot, 1.0, 0.0)
    weighted = (placed * jnp.broadcast_to(gate[:, None, :], shape)).reshape(rows, tokens)
    place_ref[...] = placed.reshape(rows, tokens).astype(BF)
    mix = weighted.T
    high = mix.astype(BF)
    higat_ref[...] = high
    low_ref[...] = (mix - high.astype(F32)).astype(BF)


def pack_body(at_ref, p0, p1, p2, p3, res_ref, gain_ref, place_ref, packed_ref, att_ref, rows, gains):
    quarter = att_ref.shape[1]
    start = pl.multiple_of(at_ref[0] * quarter, quarter)
    att = res_ref[pl.ds(start, quarter), :].astype(F32).T
    for p in (p0, p1, p2, p3):
        att = att + p[:, :quarter].astype(F32)
    att_ref[...] = att
    square = jnp.sum(att * att, axis=1, keepdims=True)
    high = square.astype(BF).astype(F32)
    middle = (square - high).astype(BF).astype(F32)
    low = square - high - middle
    lane = lax.broadcasted_iota(jnp.int32, (att.shape[0], SPARE), 1)
    extra = jnp.where(lane == 0, high, jnp.where(lane == 1, middle, jnp.where(lane == 2, low, 0.0)))
    for q in range(4):
        gains[q] = gain_ref[:, q * quarter : (q + 1) * quarter]
    rows[:, :quarter] = (att * gains[at_ref[0]]).astype(BF)
    rows[:, quarter:] = extra.astype(BF)
    packed_ref[...] = dot(place_ref[...], rows[...]).astype(BF)


def weights_body(at_ref, gate_ref, up_ref, down_ref, mid_ref, out_ref):
    hidden, features = down_ref.shape
    quarter = features // 4
    padded = mid_ref.shape[1]
    wide = mid_ref.shape[2] // 2
    for q in range(4):
        place = lax.rem(q + 4 - at_ref[0], 4)
        cols = slice(q * quarter, (q + 1) * quarter)
        for side, ref in enumerate((gate_ref, up_ref)):
            lanes = slice(side * wide, (side + 1) * wide)
            tall = [ref[:, cols].astype(F32), jnp.zeros((wide - hidden, quarter), F32)]
            mid_ref[place, :quarter, lanes] = jnp.concatenate(tall, axis=0).T.astype(BF)
            mid_ref[place, quarter:, lanes] = jnp.zeros((padded - quarter, wide), BF)
        pad = jnp.zeros((hidden, padded - quarter), BF)
        out_ref[place] = jnp.concatenate([down_ref[:, cols], pad], axis=1)


def expert_body(features, x0, x1, x2, x3, mid0, out0, mid1, out1, t0, t1, t2, t3, held, total):
    quarter = features // 4
    hidden_count = out0.shape[1]
    wide = mid0.shape[2] // 2
    square = None
    for j, x in enumerate((x0, x1, x2, x3)):
        held[j] = x[...]
        tail = jnp.sum(x[:, quarter:].astype(F32), axis=1, keepdims=True)
        square = tail if j == 0 else square + tail
    scaling = lax.rsqrt(square * (1.0 / features) + 1e-06)
    total[...] = jnp.zeros_like(total)

    def gather(j, carry):
        row = held[j]
        total[0] += dot(row, mid0[j])
        total[1] += dot(row, mid1[j])
        return carry

    lax.fori_loop(0, 4, gather, 0)
    hidden = []
    for side in range(2):
        gate = total[side, :, :hidden_count] * scaling
        up = total[side, :, wide : wide + hidden_count] * scaling
        hidden.append((gate / (1.0 + jnp.exp(-gate)) * up).astype(BF))

    def spread(j, carry):
        held[j] = (dot(hidden[0], out0[j]) + dot(hidden[1], out1[j])).astype(BF)
        return carry

    lax.fori_loop(0, 4, spread, 0)
    for j, t in enumerate((t0, t1, t2, t3)):
        t[...] = held[j]


def mix_body(at_ref, back_ref, higat_ref, low_ref, att_ref, o0, o1, o2, o3, done):
    back = back_ref[...]
    quarter = att_ref.shape[1]
    mixture = dot(higat_ref[...], back) + dot(low_ref[...], back)
    done[:, :quarter] = (att_ref[...] + mixture[:, :quarter]).astype(BF)
    done[:, quarter:] = mixture[:, quarter:].astype(BF)
    share = o0.shape[0]
    for j, o in enumerate((o0, o1, o2, o3)):
        start = pl.multiple_of(lax.rem(at_ref[0] + j, 4) * share, share)
        o[...] = done[pl.ds(start, share), :]


def join_body(at_ref, r0, r1, r2, r3, o_ref, held):
    quarter = o_ref.shape[1] // 4
    for j, r in enumerate((r0, r1, r2, r3)):
        held[lax.rem(at_ref[0] + 4 - j, 4)] = r[...]
    for q in range(4):
        o_ref[:, q * quarter : (q + 1) * quarter] = held[q, :, :quarter]


def shift(x, by):
    return lax.ppermute(x, "heads", [(i, (i + by) % 4) for i in range(4)])


def swap(x):
    return lax.ppermute(x, "core", [(0, 1), (1, 0)])


def plus(*terms):
    total = terms[0].astype(F32)
    for term in terms[1:]:
        total = total + term.astype(F32)
    return total.astype(BF)


def on_device(
    residual,
    query_rows,
    key_rows,
    value_rows,
    norm_gain,
    out_weight,
    moe_gain,
    expert_ids,
    gate_values,
    gate_weight,
    up_weight,
    down_weight,
):
    tokens, width = query_rows.shape
    features = residual.shape[1]
    quarter = features // 4
    padded = quarter + SPARE
    chip = ("z", "x")
    chips = lax.axis_size("z") * lax.axis_size("x")
    ids = tuple(
        jnp.full((1,), lax.axis_index(name).astype(jnp.int32)) for name in ("heads", "core", "z", "x")
    )
    (h_at, core_at, z_at, x_at), key_rows = lax.optimization_barrier((ids, key_rows))
    capacity = min(tokens, 3 * tokens * expert_ids.shape[1] // (2 * chips))
    rows = chips * capacity
    shape = jax.ShapeDtypeStruct

    keep, send, key_near, value_near = pl.pallas_call(
        state_body,
        out_shape=(shape((HD // 2, width), BF),) * 2 + (shape((tokens, width), BF),) * 2,
        in_specs=[SMEM_SPEC] + [VMEM_SPEC] * 2,
        out_specs=(VMEM_SPEC,) * 4,
        scratch_shapes=[pltpu.VMEM((2, HD // 2, width), BF)],
        compiler_params=params(28),
        name="own_state",
    )(core_at, key_rows, value_rows)
    taken = swap(send)
    inner = pl.pallas_call(
        inner_body,
        out_shape=shape((tokens, width), F32),
        in_specs=[VMEM_SPEC] * 3,
        out_specs=VMEM_SPEC,
        compiler_params=params(28),
        cost_estimate=cost(2e9, 2e6),
        name="inner",
    )(query_rows, key_near, value_near)
    chip_state = plus(keep, taken)
    depth, breadth = lax.axis_size("z"), lax.axis_size("x")
    beside = [
        lax.ppermute(chip_state, "x", [(i, (i + j) % breadth) for i in range(breadth)])
        for j in range(1, breadth)
    ]
    slab_state = plus(chip_state, *beside)

    def deeper(x, j):
        return lax.ppermute(x, "z", [(i, (i + j) % depth) for i in range(depth)])

    near = [deeper(slab_state, 1), deeper(slab_state, 2)]
    near, inner = lax.optimization_barrier((near, inner))
    triple = pl.pallas_call(
        triple_body,
        out_shape=shape(keep.shape, BF),
        in_specs=[SMEM_SPEC] + [VMEM_SPEC] * 3,
        out_specs=VMEM_SPEC,
        compiler_params=params(28),
        name="triple",
    )(z_at, slab_state, *near)
    mine, theirs = pl.pallas_call(
        before_body,
        out_shape=(shape(keep.shape, BF),) * 2,
        in_specs=[SMEM_SPEC] * 3 + [VMEM_SPEC] * 9,
        out_specs=(VMEM_SPEC,) * 2,
        compiler_params=params(28),
        name="before",
    )(core_at, z_at, x_at, keep, taken, *near, deeper(triple, 3), deeper(triple, 6), *beside)
    other = swap(theirs)

    place, mix_high, mix_low = pl.pallas_call(
        functools.partial(route_body, chips),
        out_shape=(shape((rows, tokens), BF), shape((tokens, rows), BF), shape((tokens, rows), BF)),
        in_specs=[VMEM_SPEC] * 2,
        out_specs=(VMEM_SPEC,) * 3,
        compiler_params=params(28),
        cost_estimate=cost(1e8, 1e6),
        name="route",
    )(expert_ids.T, gate_values.T)

    parts = pl.pallas_call(
        attend_body,
        out_shape=(shape((tokens, padded), BF),) * 4,
        in_specs=[SMEM_SPEC] * 2 + [VMEM_SPEC] * 6,
        out_specs=(VMEM_SPEC,) * 4,
        scratch_shapes=[pltpu.VMEM((tokens, width), BF), pltpu.VMEM((2, HD // 2, width), BF)],
        compiler_params=params(28),
        name="attend",
    )(h_at, core_at, query_rows, inner, mine, other, norm_gain.reshape(1, width), out_weight.T)
    across = shift(parts[2], 2)
    pieces = [parts[0], shift(parts[1], 1), across, shift(parts[3], 3)]

    packed, attended = pl.pallas_call(
        pack_body,
        out_shape=(shape((rows, padded), BF), shape((tokens, quarter), F32)),
        in_specs=[SMEM_SPEC] + [VMEM_SPEC] * 7,
        out_specs=(VMEM_SPEC,) * 2,
        scratch_shapes=[pltpu.VMEM((tokens, padded), BF), pltpu.VMEM((4, 1, quarter), F32)],
        compiler_params=params(28),
        name="pack",
    )(h_at, *pieces, residual.T, moe_gain.reshape(1, features), place)

    arrived = lax.all_to_all(
        packed.reshape(chips, capacity, padded), chip, 0, 0, tiled=True
    ).reshape(rows, padded)
    half = rows // 2
    arrived, late_h = lax.optimization_barrier((arrived, h_at))
    low, high = arrived[:half], arrived[half:]

    minus_low, plus_low = shift(low, 1), shift(low, -1)
    hidden_count = gate_weight.shape[2]
    wide = -(-hidden_count // 128) * 128
    weights = pl.pallas_call(
        weights_body,
        out_shape=(shape((4, padded, 2 * wide), BF), shape((4, hidden_count, padded), BF)),
        in_specs=[SMEM_SPEC] + [VMEM_SPEC] * 3,
        out_specs=(VMEM_SPEC,) * 2,
        compiler_params=params(28),
        cost_estimate=cost(5e9, 13e6),
        name="weights",
    )(late_h, gate_weight[0].T, up_weight[0].T, down_weight[0])
    minus_low, plus_low, high, weights = lax.optimization_barrier(
        (minus_low, plus_low, high, weights)
    )
    other_weights = tuple(swap(x) for x in weights)

    def experts(group):
        return pl.pallas_call(
            functools.partial(expert_body, features),
            out_shape=(shape((half, padded), BF),) * 4,
            in_specs=[VMEM_SPEC] * 8,
            out_specs=(VMEM_SPEC,) * 4,
            scratch_shapes=[
                pltpu.VMEM((4, half, padded), BF),
                pltpu.VMEM((2, half, 2 * wide), F32),
            ],
            compiler_params=params(28),
            cost_estimate=cost(1e6, 1e5),
            name="experts",
        )(*group, *weights, *other_weights)

    far_low, plus_high = shift(minus_low, 1), shift(high, -1)
    far_low, plus_high, high = lax.optimization_barrier((far_low, plus_high, high))
    far_high, minus_high = shift(plus_high, -1), shift(high, 1)
    sum_low = experts((low, plus_low, far_low, minus_low))
    via_low, got_low_plus = shift(sum_low[2], 1), shift(sum_low[3], -1)
    sum_high = experts((high, plus_high, far_high, minus_high))
    via_low, got_low_plus = lax.optimization_barrier((via_low, got_low_plus))
    got_low_minus = shift(plus(sum_low[1], via_low), 1)
    via_high = shift(sum_high[2], -1)
    got_high_minus = shift(sum_high[1], 1)
    got_high_plus = shift(plus(sum_high[3], via_high), -1)
    total_low = plus(sum_low[0], got_low_minus, got_low_plus)
    total_high = plus(sum_high[0], got_high_minus, got_high_plus)
    leaving = jnp.concatenate([total_low, total_high], axis=0).reshape(chips, capacity, padded)
    returned = lax.all_to_all(leaving, chip, 0, 0, tiled=True).reshape(rows, padded)

    share = tokens // 4
    ends = pl.pallas_call(
        mix_body,
        out_shape=(shape((share, padded), BF),) * 4,
        in_specs=[SMEM_SPEC] + [VMEM_SPEC] * 4,
        out_specs=(VMEM_SPEC,) * 4,
        scratch_shapes=[pltpu.VMEM((tokens, padded), BF)],
        compiler_params=params(28),
        name="mix",
    )(h_at, returned, mix_high, mix_low, attended)
    across = shift(ends[2], 2)
    finals = [ends[0], shift(ends[1], 1), across, shift(ends[3], 3)]
    return pl.pallas_call(
        join_body,
        out_shape=shape((share, features), BF),
        in_specs=[SMEM_SPEC] + [VMEM_SPEC] * 4,
        out_specs=VMEM_SPEC,
        scratch_shapes=[pltpu.VMEM((4, share, padded), BF)],
        compiler_params=params(28),
        name="join",
    )(h_at, *finals)


def solution(mesh):
    devices = mesh.devices
    split = Mesh(
        devices.reshape(-1, BREADTH, CORES, devices.shape[1]), ("z", "x", "core", "heads")
    )
    context = ("z", "x", "core")
    in_specs = (
        P(context, None),
        P(context, "heads"),
        P(context, "heads"),
        P(context, "heads"),
        P("heads"),
        P("heads", None),
        P(),
        P(context, None),
        P(context, None),
        P(context, None, "heads"),
        P(context, None, "heads"),
        P(context, "heads", None),
    )
    return jax.shard_map(
        on_device,
        mesh=split,
        in_specs=in_specs,
        out_specs=P(("z", "x", "core", "heads"), None),
        check_vma=False,
    )
```

```python
import functools

import jax
import jax.numpy as jnp
from jax import lax
from jax.experimental import pallas as pl
from jax.experimental.pallas import tpu as pltpu
from jax.sharding import Mesh
from jax.sharding import PartitionSpec as P

HD = 64
PAIR = 2 * HD
CORES = 2
BREADTH = 4
SPARE = 48
BF = jnp.bfloat16
F32 = jnp.float32
VMEM_SPEC = pl.BlockSpec(memory_space=pltpu.VMEM)
SMEM_SPEC = pl.BlockSpec(memory_space=pltpu.SMEM)


def params(mib):
    return pltpu.CompilerParams(vmem_limit_bytes=mib << 20)


def cost(flops, moved):
    return pl.CostEstimate(flops=int(flops), bytes_accessed=int(moved), transcendentals=0)


def dot(a, b, dims=((1,), (0,))):
    return lax.dot_general(a, b, (dims, ((), ())), preferred_element_type=F32)


def state_body(at_ref, k_ref, v_ref, keep_ref, send_ref, k_out, v_out, both_ref):
    k_out[...] = k_ref[...]
    v_out[...] = v_ref[...]
    first = lax.broadcasted_iota(jnp.int32, (HD, PAIR), 1) < HD
    half = HD // 2
    for p in range(k_ref.shape[1] // PAIR):
        cols = slice(p * PAIR, (p + 1) * PAIR)
        both = dot(k_ref[:, cols], v_ref[:, cols], ((0,), (0,)))
        state = jnp.where(first, both[:HD], both[HD:]).astype(BF)
        both_ref[0, :, cols] = state[:half]
        both_ref[1, :, cols] = state[half:]
    keep_ref[...] = both_ref[at_ref[0]]
    send_ref[...] = both_ref[1 - at_ref[0]]


def flag(condition):
    return jnp.where(condition, 1.0, 0.0)


def triple_body(at_ref, slab_ref, near_ref, next_ref, o_ref):
    z = at_ref[0]
    total = slab_ref[...].astype(F32) + flag(z >= 1) * near_ref[...].astype(F32)
    o_ref[...] = (total + flag(z >= 2) * next_ref[...].astype(F32)).astype(BF)


def before_body(core_ref, z_ref, x_ref, keep_ref, taken_ref, *rest):
    mine_ref, theirs_ref = rest[-2:]
    z, x, later = z_ref[0], x_ref[0], flag(core_ref[0] == 1)
    weights = [flag(z >= j) for j in (1, 2, 3, 6)] + [flag(x > j) for j in range(3)]
    base = jnp.zeros(keep_ref.shape, F32)
    for weight, ref in zip(weights, rest[:-2]):
        base = base + weight * ref[...].astype(F32)
    mine_ref[...] = (base + later * taken_ref[...].astype(F32)).astype(BF)
    theirs_ref[...] = (base + (1.0 - later) * keep_ref[...].astype(F32)).astype(BF)


def inner_body(q_ref, k_ref, v_ref, o_ref):
    tokens = q_ref.shape[0]
    first = lax.broadcasted_iota(jnp.int32, (tokens, PAIR), 1) < HD
    causal = lax.broadcasted_iota(jnp.int32, (tokens, tokens), 0) >= lax.broadcasted_iota(
        jnp.int32, (tokens, tokens), 1
    )
    zero = jnp.zeros((tokens, PAIR), BF)
    for p in range(q_ref.shape[1] // PAIR):
        cols = slice(p * PAIR, (p + 1) * PAIR)
        q, k, v = q_ref[:, cols], k_ref[:, cols], v_ref[:, cols]
        inner = []
        for keep in (jnp.where(first, q, zero), jnp.where(first, zero, q)):
            scores = dot(keep, k, ((1,), (1,)))
            weights = jnp.where(causal, scores, 0.0).astype(BF)
            inner.append(dot(weights, v))
        o_ref[:, cols] = jnp.where(first, inner[0], inner[1])


def attend_body(
    at_ref, core_ref, q_ref, inner_ref, mine_ref, other_ref, gain_ref, w_ref, o0, o1, o2, o3, normed, state
):
    tokens = q_ref.shape[0]
    first = lax.broadcasted_iota(jnp.int32, (tokens, PAIR), 1) < HD
    first_s = lax.broadcasted_iota(jnp.int32, (HD, PAIR), 1) < HD
    state[core_ref[0]] = mine_ref[...]
    state[1 - core_ref[0]] = other_ref[...]

    def halves_mean(x):
        a = jnp.sum(jnp.where(first, x, 0.0), axis=1, keepdims=True)
        b = jnp.sum(jnp.where(first, 0.0, x), axis=1, keepdims=True)
        return jnp.where(first, a, b) * (1.0 / HD)

    for p in range(q_ref.shape[1] // PAIR):
        cols = slice(p * PAIR, (p + 1) * PAIR)
        s = jnp.concatenate([state[0, :, cols], state[1, :, cols]], axis=0)
        s_zero = jnp.zeros_like(s)
        block = jnp.concatenate(
            [jnp.where(first_s, s, s_zero), jnp.where(first_s, s_zero, s)], axis=0
        )
        mixed = inner_ref[:, cols] + dot(q_ref[:, cols], block)
        centered = mixed - halves_mean(mixed)
        spread = halves_mean(centered * centered)
        normed[:, cols] = (centered * lax.rsqrt(spread + 1e-05) * gain_ref[:, cols]).astype(BF)
    quarter = w_ref.shape[0] // 4
    pad = jnp.zeros((tokens, o0.shape[1] - quarter), BF)
    for j, o in enumerate((o0, o1, o2, o3)):
        start = pl.multiple_of(lax.rem(at_ref[0] + j, 4) * quarter, quarter)
        part = dot(normed[...], w_ref[pl.ds(start, quarter), :], ((1,), (1,)))
        o[:, :quarter] = part.astype(BF)
        o[:, quarter:] = pad


def route_body(experts, ids_ref, gates_ref, place_ref, higat_ref, low_ref):
    top, tokens = ids_ref.shape
    rows = place_ref.shape[0]
    capacity = rows // experts
    expert = lax.broadcasted_iota(jnp.int32, (experts, tokens), 0)
    member = jnp.zeros((experts, tokens), F32)
    gate = jnp.zeros((experts, tokens), F32)
    for c in range(top):
        hit = ids_ref[c : c + 1, :] == expert
        member = member + jnp.where(hit, 1.0, 0.0)
        gate = gate + jnp.where(hit, gates_ref[c : c + 1, :], 0.0)
    earlier = lax.broadcasted_iota(jnp.int32, (tokens, tokens), 0) < lax.broadcasted_iota(
        jnp.int32, (tokens, tokens), 1
    )
    rank = dot(member.astype(BF), jnp.where(earlier, 1.0, 0.0).astype(BF))
    rank = jnp.where(member > 0.0, rank, -1.0)
    shape = (experts, capacity, tokens)
    slot = lax.broadcasted_iota(jnp.int32, shape, 1).astype(F32)
    placed = jnp.where(jnp.broadcast_to(rank[:, None, :], shape) == slot, 1.0, 0.0)
    weighted = (placed * jnp.broadcast_to(gate[:, None, :], shape)).reshape(rows, tokens)
    place_ref[...] = placed.reshape(rows, tokens).astype(BF)
    mix = weighted.T
    high = mix.astype(BF)
    higat_ref[...] = high
    low_ref[...] = (mix - high.astype(F32)).astype(BF)


def pack_body(at_ref, p0, p1, p2, p3, res_ref, gain_ref, place_ref, packed_ref, att_ref, rows, gains):
    quarter = att_ref.shape[1]
    start = pl.multiple_of(at_ref[0] * quarter, quarter)
    att = res_ref[pl.ds(start, quarter), :].astype(F32).T
    for p in (p0, p1, p2, p3):
        att = att + p[:, :quarter].astype(F32)
    att_ref[...] = att
    square = jnp.sum(att * att, axis=1, keepdims=True)
    high = square.astype(BF).astype(F32)
    middle = (square - high).astype(BF).astype(F32)
    low = square - high - middle
    lane = lax.broadcasted_iota(jnp.int32, (att.shape[0], SPARE), 1)
    extra = jnp.where(lane == 0, high, jnp.where(lane == 1, middle, jnp.where(lane == 2, low, 0.0)))
    for q in range(4):
        gains[q] = gain_ref[:, q * quarter : (q + 1) * quarter]
    rows[:, :quarter] = (att * gains[at_ref[0]]).astype(BF)
    rows[:, quarter:] = extra.astype(BF)
    packed_ref[...] = dot(place_ref[...], rows[...]).astype(BF)


def weights_body(at_ref, gate_ref, up_ref, down_ref, mid_ref, out_ref):
    hidden, features = down_ref.shape
    quarter = features // 4
    padded = mid_ref.shape[1]
    wide = mid_ref.shape[2] // 2
    for q in range(4):
        place = lax.rem(q + 4 - at_ref[0], 4)
        cols = slice(q * quarter, (q + 1) * quarter)
        for side, ref in enumerate((gate_ref, up_ref)):
            lanes = slice(side * wide, (side + 1) * wide)
            tall = [ref[:, cols].astype(F32), jnp.zeros((wide - hidden, quarter), F32)]
            mid_ref[place, :quarter, lanes] = jnp.concatenate(tall, axis=0).T.astype(BF)
            mid_ref[place, quarter:, lanes] = jnp.zeros((padded - quarter, wide), BF)
        pad = jnp.zeros((hidden, padded - quarter), BF)
        out_ref[place] = jnp.concatenate([down_ref[:, cols], pad], axis=1)


def expert_body(features, x0, x1, x2, x3, mid0, out0, mid1, out1, t0, t1, t2, t3, held, total):
    quarter = features // 4
    hidden_count = out0.shape[1]
    wide = mid0.shape[2] // 2
    square = None
    for j, x in enumerate((x0, x1, x2, x3)):
        held[j] = x[...]
        tail = jnp.sum(x[:, quarter:].astype(F32), axis=1, keepdims=True)
        square = tail if j == 0 else square + tail
    scaling = lax.rsqrt(square * (1.0 / features) + 1e-06)
    total[...] = jnp.zeros_like(total)

    def gather(j, carry):
        row = held[j]
        total[0] += dot(row, mid0[j])
        total[1] += dot(row, mid1[j])
        return carry

    lax.fori_loop(0, 4, gather, 0)
    hidden = []
    for side in range(2):
        gate = total[side, :, :hidden_count] * scaling
        up = total[side, :, wide : wide + hidden_count] * scaling
        hidden.append((gate / (1.0 + jnp.exp(-gate)) * up).astype(BF))

    def spread(j, carry):
        held[j] = (dot(hidden[0], out0[j]) + dot(hidden[1], out1[j])).astype(BF)
        return carry

    lax.fori_loop(0, 4, spread, 0)
    for j, t in enumerate((t0, t1, t2, t3)):
        t[...] = held[j]


def mix_body(at_ref, back_ref, higat_ref, low_ref, att_ref, o0, o1, o2, o3, done):
    back = back_ref[...]
    quarter = att_ref.shape[1]
    mixture = dot(higat_ref[...], back) + dot(low_ref[...], back)
    done[:, :quarter] = (att_ref[...] + mixture[:, :quarter]).astype(BF)
    done[:, quarter:] = mixture[:, quarter:].astype(BF)
    share = o0.shape[0]
    for j, o in enumerate((o0, o1, o2, o3)):
        start = pl.multiple_of(lax.rem(at_ref[0] + j, 4) * share, share)
        o[...] = done[pl.ds(start, share), :]


def join_body(at_ref, r0, r1, r2, r3, o_ref, held):
    quarter = o_ref.shape[1] // 4
    for j, r in enumerate((r0, r1, r2, r3)):
        held[lax.rem(at_ref[0] + 4 - j, 4)] = r[...]
    for q in range(4):
        o_ref[:, q * quarter : (q + 1) * quarter] = held[q, :, :quarter]


def shift(x, by):
    return lax.ppermute(x, "heads", [(i, (i + by) % 4) for i in range(4)])


def swap(x):
    return lax.ppermute(x, "core", [(0, 1), (1, 0)])


def plus(*terms):
    total = terms[0].astype(F32)
    for term in terms[1:]:
        total = total + term.astype(F32)
    return total.astype(BF)


def on_device(
    residual,
    query_rows,
    key_rows,
    value_rows,
    norm_gain,
    out_weight,
    moe_gain,
    expert_ids,
    gate_values,
    gate_weight,
    up_weight,
    down_weight,
):
    tokens, width = query_rows.shape
    features = residual.shape[1]
    quarter = features // 4
    padded = quarter + SPARE
    chip = ("z", "x")
    chips = lax.axis_size("z") * lax.axis_size("x")
    ids = tuple(
        jnp.full((1,), lax.axis_index(name).astype(jnp.int32)) for name in ("heads", "core", "z", "x")
    )
    (h_at, core_at, z_at, x_at), key_rows = lax.optimization_barrier((ids, key_rows))
    capacity = min(tokens, 3 * tokens * expert_ids.shape[1] // (2 * chips))
    rows = chips * capacity
    shape = jax.ShapeDtypeStruct

    keep, send, key_near, value_near = pl.pallas_call(
        state_body,
        out_shape=(shape((HD // 2, width), BF),) * 2 + (shape((tokens, width), BF),) * 2,
        in_specs=[SMEM_SPEC] + [VMEM_SPEC] * 2,
        out_specs=(VMEM_SPEC,) * 4,
        scratch_shapes=[pltpu.VMEM((2, HD // 2, width), BF)],
        compiler_params=params(28),
        name="own_state",
    )(core_at, key_rows, value_rows)
    taken = swap(send)
    inner = pl.pallas_call(
        inner_body,
        out_shape=shape((tokens, width), F32),
        in_specs=[VMEM_SPEC] * 3,
        out_specs=VMEM_SPEC,
        compiler_params=params(28),
        cost_estimate=cost(2e9, 2e6),
        name="inner",
    )(query_rows, key_near, value_near)
    chip_state = plus(keep, taken)
    depth, breadth = lax.axis_size("z"), lax.axis_size("x")
    beside = [
        lax.ppermute(chip_state, "x", [(i, (i + j) % breadth) for i in range(breadth)])
        for j in range(1, breadth)
    ]
    slab_state = plus(chip_state, *beside)

    def deeper(x, j):
        return lax.ppermute(x, "z", [(i, (i + j) % depth) for i in range(depth)])

    near = [deeper(slab_state, 1), deeper(slab_state, 2)]
    near, inner = lax.optimization_barrier((near, inner))
    triple = pl.pallas_call(
        triple_body,
        out_shape=shape(keep.shape, BF),
        in_specs=[SMEM_SPEC] + [VMEM_SPEC] * 3,
        out_specs=VMEM_SPEC,
        compiler_params=params(28),
        name="triple",
    )(z_at, slab_state, *near)
    mine, theirs = pl.pallas_call(
        before_body,
        out_shape=(shape(keep.shape, BF),) * 2,
        in_specs=[SMEM_SPEC] * 3 + [VMEM_SPEC] * 9,
        out_specs=(VMEM_SPEC,) * 2,
        compiler_params=params(28),
        name="before",
    )(core_at, z_at, x_at, keep, taken, *near, deeper(triple, 3), deeper(triple, 6), *beside)
    other = swap(theirs)

    place, mix_high, mix_low = pl.pallas_call(
        functools.partial(route_body, chips),
        out_shape=(shape((rows, tokens), BF), shape((tokens, rows), BF), shape((tokens, rows), BF)),
        in_specs=[VMEM_SPEC] * 2,
        out_specs=(VMEM_SPEC,) * 3,
        compiler_params=params(28),
        cost_estimate=cost(1e8, 1e6),
        name="route",
    )(expert_ids.T, gate_values.T)

    parts = pl.pallas_call(
        attend_body,
        out_shape=(shape((tokens, padded), BF),) * 4,
        in_specs=[SMEM_SPEC] * 2 + [VMEM_SPEC] * 6,
        out_specs=(VMEM_SPEC,) * 4,
        scratch_shapes=[pltpu.VMEM((tokens, width), BF), pltpu.VMEM((2, HD // 2, width), BF)],
        compiler_params=params(28),
        name="attend",
    )(h_at, core_at, query_rows, inner, mine, other, norm_gain.reshape(1, width), out_weight.T)
    across = shift(parts[2], 2)
    pieces = [parts[0], shift(parts[1], 1), across, shift(parts[3], 3)]

    packed, attended = pl.pallas_call(
        pack_body,
        out_shape=(shape((rows, padded), BF), shape((tokens, quarter), F32)),
        in_specs=[SMEM_SPEC] + [VMEM_SPEC] * 7,
        out_specs=(VMEM_SPEC,) * 2,
        scratch_shapes=[pltpu.VMEM((tokens, padded), BF), pltpu.VMEM((4, 1, quarter), F32)],
        compiler_params=params(28),
        name="pack",
    )(h_at, *pieces, residual.T, moe_gain.reshape(1, features), place)

    arrived = lax.all_to_all(
        packed.reshape(chips, capacity, padded), chip, 0, 0, tiled=True
    ).reshape(rows, padded)
    half = rows // 2
    arrived, late_h = lax.optimization_barrier((arrived, h_at))
    low, high = arrived[:half], arrived[half:]

    minus_low, plus_low = shift(low, 1), shift(low, -1)
    hidden_count = gate_weight.shape[2]
    wide = -(-hidden_count // 128) * 128
    weights = pl.pallas_call(
        weights_body,
        out_shape=(shape((4, padded, 2 * wide), BF), shape((4, hidden_count, padded), BF)),
        in_specs=[SMEM_SPEC] + [VMEM_SPEC] * 3,
        out_specs=(VMEM_SPEC,) * 2,
        compiler_params=params(28),
        cost_estimate=cost(5e9, 13e6),
        name="weights",
    )(late_h, gate_weight[0].T, up_weight[0].T, down_weight[0])
    minus_low, plus_low, high, weights = lax.optimization_barrier(
        (minus_low, plus_low, high, weights)
    )
    other_weights = tuple(swap(x) for x in weights)

    def experts(group):
        return pl.pallas_call(
            functools.partial(expert_body, features),
            out_shape=(shape((half, padded), BF),) * 4,
            in_specs=[VMEM_SPEC] * 8,
            out_specs=(VMEM_SPEC,) * 4,
            scratch_shapes=[
                pltpu.VMEM((4, half, padded), BF),
                pltpu.VMEM((2, half, 2 * wide), F32),
            ],
            compiler_params=params(28),
            cost_estimate=cost(1e6, 1e5),
            name="experts",
        )(*group, *weights, *other_weights)

    far_low, plus_high = shift(minus_low, 1), shift(high, -1)
    far_low, high = lax.optimization_barrier((far_low, high))
    far_high, minus_high = shift(plus_high, -1), shift(high, 1)
    sum_low = experts((low, plus_low, far_low, minus_low))
    via_low, got_low_plus = shift(sum_low[2], 1), shift(sum_low[3], -1)
    sum_high = experts((high, plus_high, far_high, minus_high))
    via_low, got_low_plus = lax.optimization_barrier((via_low, got_low_plus))
    got_low_minus = shift(plus(sum_low[1], via_low), 1)
    via_high = shift(sum_high[2], -1)
    got_high_minus = shift(sum_high[1], 1)
    got_high_plus = shift(plus(sum_high[3], via_high), -1)
    total_low = plus(sum_low[0], got_low_minus, got_low_plus)
    total_high = plus(sum_high[0], got_high_minus, got_high_plus)
    leaving = jnp.concatenate([total_low, total_high], axis=0).reshape(chips, capacity, padded)
    returned = lax.all_to_all(leaving, chip, 0, 0, tiled=True).reshape(rows, padded)

    share = tokens // 4
    ends = pl.pallas_call(
        mix_body,
        out_shape=(shape((share, padded), BF),) * 4,
        in_specs=[SMEM_SPEC] + [VMEM_SPEC] * 4,
        out_specs=(VMEM_SPEC,) * 4,
        scratch_shapes=[pltpu.VMEM((tokens, padded), BF)],
        compiler_params=params(28),
        name="mix",
    )(h_at, returned, mix_high, mix_low, attended)
    across = shift(ends[2], 2)
    finals = [ends[0], shift(ends[1], 1), across, shift(ends[3], 3)]
    return pl.pallas_call(
        join_body,
        out_shape=shape((share, features), BF),
        in_specs=[SMEM_SPEC] + [VMEM_SPEC] * 4,
        out_specs=VMEM_SPEC,
        scratch_shapes=[pltpu.VMEM((4, share, padded), BF)],
        compiler_params=params(28),
        name="join",
    )(h_at, *finals)


def solution(mesh):
    devices = mesh.devices
    split = Mesh(
        devices.reshape(-1, BREADTH, CORES, devices.shape[1]), ("z", "x", "core", "heads")
    )
    context = ("z", "x", "core")
    in_specs = (
        P(context, None),
        P(context, "heads"),
        P(context, "heads"),
        P(context, "heads"),
        P("heads"),
        P("heads", None),
        P(),
        P(context, None),
        P(context, None),
        P(context, None, "heads"),
        P(context, None, "heads"),
        P(context, "heads", None),
    )
    return jax.shard_map(
        on_device,
        mesh=split,
        in_specs=in_specs,
        out_specs=P(("z", "x", "core", "heads"), None),
        check_vma=False,
    )
```

```python
import functools

import jax
import jax.numpy as jnp
from jax import lax
from jax.experimental import pallas as pl
from jax.experimental.pallas import tpu as pltpu
from jax.sharding import Mesh
from jax.sharding import PartitionSpec as P

HD = 64
PAIR = 2 * HD
CORES = 2
BREADTH = 4
SPARE = 48
BF = jnp.bfloat16
F32 = jnp.float32
VMEM_SPEC = pl.BlockSpec(memory_space=pltpu.VMEM)
SMEM_SPEC = pl.BlockSpec(memory_space=pltpu.SMEM)


def params(mib):
    return pltpu.CompilerParams(vmem_limit_bytes=mib << 20)


def cost(flops, moved):
    return pl.CostEstimate(flops=int(flops), bytes_accessed=int(moved), transcendentals=0)


def dot(a, b, dims=((1,), (0,))):
    return lax.dot_general(a, b, (dims, ((), ())), preferred_element_type=F32)


def state_body(at_ref, k_ref, v_ref, keep_ref, send_ref, k_out, v_out, both_ref):
    k_out[...] = k_ref[...]
    v_out[...] = v_ref[...]
    first = lax.broadcasted_iota(jnp.int32, (HD, PAIR), 1) < HD
    half = HD // 2
    for p in range(k_ref.shape[1] // PAIR):
        cols = slice(p * PAIR, (p + 1) * PAIR)
        both = dot(k_ref[:, cols], v_ref[:, cols], ((0,), (0,)))
        state = jnp.where(first, both[:HD], both[HD:]).astype(BF)
        both_ref[0, :, cols] = state[:half]
        both_ref[1, :, cols] = state[half:]
    keep_ref[...] = both_ref[at_ref[0]]
    send_ref[...] = both_ref[1 - at_ref[0]]


def flag(condition):
    return jnp.where(condition, 1.0, 0.0)


def triple_body(at_ref, slab_ref, near_ref, next_ref, o_ref):
    z = at_ref[0]
    total = slab_ref[...].astype(F32) + flag(z >= 1) * near_ref[...].astype(F32)
    o_ref[...] = (total + flag(z >= 2) * next_ref[...].astype(F32)).astype(BF)


def before_body(core_ref, z_ref, x_ref, keep_ref, taken_ref, *rest):
    mine_ref, theirs_ref = rest[-2:]
    z, x, later = z_ref[0], x_ref[0], flag(core_ref[0] == 1)
    weights = [flag(z >= j) for j in (1, 2, 3, 6)] + [flag(x > j) for j in range(3)]
    base = jnp.zeros(keep_ref.shape, F32)
    for weight, ref in zip(weights, rest[:-2]):
        base = base + weight * ref[...].astype(F32)
    mine_ref[...] = (base + later * taken_ref[...].astype(F32)).astype(BF)
    theirs_ref[...] = (base + (1.0 - later) * keep_ref[...].astype(F32)).astype(BF)


def inner_body(q_ref, k_ref, v_ref, o_ref):
    tokens = q_ref.shape[0]
    first = lax.broadcasted_iota(jnp.int32, (tokens, PAIR), 1) < HD
    causal = lax.broadcasted_iota(jnp.int32, (tokens, tokens), 0) >= lax.broadcasted_iota(
        jnp.int32, (tokens, tokens), 1
    )
    zero = jnp.zeros((tokens, PAIR), BF)
    for p in range(q_ref.shape[1] // PAIR):
        cols = slice(p * PAIR, (p + 1) * PAIR)
        q, k, v = q_ref[:, cols], k_ref[:, cols], v_ref[:, cols]
        inner = []
        for keep in (jnp.where(first, q, zero), jnp.where(first, zero, q)):
            scores = dot(keep, k, ((1,), (1,)))
            weights = jnp.where(causal, scores, 0.0).astype(BF)
            inner.append(dot(weights, v))
        o_ref[:, cols] = jnp.where(first, inner[0], inner[1])


def attend_body(
    at_ref, core_ref, q_ref, inner_ref, mine_ref, other_ref, gain_ref, w_ref, o0, o1, o2, o3, normed, state
):
    tokens = q_ref.shape[0]
    first = lax.broadcasted_iota(jnp.int32, (tokens, PAIR), 1) < HD
    first_s = lax.broadcasted_iota(jnp.int32, (HD, PAIR), 1) < HD
    state[core_ref[0]] = mine_ref[...]
    state[1 - core_ref[0]] = other_ref[...]

    def halves_mean(x):
        a = jnp.sum(jnp.where(first, x, 0.0), axis=1, keepdims=True)
        b = jnp.sum(jnp.where(first, 0.0, x), axis=1, keepdims=True)
        return jnp.where(first, a, b) * (1.0 / HD)

    for p in range(q_ref.shape[1] // PAIR):
        cols = slice(p * PAIR, (p + 1) * PAIR)
        s = jnp.concatenate([state[0, :, cols], state[1, :, cols]], axis=0)
        s_zero = jnp.zeros_like(s)
        block = jnp.concatenate(
            [jnp.where(first_s, s, s_zero), jnp.where(first_s, s_zero, s)], axis=0
        )
        mixed = inner_ref[:, cols] + dot(q_ref[:, cols], block)
        centered = mixed - halves_mean(mixed)
        spread = halves_mean(centered * centered)
        normed[:, cols] = (centered * lax.rsqrt(spread + 1e-05) * gain_ref[:, cols]).astype(BF)
    quarter = w_ref.shape[0] // 4
    pad = jnp.zeros((tokens, o0.shape[1] - quarter), BF)
    for j, o in enumerate((o0, o1, o2, o3)):
        start = pl.multiple_of(lax.rem(at_ref[0] + j, 4) * quarter, quarter)
        part = dot(normed[...], w_ref[pl.ds(start, quarter), :], ((1,), (1,)))
        o[:, :quarter] = part.astype(BF)
        o[:, quarter:] = pad


def route_body(experts, ids_ref, gates_ref, place_ref, higat_ref, low_ref):
    top, tokens = ids_ref.shape
    rows = place_ref.shape[0]
    capacity = rows // experts
    expert = lax.broadcasted_iota(jnp.int32, (experts, tokens), 0)
    member = jnp.zeros((experts, tokens), F32)
    gate = jnp.zeros((experts, tokens), F32)
    for c in range(top):
        hit = ids_ref[c : c + 1, :] == expert
        member = member + jnp.where(hit, 1.0, 0.0)
        gate = gate + jnp.where(hit, gates_ref[c : c + 1, :], 0.0)
    earlier = lax.broadcasted_iota(jnp.int32, (tokens, tokens), 0) < lax.broadcasted_iota(
        jnp.int32, (tokens, tokens), 1
    )
    rank = dot(member.astype(BF), jnp.where(earlier, 1.0, 0.0).astype(BF))
    rank = jnp.where(member > 0.0, rank, -1.0)
    shape = (experts, capacity, tokens)
    slot = lax.broadcasted_iota(jnp.int32, shape, 1).astype(F32)
    placed = jnp.where(jnp.broadcast_to(rank[:, None, :], shape) == slot, 1.0, 0.0)
    weighted = (placed * jnp.broadcast_to(gate[:, None, :], shape)).reshape(rows, tokens)
    place_ref[...] = placed.reshape(rows, tokens).astype(BF)
    mix = weighted.T
    high = mix.astype(BF)
    higat_ref[...] = high
    low_ref[...] = (mix - high.astype(F32)).astype(BF)


def pack_body(at_ref, p0, p1, p2, p3, res_ref, gain_ref, place_ref, packed_ref, att_ref, rows, gains):
    quarter = att_ref.shape[1]
    start = pl.multiple_of(at_ref[0] * quarter, quarter)
    att = res_ref[pl.ds(start, quarter), :].astype(F32).T
    for p in (p0, p1, p2, p3):
        att = att + p[:, :quarter].astype(F32)
    att_ref[...] = att
    square = jnp.sum(att * att, axis=1, keepdims=True)
    high = square.astype(BF).astype(F32)
    middle = (square - high).astype(BF).astype(F32)
    low = square - high - middle
    lane = lax.broadcasted_iota(jnp.int32, (att.shape[0], SPARE), 1)
    extra = jnp.where(lane == 0, high, jnp.where(lane == 1, middle, jnp.where(lane == 2, low, 0.0)))
    for q in range(4):
        gains[q] = gain_ref[:, q * quarter : (q + 1) * quarter]
    rows[:, :quarter] = (att * gains[at_ref[0]]).astype(BF)
    rows[:, quarter:] = extra.astype(BF)
    packed_ref[...] = dot(place_ref[...], rows[...]).astype(BF)


def weights_body(at_ref, gate_ref, up_ref, down_ref, mid_ref, out_ref):
    hidden, features = down_ref.shape
    quarter = features // 4
    padded = mid_ref.shape[1]
    wide = mid_ref.shape[2] // 2
    for q in range(4):
        place = lax.rem(q + 4 - at_ref[0], 4)
        cols = slice(q * quarter, (q + 1) * quarter)
        for side, ref in enumerate((gate_ref, up_ref)):
            lanes = slice(side * wide, (side + 1) * wide)
            tall = [ref[:, cols].astype(F32), jnp.zeros((wide - hidden, quarter), F32)]
            mid_ref[place, :quarter, lanes] = jnp.concatenate(tall, axis=0).T.astype(BF)
            mid_ref[place, quarter:, lanes] = jnp.zeros((padded - quarter, wide), BF)
        pad = jnp.zeros((hidden, padded - quarter), BF)
        out_ref[place] = jnp.concatenate([down_ref[:, cols], pad], axis=1)


def expert_body(features, x0, x1, x2, x3, mid0, out0, mid1, out1, t0, t1, t2, t3, held, total):
    quarter = features // 4
    hidden_count = out0.shape[1]
    wide = mid0.shape[2] // 2
    square = None
    for j, x in enumerate((x0, x1, x2, x3)):
        held[j] = x[...]
        tail = jnp.sum(x[:, quarter:].astype(F32), axis=1, keepdims=True)
        square = tail if j == 0 else square + tail
    scaling = lax.rsqrt(square * (1.0 / features) + 1e-06)
    total[...] = jnp.zeros_like(total)

    def gather(j, carry):
        row = held[j]
        total[0] += dot(row, mid0[j])
        total[1] += dot(row, mid1[j])
        return carry

    lax.fori_loop(0, 4, gather, 0)
    hidden = []
    for side in range(2):
        gate = total[side, :, :hidden_count] * scaling
        up = total[side, :, wide : wide + hidden_count] * scaling
        hidden.append((gate / (1.0 + jnp.exp(-gate)) * up).astype(BF))

    def spread(j, carry):
        held[j] = (dot(hidden[0], out0[j]) + dot(hidden[1], out1[j])).astype(BF)
        return carry

    lax.fori_loop(0, 4, spread, 0)
    for j, t in enumerate((t0, t1, t2, t3)):
        t[...] = held[j]


def mix_body(at_ref, back_ref, higat_ref, low_ref, att_ref, o0, o1, o2, o3, done):
    back = back_ref[...]
    quarter = att_ref.shape[1]
    mixture = dot(higat_ref[...], back) + dot(low_ref[...], back)
    done[:, :quarter] = (att_ref[...] + mixture[:, :quarter]).astype(BF)
    done[:, quarter:] = mixture[:, quarter:].astype(BF)
    share = o0.shape[0]
    for j, o in enumerate((o0, o1, o2, o3)):
        start = pl.multiple_of(lax.rem(at_ref[0] + j, 4) * share, share)
        o[...] = done[pl.ds(start, share), :]


def join_body(at_ref, r0, r1, r2, r3, o_ref, held):
    quarter = o_ref.shape[1] // 4
    for j, r in enumerate((r0, r1, r2, r3)):
        held[lax.rem(at_ref[0] + 4 - j, 4)] = r[...]
    for q in range(4):
        o_ref[:, q * quarter : (q + 1) * quarter] = held[q, :, :quarter]


def shift(x, by):
    return lax.ppermute(x, "heads", [(i, (i + by) % 4) for i in range(4)])


def swap(x):
    return lax.ppermute(x, "core", [(0, 1), (1, 0)])


def plus(*terms):
    total = terms[0].astype(F32)
    for term in terms[1:]:
        total = total + term.astype(F32)
    return total.astype(BF)


def on_device(
    residual,
    query_rows,
    key_rows,
    value_rows,
    norm_gain,
    out_weight,
    moe_gain,
    expert_ids,
    gate_values,
    gate_weight,
    up_weight,
    down_weight,
):
    tokens, width = query_rows.shape
    features = residual.shape[1]
    quarter = features // 4
    padded = quarter + SPARE
    chip = ("z", "x")
    chips = lax.axis_size("z") * lax.axis_size("x")
    ids = tuple(
        jnp.full((1,), lax.axis_index(name).astype(jnp.int32)) for name in ("heads", "core", "z", "x")
    )
    (h_at, core_at, z_at, x_at), key_rows = lax.optimization_barrier((ids, key_rows))
    capacity = min(tokens, 3 * tokens * expert_ids.shape[1] // (2 * chips))
    rows = chips * capacity
    shape = jax.ShapeDtypeStruct

    keep, send, key_near, value_near = pl.pallas_call(
        state_body,
        out_shape=(shape((HD // 2, width), BF),) * 2 + (shape((tokens, width), BF),) * 2,
        in_specs=[SMEM_SPEC] + [VMEM_SPEC] * 2,
        out_specs=(VMEM_SPEC,) * 4,
        scratch_shapes=[pltpu.VMEM((2, HD // 2, width), BF)],
        compiler_params=params(28),
        name="own_state",
    )(core_at, key_rows, value_rows)
    taken = swap(send)
    inner = pl.pallas_call(
        inner_body,
        out_shape=shape((tokens, width), F32),
        in_specs=[VMEM_SPEC] * 3,
        out_specs=VMEM_SPEC,
        compiler_params=params(28),
        cost_estimate=cost(2e9, 2e6),
        name="inner",
    )(query_rows, key_near, value_near)
    chip_state = plus(keep, taken)
    depth, breadth = lax.axis_size("z"), lax.axis_size("x")
    beside = [
        lax.ppermute(chip_state, "x", [(i, (i + j) % breadth) for i in range(breadth)])
        for j in range(1, breadth)
    ]
    slab_state = plus(chip_state, *beside)

    def deeper(x, j):
        return lax.ppermute(x, "z", [(i, (i + j) % depth) for i in range(depth)])

    near = [deeper(slab_state, 1), deeper(slab_state, 2)]
    near, inner = lax.optimization_barrier((near, inner))
    triple = pl.pallas_call(
        triple_body,
        out_shape=shape(keep.shape, BF),
        in_specs=[SMEM_SPEC] + [VMEM_SPEC] * 3,
        out_specs=VMEM_SPEC,
        compiler_params=params(28),
        name="triple",
    )(z_at, slab_state, *near)
    mine, theirs = pl.pallas_call(
        before_body,
        out_shape=(shape(keep.shape, BF),) * 2,
        in_specs=[SMEM_SPEC] * 3 + [VMEM_SPEC] * 9,
        out_specs=(VMEM_SPEC,) * 2,
        compiler_params=params(28),
        name="before",
    )(core_at, z_at, x_at, keep, taken, *near, deeper(triple, 3), deeper(triple, 6), *beside)
    other = swap(theirs)

    place, mix_high, mix_low = pl.pallas_call(
        functools.partial(route_body, chips),
        out_shape=(shape((rows, tokens), BF), shape((tokens, rows), BF), shape((tokens, rows), BF)),
        in_specs=[VMEM_SPEC] * 2,
        out_specs=(VMEM_SPEC,) * 3,
        compiler_params=params(28),
        cost_estimate=cost(1e8, 1e6),
        name="route",
    )(expert_ids.T, gate_values.T)

    parts = pl.pallas_call(
        attend_body,
        out_shape=(shape((tokens, padded), BF),) * 4,
        in_specs=[SMEM_SPEC] * 2 + [VMEM_SPEC] * 6,
        out_specs=(VMEM_SPEC,) * 4,
        scratch_shapes=[pltpu.VMEM((tokens, width), BF), pltpu.VMEM((2, HD // 2, width), BF)],
        compiler_params=params(28),
        name="attend",
    )(h_at, core_at, query_rows, inner, mine, other, norm_gain.reshape(1, width), out_weight.T)
    parts, late_h = lax.optimization_barrier((parts, h_at))
    hidden_count = gate_weight.shape[2]
    wide = -(-hidden_count // 128) * 128
    weights = pl.pallas_call(
        weights_body,
        out_shape=(shape((4, padded, 2 * wide), BF), shape((4, hidden_count, padded), BF)),
        in_specs=[SMEM_SPEC] + [VMEM_SPEC] * 3,
        out_specs=(VMEM_SPEC,) * 2,
        compiler_params=params(28),
        cost_estimate=cost(5e9, 13e6),
        name="weights",
    )(late_h, gate_weight[0].T, up_weight[0].T, down_weight[0])
    across = shift(parts[2], 2)
    pieces = [parts[0], shift(parts[1], 1), across, shift(parts[3], 3)]
    pieces, weights = lax.optimization_barrier((pieces, weights))

    packed, attended = pl.pallas_call(
        pack_body,
        out_shape=(shape((rows, padded), BF), shape((tokens, quarter), F32)),
        in_specs=[SMEM_SPEC] + [VMEM_SPEC] * 7,
        out_specs=(VMEM_SPEC,) * 2,
        scratch_shapes=[pltpu.VMEM((tokens, padded), BF), pltpu.VMEM((4, 1, quarter), F32)],
        compiler_params=params(28),
        name="pack",
    )(h_at, *pieces, residual.T, moe_gain.reshape(1, features), place)

    arrived = lax.all_to_all(
        packed.reshape(chips, capacity, padded), chip, 0, 0, tiled=True
    ).reshape(rows, padded)
    half = rows // 2
    arrived, weights = lax.optimization_barrier((arrived, weights))
    low, high = arrived[:half], arrived[half:]
    minus_low, plus_low = shift(low, 1), shift(low, -1)
    minus_low, plus_low, high, weights = lax.optimization_barrier(
        (minus_low, plus_low, high, weights)
    )
    other_weights = tuple(swap(x) for x in weights)

    def experts(group):
        return pl.pallas_call(
            functools.partial(expert_body, features),
            out_shape=(shape((half, padded), BF),) * 4,
            in_specs=[VMEM_SPEC] * 8,
            out_specs=(VMEM_SPEC,) * 4,
            scratch_shapes=[
                pltpu.VMEM((4, half, padded), BF),
                pltpu.VMEM((2, half, 2 * wide), F32),
            ],
            compiler_params=params(28),
            cost_estimate=cost(1e6, 1e5),
            name="experts",
        )(*group, *weights, *other_weights)

    far_low, plus_high = shift(minus_low, 1), shift(high, -1)
    far_low, high = lax.optimization_barrier((far_low, high))
    far_high, minus_high = shift(plus_high, -1), shift(high, 1)
    sum_low = experts((low, plus_low, far_low, minus_low))
    via_low, got_low_plus = shift(sum_low[2], 1), shift(sum_low[3], -1)
    sum_high = experts((high, plus_high, far_high, minus_high))
    via_low, got_low_plus = lax.optimization_barrier((via_low, got_low_plus))
    got_low_minus = shift(plus(sum_low[1], via_low), 1)
    via_high = shift(sum_high[2], -1)
    got_high_minus = shift(sum_high[1], 1)
    got_high_plus = shift(plus(sum_high[3], via_high), -1)
    total_low = plus(sum_low[0], got_low_minus, got_low_plus)
    total_high = plus(sum_high[0], got_high_minus, got_high_plus)
    leaving = jnp.concatenate([total_low, total_high], axis=0).reshape(chips, capacity, padded)
    returned = lax.all_to_all(leaving, chip, 0, 0, tiled=True).reshape(rows, padded)

    share = tokens // 4
    ends = pl.pallas_call(
        mix_body,
        out_shape=(shape((share, padded), BF),) * 4,
        in_specs=[SMEM_SPEC] + [VMEM_SPEC] * 4,
        out_specs=(VMEM_SPEC,) * 4,
        scratch_shapes=[pltpu.VMEM((tokens, padded), BF)],
        compiler_params=params(28),
        name="mix",
    )(h_at, returned, mix_high, mix_low, attended)
    across = shift(ends[2], 2)
    finals = [ends[0], shift(ends[1], 1), across, shift(ends[3], 3)]
    return pl.pallas_call(
        join_body,
        out_shape=shape((share, features), BF),
        in_specs=[SMEM_SPEC] + [VMEM_SPEC] * 4,
        out_specs=VMEM_SPEC,
        scratch_shapes=[pltpu.VMEM((4, share, padded), BF)],
        compiler_params=params(28),
        name="join",
    )(h_at, *finals)


def solution(mesh):
    devices = mesh.devices
    split = Mesh(
        devices.reshape(-1, BREADTH, CORES, devices.shape[1]), ("z", "x", "core", "heads")
    )
    context = ("z", "x", "core")
    in_specs = (
        P(context, None),
        P(context, "heads"),
        P(context, "heads"),
        P(context, "heads"),
        P("heads"),
        P("heads", None),
        P(),
        P(context, None),
        P(context, None),
        P(context, None, "heads"),
        P(context, None, "heads"),
        P(context, "heads", None),
    )
    return jax.shard_map(
        on_device,
        mesh=split,
        in_specs=in_specs,
        out_specs=P(("z", "x", "core", "heads"), None),
        check_vma=False,
    )
```

```python
import functools

import jax
import jax.numpy as jnp
from jax import lax
from jax.experimental import pallas as pl
from jax.experimental.pallas import tpu as pltpu
from jax.sharding import Mesh
from jax.sharding import PartitionSpec as P

HD = 64
PAIR = 2 * HD
CORES = 2
BREADTH = 4
SPARE = 48
BF = jnp.bfloat16
F32 = jnp.float32
VMEM_SPEC = pl.BlockSpec(memory_space=pltpu.VMEM)
SMEM_SPEC = pl.BlockSpec(memory_space=pltpu.SMEM)


def params(mib):
    return pltpu.CompilerParams(vmem_limit_bytes=mib << 20)


def cost(flops, moved):
    return pl.CostEstimate(flops=int(flops), bytes_accessed=int(moved), transcendentals=0)


def dot(a, b, dims=((1,), (0,))):
    return lax.dot_general(a, b, (dims, ((), ())), preferred_element_type=F32)


def state_body(at_ref, k_ref, v_ref, keep_ref, send_ref, k_out, v_out, both_ref):
    k_out[...] = k_ref[...]
    v_out[...] = v_ref[...]
    first = lax.broadcasted_iota(jnp.int32, (HD, PAIR), 1) < HD
    half = HD // 2
    for p in range(k_ref.shape[1] // PAIR):
        cols = slice(p * PAIR, (p + 1) * PAIR)
        both = dot(k_ref[:, cols], v_ref[:, cols], ((0,), (0,)))
        state = jnp.where(first, both[:HD], both[HD:]).astype(BF)
        both_ref[0, :, cols] = state[:half]
        both_ref[1, :, cols] = state[half:]
    keep_ref[...] = both_ref[at_ref[0]]
    send_ref[...] = both_ref[1 - at_ref[0]]


def flag(condition):
    return jnp.where(condition, 1.0, 0.0)


def triple_body(at_ref, slab_ref, near_ref, next_ref, o_ref):
    z = at_ref[0]
    total = slab_ref[...].astype(F32) + flag(z >= 1) * near_ref[...].astype(F32)
    o_ref[...] = (total + flag(z >= 2) * next_ref[...].astype(F32)).astype(BF)


def before_body(core_ref, z_ref, x_ref, keep_ref, taken_ref, *rest):
    mine_ref, theirs_ref = rest[-2:]
    z, x, later = z_ref[0], x_ref[0], flag(core_ref[0] == 1)
    weights = [flag(z >= j) for j in (1, 2, 3, 6)] + [flag(x > j) for j in range(3)]
    base = jnp.zeros(keep_ref.shape, F32)
    for weight, ref in zip(weights, rest[:-2]):
        base = base + weight * ref[...].astype(F32)
    mine_ref[...] = (base + later * taken_ref[...].astype(F32)).astype(BF)
    theirs_ref[...] = (base + (1.0 - later) * keep_ref[...].astype(F32)).astype(BF)


def inner_body(q_ref, k_ref, v_ref, o_ref):
    tokens = q_ref.shape[0]
    first = lax.broadcasted_iota(jnp.int32, (tokens, PAIR), 1) < HD
    causal = lax.broadcasted_iota(jnp.int32, (tokens, tokens), 0) >= lax.broadcasted_iota(
        jnp.int32, (tokens, tokens), 1
    )
    zero = jnp.zeros((tokens, PAIR), BF)
    for p in range(q_ref.shape[1] // PAIR):
        cols = slice(p * PAIR, (p + 1) * PAIR)
        q, k, v = q_ref[:, cols], k_ref[:, cols], v_ref[:, cols]
        inner = []
        for keep in (jnp.where(first, q, zero), jnp.where(first, zero, q)):
            scores = dot(keep, k, ((1,), (1,)))
            weights = jnp.where(causal, scores, 0.0).astype(BF)
            inner.append(dot(weights, v))
        o_ref[:, cols] = jnp.where(first, inner[0], inner[1])


def attend_body(
    at_ref, core_ref, q_ref, inner_ref, mine_ref, other_ref, gain_ref, w_ref, o0, o1, o2, o3, normed, state
):
    tokens = q_ref.shape[0]
    first = lax.broadcasted_iota(jnp.int32, (tokens, PAIR), 1) < HD
    first_s = lax.broadcasted_iota(jnp.int32, (HD, PAIR), 1) < HD
    state[core_ref[0]] = mine_ref[...]
    state[1 - core_ref[0]] = other_ref[...]

    def halves_mean(x):
        a = jnp.sum(jnp.where(first, x, 0.0), axis=1, keepdims=True)
        b = jnp.sum(jnp.where(first, 0.0, x), axis=1, keepdims=True)
        return jnp.where(first, a, b) * (1.0 / HD)

    for p in range(q_ref.shape[1] // PAIR):
        cols = slice(p * PAIR, (p + 1) * PAIR)
        s = jnp.concatenate([state[0, :, cols], state[1, :, cols]], axis=0)
        s_zero = jnp.zeros_like(s)
        block = jnp.concatenate(
            [jnp.where(first_s, s, s_zero), jnp.where(first_s, s_zero, s)], axis=0
        )
        mixed = inner_ref[:, cols] + dot(q_ref[:, cols], block)
        centered = mixed - halves_mean(mixed)
        spread = halves_mean(centered * centered)
        normed[:, cols] = (centered * lax.rsqrt(spread + 1e-05) * gain_ref[:, cols]).astype(BF)
    quarter = w_ref.shape[0] // 4
    pad = jnp.zeros((tokens, o0.shape[1] - quarter), BF)
    for j, o in enumerate((o0, o1, o2, o3)):
        start = pl.multiple_of(lax.rem(at_ref[0] + j, 4) * quarter, quarter)
        part = dot(normed[...], w_ref[pl.ds(start, quarter), :], ((1,), (1,)))
        o[:, :quarter] = part.astype(BF)
        o[:, quarter:] = pad


def route_body(experts, ids_ref, gates_ref, place_ref, higat_ref, low_ref):
    top, tokens = ids_ref.shape
    rows = place_ref.shape[0]
    capacity = rows // experts
    expert = lax.broadcasted_iota(jnp.int32, (experts, tokens), 0)
    member = jnp.zeros((experts, tokens), F32)
    gate = jnp.zeros((experts, tokens), F32)
    for c in range(top):
        hit = ids_ref[c : c + 1, :] == expert
        member = member + jnp.where(hit, 1.0, 0.0)
        gate = gate + jnp.where(hit, gates_ref[c : c + 1, :], 0.0)
    earlier = lax.broadcasted_iota(jnp.int32, (tokens, tokens), 0) < lax.broadcasted_iota(
        jnp.int32, (tokens, tokens), 1
    )
    rank = dot(member.astype(BF), jnp.where(earlier, 1.0, 0.0).astype(BF))
    rank = jnp.where(member > 0.0, rank, -1.0)
    shape = (experts, capacity, tokens)
    slot = lax.broadcasted_iota(jnp.int32, shape, 1).astype(F32)
    placed = jnp.where(jnp.broadcast_to(rank[:, None, :], shape) == slot, 1.0, 0.0)
    weighted = (placed * jnp.broadcast_to(gate[:, None, :], shape)).reshape(rows, tokens)
    place_ref[...] = placed.reshape(rows, tokens).astype(BF)
    mix = weighted.T
    high = mix.astype(BF)
    higat_ref[...] = high
    low_ref[...] = (mix - high.astype(F32)).astype(BF)


def pack_body(at_ref, p0, p1, p2, p3, res_ref, gain_ref, place_ref, packed_ref, att_ref, rows, gains):
    quarter = att_ref.shape[1]
    start = pl.multiple_of(at_ref[0] * quarter, quarter)
    att = res_ref[pl.ds(start, quarter), :].astype(F32).T
    for p in (p0, p1, p2, p3):
        att = att + p[:, :quarter].astype(F32)
    att_ref[...] = att
    square = jnp.sum(att * att, axis=1, keepdims=True)
    high = square.astype(BF).astype(F32)
    middle = (square - high).astype(BF).astype(F32)
    low = square - high - middle
    lane = lax.broadcasted_iota(jnp.int32, (att.shape[0], SPARE), 1)
    extra = jnp.where(lane == 0, high, jnp.where(lane == 1, middle, jnp.where(lane == 2, low, 0.0)))
    for q in range(4):
        gains[q] = gain_ref[:, q * quarter : (q + 1) * quarter]
    rows[:, :quarter] = (att * gains[at_ref[0]]).astype(BF)
    rows[:, quarter:] = extra.astype(BF)
    packed_ref[...] = dot(place_ref[...], rows[...]).astype(BF)


def weights_body(at_ref, gate_ref, up_ref, down_ref, mid_ref, out_ref):
    hidden, features = down_ref.shape
    quarter = features // 4
    padded = mid_ref.shape[1]
    wide = mid_ref.shape[2] // 2
    for q in range(4):
        place = lax.rem(q + 4 - at_ref[0], 4)
        cols = slice(q * quarter, (q + 1) * quarter)
        for side, ref in enumerate((gate_ref, up_ref)):
            lanes = slice(side * wide, (side + 1) * wide)
            tall = [ref[:, cols].astype(F32), jnp.zeros((wide - hidden, quarter), F32)]
            mid_ref[place, :quarter, lanes] = jnp.concatenate(tall, axis=0).T.astype(BF)
            mid_ref[place, quarter:, lanes] = jnp.zeros((padded - quarter, wide), BF)
        pad = jnp.zeros((hidden, padded - quarter), BF)
        out_ref[place] = jnp.concatenate([down_ref[:, cols], pad], axis=1)


def expert_body(features, x0, x1, x2, x3, mid0, out0, mid1, out1, t0, t1, t2, t3, held, total):
    quarter = features // 4
    hidden_count = out0.shape[1]
    wide = mid0.shape[2] // 2
    square = None
    for j, x in enumerate((x0, x1, x2, x3)):
        held[j] = x[...]
        tail = jnp.sum(x[:, quarter:].astype(F32), axis=1, keepdims=True)
        square = tail if j == 0 else square + tail
    scaling = lax.rsqrt(square * (1.0 / features) + 1e-06)
    total[...] = jnp.zeros_like(total)

    def gather(j, carry):
        row = held[j]
        total[0] += dot(row, mid0[j])
        total[1] += dot(row, mid1[j])
        return carry

    lax.fori_loop(0, 4, gather, 0)
    hidden = []
    for side in range(2):
        gate = total[side, :, :hidden_count] * scaling
        up = total[side, :, wide : wide + hidden_count] * scaling
        hidden.append((gate / (1.0 + jnp.exp(-gate)) * up).astype(BF))

    def spread(j, carry):
        held[j] = (dot(hidden[0], out0[j]) + dot(hidden[1], out1[j])).astype(BF)
        return carry

    lax.fori_loop(0, 4, spread, 0)
    for j, t in enumerate((t0, t1, t2, t3)):
        t[...] = held[j]


def mix_body(at_ref, back_ref, higat_ref, low_ref, att_ref, o0, o1, o2, o3, done):
    back = back_ref[...]
    quarter = att_ref.shape[1]
    mixture = dot(higat_ref[...], back) + dot(low_ref[...], back)
    done[:, :quarter] = (att_ref[...] + mixture[:, :quarter]).astype(BF)
    done[:, quarter:] = mixture[:, quarter:].astype(BF)
    share = o0.shape[0]
    for j, o in enumerate((o0, o1, o2, o3)):
        start = pl.multiple_of(lax.rem(at_ref[0] + j, 4) * share, share)
        o[...] = done[pl.ds(start, share), :]


def join_body(at_ref, r0, r1, r2, r3, o_ref, held):
    quarter = o_ref.shape[1] // 4
    for j, r in enumerate((r0, r1, r2, r3)):
        held[lax.rem(at_ref[0] + 4 - j, 4)] = r[...]
    for q in range(4):
        o_ref[:, q * quarter : (q + 1) * quarter] = held[q, :, :quarter]


def shift(x, by):
    return lax.ppermute(x, "heads", [(i, (i + by) % 4) for i in range(4)])


def swap(x):
    return lax.ppermute(x, "core", [(0, 1), (1, 0)])


def plus(*terms):
    total = terms[0].astype(F32)
    for term in terms[1:]:
        total = total + term.astype(F32)
    return total.astype(BF)


def on_device(
    residual,
    query_rows,
    key_rows,
    value_rows,
    norm_gain,
    out_weight,
    moe_gain,
    expert_ids,
    gate_values,
    gate_weight,
    up_weight,
    down_weight,
):
    tokens, width = query_rows.shape
    features = residual.shape[1]
    quarter = features // 4
    padded = quarter + SPARE
    chip = ("z", "x")
    chips = lax.axis_size("z") * lax.axis_size("x")
    ids = tuple(
        jnp.full((1,), lax.axis_index(name).astype(jnp.int32)) for name in ("heads", "core", "z", "x")
    )
    (h_at, core_at, z_at, x_at), key_rows = lax.optimization_barrier((ids, key_rows))
    capacity = min(tokens, 3 * tokens * expert_ids.shape[1] // (2 * chips))
    rows = chips * capacity
    shape = jax.ShapeDtypeStruct

    keep, send, key_near, value_near = pl.pallas_call(
        state_body,
        out_shape=(shape((HD // 2, width), BF),) * 2 + (shape((tokens, width), BF),) * 2,
        in_specs=[SMEM_SPEC] + [VMEM_SPEC] * 2,
        out_specs=(VMEM_SPEC,) * 4,
        scratch_shapes=[pltpu.VMEM((2, HD // 2, width), BF)],
        compiler_params=params(28),
        name="own_state",
    )(core_at, key_rows, value_rows)
    taken = swap(send)
    inner = pl.pallas_call(
        inner_body,
        out_shape=shape((tokens, width), F32),
        in_specs=[VMEM_SPEC] * 3,
        out_specs=VMEM_SPEC,
        compiler_params=params(28),
        cost_estimate=cost(2e9, 2e6),
        name="inner",
    )(query_rows, key_near, value_near)
    chip_state = plus(keep, taken)
    depth, breadth = lax.axis_size("z"), lax.axis_size("x")
    beside = [
        lax.ppermute(chip_state, "x", [(i, (i + j) % breadth) for i in range(breadth)])
        for j in range(1, breadth)
    ]
    slab_state = plus(chip_state, *beside)

    def deeper(x, j):
        return lax.ppermute(x, "z", [(i, (i + j) % depth) for i in range(depth)])

    near = [deeper(slab_state, 1), deeper(slab_state, 2)]
    near, inner = lax.optimization_barrier((near, inner))
    triple = pl.pallas_call(
        triple_body,
        out_shape=shape(keep.shape, BF),
        in_specs=[SMEM_SPEC] + [VMEM_SPEC] * 3,
        out_specs=VMEM_SPEC,
        compiler_params=params(28),
        name="triple",
    )(z_at, slab_state, *near)
    mine, theirs = pl.pallas_call(
        before_body,
        out_shape=(shape(keep.shape, BF),) * 2,
        in_specs=[SMEM_SPEC] * 3 + [VMEM_SPEC] * 9,
        out_specs=(VMEM_SPEC,) * 2,
        compiler_params=params(28),
        name="before",
    )(core_at, z_at, x_at, keep, taken, *near, deeper(triple, 3), deeper(triple, 6), *beside)
    other = swap(theirs)

    place, mix_high, mix_low = pl.pallas_call(
        functools.partial(route_body, chips),
        out_shape=(shape((rows, tokens), BF), shape((tokens, rows), BF), shape((tokens, rows), BF)),
        in_specs=[VMEM_SPEC] * 2,
        out_specs=(VMEM_SPEC,) * 3,
        compiler_params=params(28),
        cost_estimate=cost(1e8, 1e6),
        name="route",
    )(expert_ids.T, gate_values.T)

    parts = pl.pallas_call(
        attend_body,
        out_shape=(shape((tokens, padded), BF),) * 4,
        in_specs=[SMEM_SPEC] * 2 + [VMEM_SPEC] * 6,
        out_specs=(VMEM_SPEC,) * 4,
        scratch_shapes=[pltpu.VMEM((tokens, width), BF), pltpu.VMEM((2, HD // 2, width), BF)],
        compiler_params=params(28),
        name="attend",
    )(h_at, core_at, query_rows, inner, mine, other, norm_gain.reshape(1, width), out_weight.T)
    parts, late_h = lax.optimization_barrier((parts, h_at))
    hidden_count = gate_weight.shape[2]
    wide = -(-hidden_count // 128) * 128
    weights = pl.pallas_call(
        weights_body,
        out_shape=(shape((4, padded, 2 * wide), BF), shape((4, hidden_count, padded), BF)),
        in_specs=[SMEM_SPEC] + [VMEM_SPEC] * 3,
        out_specs=(VMEM_SPEC,) * 2,
        compiler_params=params(28),
        cost_estimate=cost(5e9, 13e6),
        name="weights",
    )(late_h, gate_weight[0].T, up_weight[0].T, down_weight[0])
    across = shift(parts[2], 2)
    pieces = [parts[0], shift(parts[1], 1), across, shift(parts[3], 3)]
    pieces, weights = lax.optimization_barrier((pieces, weights))

    packed, attended = pl.pallas_call(
        pack_body,
        out_shape=(shape((rows, padded), BF), shape((tokens, quarter), F32)),
        in_specs=[SMEM_SPEC] + [VMEM_SPEC] * 7,
        out_specs=(VMEM_SPEC,) * 2,
        scratch_shapes=[pltpu.VMEM((tokens, padded), BF), pltpu.VMEM((4, 1, quarter), F32)],
        compiler_params=params(28),
        name="pack",
    )(h_at, *pieces, residual.T, moe_gain.reshape(1, features), place)

    arrived = lax.all_to_all(
        packed.reshape(chips, capacity, padded), chip, 0, 0, tiled=True
    ).reshape(rows, padded)
    half = rows // 2
    arrived, weights = lax.optimization_barrier((arrived, weights))
    low, high = arrived[:half], arrived[half:]
    minus_low, plus_low = shift(low, 1), shift(low, -1)
    other_weights = tuple(swap(x) for x in weights)
    minus_low, plus_low, high, other_weights = lax.optimization_barrier(
        (minus_low, plus_low, high, other_weights)
    )

    def experts(group):
        return pl.pallas_call(
            functools.partial(expert_body, features),
            out_shape=(shape((half, padded), BF),) * 4,
            in_specs=[VMEM_SPEC] * 8,
            out_specs=(VMEM_SPEC,) * 4,
            scratch_shapes=[
                pltpu.VMEM((4, half, padded), BF),
                pltpu.VMEM((2, half, 2 * wide), F32),
            ],
            compiler_params=params(28),
            cost_estimate=cost(1e6, 1e5),
            name="experts",
        )(*group, *weights, *other_weights)

    far_low, plus_high = shift(minus_low, 1), shift(high, -1)
    far_low, high = lax.optimization_barrier((far_low, high))
    far_high, minus_high = shift(plus_high, -1), shift(high, 1)
    sum_low = experts((low, plus_low, far_low, minus_low))
    via_low, got_low_plus = shift(sum_low[2], 1), shift(sum_low[3], -1)
    sum_high = experts((high, plus_high, far_high, minus_high))
    via_low, got_low_plus = lax.optimization_barrier((via_low, got_low_plus))
    got_low_minus = shift(plus(sum_low[1], via_low), 1)
    via_high = shift(sum_high[2], -1)
    got_high_minus = shift(sum_high[1], 1)
    got_high_plus = shift(plus(sum_high[3], via_high), -1)
    total_low = plus(sum_low[0], got_low_minus, got_low_plus)
    total_high = plus(sum_high[0], got_high_minus, got_high_plus)
    leaving = jnp.concatenate([total_low, total_high], axis=0).reshape(chips, capacity, padded)
    returned = lax.all_to_all(leaving, chip, 0, 0, tiled=True).reshape(rows, padded)

    share = tokens // 4
    ends = pl.pallas_call(
        mix_body,
        out_shape=(shape((share, padded), BF),) * 4,
        in_specs=[SMEM_SPEC] + [VMEM_SPEC] * 4,
        out_specs=(VMEM_SPEC,) * 4,
        scratch_shapes=[pltpu.VMEM((tokens, padded), BF)],
        compiler_params=params(28),
        name="mix",
    )(h_at, returned, mix_high, mix_low, attended)
    across = shift(ends[2], 2)
    finals = [ends[0], shift(ends[1], 1), across, shift(ends[3], 3)]
    return pl.pallas_call(
        join_body,
        out_shape=shape((share, features), BF),
        in_specs=[SMEM_SPEC] + [VMEM_SPEC] * 4,
        out_specs=VMEM_SPEC,
        scratch_shapes=[pltpu.VMEM((4, share, padded), BF)],
        compiler_params=params(28),
        name="join",
    )(h_at, *finals)


def solution(mesh):
    devices = mesh.devices
    split = Mesh(
        devices.reshape(-1, BREADTH, CORES, devices.shape[1]), ("z", "x", "core", "heads")
    )
    context = ("z", "x", "core")
    in_specs = (
        P(context, None),
        P(context, "heads"),
        P(context, "heads"),
        P(context, "heads"),
        P("heads"),
        P("heads", None),
        P(),
        P(context, None),
        P(context, None),
        P(context, None, "heads"),
        P(context, None, "heads"),
        P(context, "heads", None),
    )
    return jax.shard_map(
        on_device,
        mesh=split,
        in_specs=in_specs,
        out_specs=P(("z", "x", "core", "heads"), None),
        check_vma=False,
    )
```
